512 devices in a mesh: kv: 4 (over x), seq: 16 (over z), exp: 8 (over y, core).
Axes of the slice: x: 4, y: 4, z: 16, core: 2. Of those that a mesh axis runs over, the one named last changes fastest.
Arguments:
- queries: bfloat16 [64, 64, 2048], P(('kv', 'seq')), may hold values from -8 to 8
- draft_kv: bfloat16 [2, 64, 64, 2048], P(None, ('kv', 'seq'), 'exp'), may hold values from -12 to 12
- kv_pool: bfloat16 [2, 6144, 16, 2048], P(None, ('kv', 'seq', 'exp')), may hold values from -12 to 12
- page_table: int32 [64, 12, 8], P(('kv', 'seq'), None, 'exp'), may hold values from 0 to 11, as said below
- cache_lens: int32 [64], P(('kv', 'seq')), may hold values from 1 to 1536, as said below
- parents: int32 [64, 64], P(('kv', 'seq')), may hold values from -1 to 62, as said below
- hidden: bfloat16 [64, 64, 2048], P(('kv', 'seq')), may hold values from -36 to 36
- norm_gain: bfloat16 [2048], replicated, may hold values from 0.5 to 1.5
- out_proj: bfloat16 [2048, 2048], P('exp'), may hold values from -0.125 to 0.125
- router: bfloat16 [2048, 64], replicated, may hold values from -0.125 to 0.125
- routes: int32 [64, 64, 8], P(('kv', 'seq')), may hold values from 0 to 63, all different within a row; in each aligned block of 64 rows (0 to 63, 64 to 127, ..., all dimensions but the last counted through in order) at most 16 rows name the same one
- gate_w: bfloat16 [64, 2048, 1024], P(('kv', 'seq'), None, 'exp'), may hold values from -0.125 to 0.125
- up_w: bfloat16 [64, 2048, 1024], P(('kv', 'seq'), None, 'exp'), may hold values from -0.125 to 0.125
- down_w: bfloat16 [64, 1024, 2048], P(('kv', 'seq'), 'exp'), may hold values from -0.1875 to 0.1875
Outputs:
- output: bfloat16 [64, 64, 2048], P(('kv', 'seq'), None, 'exp')
The draws below stay inside these ranges and needn't reach their ends.
Inputs may be any that keep to these rules, and one draw needn't show every extreme that they name: For one block of 1 request and one page set s, the entries page_table[r, j, s] over the block's requests r and all j are a permutation of 0 .. 11. `cache_lens`: some request has exactly 1536 cached positions. parents[r, 0] = -1; for i >= 1, parents[r, i] is an earlier draft position. `routes`: in each aligned block of 64 token rows (the rows of one device, requests in order), no expert is named by more than 16 rows.
All inputs are finite; a program needn't handle non-finite values.
Results may differ from the reference program's by a relative error of at most 0.02.
Values may be sent and summed in bfloat16 or wider, within the bound.
No kernel may reach another device: no remote copies, remote signals or barrier semaphores. Data moves between devices by JAX's collectives and lax.ppermute only.
A program may use at most 64 MiB of HBM per device.

```python
import math
import jax
import jax.numpy as jnp
import numpy as np
from jax import lax

D = 2048
H = 16
HD = 128
FF = 1024
EXPERTS = 64
TOPK = 8
DRAFT = 64
PAGE = 16
RK = 1
PPD = 12
SETS = 8
REQS = 64
MAXLEN = 1536
POOL = 6144
CAP = 16


def draw_queries(key, part):
    array_shape = (REQS, DRAFT, H * HD)
    noise_key = jax.random.fold_in(key, 101)
    values = jnp.clip(jax.random.normal(noise_key, array_shape, jnp.float32), -6.0, 6.0)
    return values.astype(jnp.bfloat16)


def draw_draft_kv(key, part):
    array_shape = (REQS, DRAFT, H * HD)
    key_noise = jax.random.fold_in(key, 201)
    value_noise = jax.random.fold_in(key, 202)
    key_rows = 2.5 * jnp.clip(jax.random.normal(key_noise, array_shape, jnp.float32), -4.0, 4.0)
    value_rows = jnp.clip(jax.random.normal(value_noise, array_shape, jnp.float32), -6.0, 6.0)
    return jnp.stack([key_rows, value_rows]).astype(jnp.bfloat16)


def draw_kv_pool(key, part):
    array_shape = (POOL, PAGE, H * HD)
    key_noise = jax.random.fold_in(key, 301)
    value_noise = jax.random.fold_in(key, 302)
    key_rows = 2.5 * jnp.clip(jax.random.normal(key_noise, array_shape, jnp.float32), -4.0, 4.0)
    value_rows = jnp.clip(jax.random.normal(value_noise, array_shape, jnp.float32), -6.0, 6.0)
    return jnp.stack([key_rows, value_rows]).astype(jnp.bfloat16)


def draw_page_table(key, part):
    blocks = REQS // RK
    key_list = jax.random.split(jax.random.fold_in(key, 351), blocks * SETS)
    orders = jax.vmap(lambda single_key: jax.random.permutation(single_key, RK * PPD))(key_list)
    orders = orders.reshape(blocks, SETS, RK, PPD)
    return jnp.transpose(orders, (0, 2, 3, 1)).reshape(REQS, PPD, SETS).astype(jnp.int32)


def draw_cache_lens(key, part):
    first_draw = jax.random.randint(jax.random.fold_in(key, 401), (REQS,), 1, MAXLEN + 1)
    second_draw = jax.random.randint(jax.random.fold_in(key, 402), (REQS,), 1, MAXLEN + 1)
    longest = jax.random.randint(jax.random.fold_in(key, 403), (), 0, REQS)
    lengths = jnp.minimum(first_draw, second_draw)
    return jnp.where(jnp.arange(REQS, dtype=jnp.int32) == longest, MAXLEN, lengths).astype(jnp.int32)


def draw_parents(key, part):
    raw_bits = jax.random.randint(jax.random.fold_in(key, 451), (REQS, DRAFT), 0, 1 << 20)
    position = jnp.arange(DRAFT, dtype=jnp.int32)[None, :]
    lowest = jnp.maximum(position - 4, 0)
    spread = jnp.maximum(position - lowest, 1)
    linked = jnp.where(position == DRAFT - 1, DRAFT - 2, lowest + raw_bits % spread)
    return jnp.where(position == 0, -1, linked).astype(jnp.int32)


def draw_hidden(key, part):
    row_scale = jnp.exp(jax.random.uniform(jax.random.fold_in(key, 501), (REQS, DRAFT, 1), jnp.float32, math.log(0.3), math.log(3.0)))
    column_scale = jnp.exp(jax.random.uniform(jax.random.fold_in(key, 502), (1, 1, D), jnp.float32, math.log(0.3), math.log(3.0)))
    noise_key = jax.random.fold_in(key, 503)
    drawn_rows = jnp.clip(jax.random.normal(noise_key, (REQS, DRAFT, D), jnp.float32), -4.0, 4.0)
    return (drawn_rows * row_scale * column_scale).astype(jnp.bfloat16)


def level_of(key, shape, cuts, low, largest):
    factor_of = 1.0
    for dim, blocks in cuts:
        steps = jax.random.uniform(jax.random.fold_in(jax.random.fold_in(key, 6), dim), (blocks,), jnp.float32, low / len(cuts), largest / len(cuts))
        factor_of = factor_of * jnp.repeat(jnp.exp(steps), shape[dim] // blocks).reshape((-1,) + (1,) * (len(shape) - 1 - dim))
    return factor_of


def routed_block(key, own, number, rows, count, top, bound, skew):
    ranking = jax.random.permutation(key, count)
    crowded, ordinary = shares(count, rows * top, bound, skew, True), shares(count, rows * top, bound, skew, False)
    places = jnp.arange(count)

    def named(tallies, turn):
        used = int((tallies > 0).sum())
        fixed = max(1, used // 4)
        shifted = fixed + (places - fixed + turn * (used - fixed)) % max(1, count - fixed)
        return jnp.zeros((count,), jnp.int32).at[ranking[jnp.where(places < fixed, places, shifted)]].set(jnp.asarray(tallies, jnp.int32))

    tallies = jnp.where(number % 4 == 0, named(crowded, number // 4), named(ordinary, number - number // 4 - 1))
    mixed = jax.random.permutation(jax.random.fold_in(own, 3), count)
    donor, receiver = mixed[0:count // 2 * 2:2], mixed[1:count // 2 * 2:2]
    slack = jnp.minimum(tallies[donor] - 1, bound - tallies[receiver]) // 2
    slack = jnp.where((donor == ranking[0]) | (receiver == ranking[0]) | (tallies[receiver] == 0), 0, jnp.maximum(slack, 0))
    shifted = jax.random.randint(jax.random.fold_in(own, 4), (count // 2,), 0, 1 << 20) % (slack + 1)
    tallies = tallies.at[donor].add(-shifted).at[receiver].add(shifted)
    items = jnp.searchsorted(jnp.cumsum(tallies), jnp.arange(rows * top), side="right").astype(jnp.int32)
    listing = items.reshape(top, rows).T
    listing = listing[jax.random.permutation(jax.random.fold_in(own, 1), rows)]
    turn = jax.random.randint(jax.random.fold_in(own, 2), (rows, 1), 0, top)
    return jnp.take_along_axis(listing, (jnp.arange(top)[None, :] + turn) % top, axis=1)


def shares(number_of, total, bound, lean, full):
    weights = [(1 << 20) // math.isqrt(rank ** lean) + 1 for rank in range(1, number_of + 1)]
    largest = bound if full else min(bound, max(-(-total // number_of), total * weights[0] // sum(weights)))
    least = 1 if total - largest >= number_of - 1 else 0
    given, surplus = [largest] + [least] * (number_of - 1), total - largest - least * (number_of - 1)
    while surplus > 0:
        free = [i for i in range(1, number_of) if given[i] < largest] or [i for i in range(1, number_of) if given[i] < bound]
        whole, remaining = sum([weights[i] for i in free]), surplus
        for i in free:
            more = min(bound - given[i], max(1, remaining * weights[i] // whole), surplus)
            given[i] = given[i] + more
            surplus = surplus - more
    return np.array(given)


def bell_draw(own_key, shape, scale, bound, pieces=(), held_as=jnp.bfloat16):
    factor_of = level_of(own_key, shape, pieces, -0.22, 0.18) if pieces else 1.0
    array = jax.random.normal(own_key, shape, jnp.float32) * scale * factor_of
    return jnp.minimum(jnp.maximum(array, -bound), bound).astype(held_as)


def setup_inputs(seed: int = 0) -> dict:
    splits = jax.random.split(jax.random.key(seed), 15)
    queries = draw_queries(jax.random.fold_in(splits[14], 71), 0)
    draft_kv = draw_draft_kv(jax.random.fold_in(splits[14], 71), 0)
    kv_pool = draw_kv_pool(jax.random.fold_in(splits[14], 71), 0)
    page_table = draw_page_table(jax.random.fold_in(splits[14], 71), 0)
    cache_lens = draw_cache_lens(jax.random.fold_in(splits[14], 71), 0)
    parents = draw_parents(jax.random.fold_in(splits[14], 71), 0)
    hidden = draw_hidden(jax.random.fold_in(splits[14], 71), 0)
    norm_gain = jnp.clip(1.0 + 0.1 * jax.random.normal(splits[7], (D,), jnp.float32), 0.5, 1.5).astype(jnp.bfloat16)
    out_proj = bell_draw(splits[8], (H * HD, D), (H * HD) ** -0.5, 0.125, ((0, 8),))
    router = bell_draw(splits[9], (D, EXPERTS), D ** -0.5, 0.125)
    routes_keys = jax.random.split(jax.random.fold_in(splits[10], 1), REQS * DRAFT // (RK * DRAFT))
    routes_turns = jax.random.permutation(jax.random.fold_in(splits[10], 3), REQS * DRAFT // (RK * DRAFT))
    routes = jax.vmap(lambda own, number: routed_block(jax.random.fold_in(splits[10], 2), own, number, RK * DRAFT, EXPERTS, TOPK, CAP, 2))(routes_keys, routes_turns).reshape((REQS, DRAFT, TOPK))
    gate_w = bell_draw(splits[11], (EXPERTS, D, FF), D ** -0.5, 0.125, ((0, 64), (2, 8)))
    up_w = bell_draw(splits[12], (EXPERTS, D, FF), D ** -0.5, 0.125, ((0, 64), (2, 8)))
    down_w = bell_draw(splits[13], (EXPERTS, FF, D), FF ** -0.5, 0.1875, ((0, 64), (1, 8)))
    return {"queries": queries, "draft_kv": draft_kv, "kv_pool": kv_pool, "page_table": page_table, "cache_lens": cache_lens, "parents": parents, "hidden": hidden, "norm_gain": norm_gain, "out_proj": out_proj, "router": router, "routes": routes, "gate_w": gate_w, "up_w": up_w, "down_w": down_w}


NEG_FILL = -1e+30
EPS_NORM = 1e-06

def ancestry(parents):
    positions = jnp.arange(DRAFT, dtype=jnp.int32)
    linked = (parents[:, :, None] == positions[None, None, :]).astype(jnp.float32)
    linked = linked + jnp.eye(DRAFT, dtype=jnp.float32)[None]
    for doubling in range((DRAFT - 1).bit_length()):
        linked = jnp.minimum(jnp.einsum('nij,njk->nik', linked, linked, precision=lax.Precision.HIGHEST), 1.0)
    return linked

def slot_numbers(flat_routes):
    expert_ids = jnp.arange(EXPERTS, dtype=jnp.int32)
    picked = (flat_routes[:, None] == expert_ids[None, :]).astype(jnp.int32)
    earlier = jnp.cumsum(picked, axis=0) - picked
    return flat_routes * CAP + lax.optimization_barrier(jnp.sum(earlier * picked, axis=1))

def set_partials(query_rows, cache_keys, cache_values, draft_keys, draft_values, cache_seen, draft_seen):
    key_rows = jnp.concatenate([cache_keys, draft_keys], axis=0).astype(jnp.float32).reshape(-1, H, HD)
    value_rows = jnp.concatenate([cache_values, draft_values], axis=0).astype(jnp.float32).reshape(-1, H, HD)
    query_heads = query_rows.astype(jnp.float32).reshape(DRAFT, H, HD)
    visible = jnp.concatenate([jnp.broadcast_to(cache_seen[None, :], (DRAFT, cache_seen.shape[0])), draft_seen], axis=1)
    scores = jnp.einsum('qhd,khd->hqk', query_heads, key_rows, precision=lax.Precision.HIGHEST) * HD ** (-0.5)
    scores = jnp.where(visible[None], scores, NEG_FILL)
    row_max = lax.optimization_barrier(jnp.max(scores, axis=2))
    weights = jnp.where(visible[None], jnp.exp(scores - row_max[:, :, None]), 0.0)
    row_sum = lax.optimization_barrier(jnp.sum(weights, axis=2))
    rounded = lax.optimization_barrier(weights.astype(jnp.bfloat16)).astype(jnp.float32)
    weighted = jnp.einsum('hqk,khd->qhd', rounded, value_rows, precision=lax.Precision.HIGHEST)
    return (jnp.transpose(row_max), jnp.transpose(row_sum), weighted)

def reference(queries, draft_kv, kv_pool, page_table, cache_lens, parents, hidden, norm_gain, out_proj, router, routes, gate_w, up_w, down_w):
    draft_share = DRAFT // SETS

    def attend(request_item):
        query_rows, draft_keys, draft_values, table_rows, length, parent, block_index = request_item
        pool_index = ((block_index * SETS + jnp.arange(SETS, dtype=jnp.int32)) * (RK * PPD))[None, :] + table_rows
        page_keys = jnp.transpose(kv_pool[0][pool_index], (1, 0, 2, 3)).reshape(SETS, PPD * PAGE, H * HD)
        page_values = jnp.transpose(kv_pool[1][pool_index], (1, 0, 2, 3)).reshape(SETS, PPD * PAGE, H * HD)
        page_ids = jnp.arange(PPD, dtype=jnp.int32)[None, :, None] * SETS + jnp.arange(SETS, dtype=jnp.int32)[:, None, None]
        positions = (page_ids * PAGE + jnp.arange(PAGE, dtype=jnp.int32)[None, None, :]).reshape(SETS, PPD * PAGE)
        cache_seen = positions < length
        linked = ancestry(parent[None])[0]
        draft_seen = jnp.transpose(linked.reshape(DRAFT, SETS, draft_share), (1, 0, 2)) > 0.5
        set_max, set_sum, set_acc = jax.vmap(set_partials, in_axes=(None, 0, 0, 0, 0, 0, 0))(query_rows, page_keys, page_values, draft_keys.reshape(SETS, draft_share, H * HD), draft_values.reshape(SETS, draft_share, H * HD), cache_seen, draft_seen)
        overall_max = lax.optimization_barrier(jnp.max(set_max, axis=0))
        set_scale = jnp.exp(set_max - overall_max[None])
        row_sum = lax.optimization_barrier(jnp.sum(set_scale * set_sum, axis=0))
        weighted = lax.optimization_barrier(jnp.sum(set_scale[..., None] * set_acc, axis=0))
        return (weighted / row_sum[..., None]).astype(jnp.bfloat16).reshape(DRAFT, H * HD)
    block_of = jnp.arange(REQS, dtype=jnp.int32) // RK
    attended = lax.map(attend, (queries, draft_kv[0], draft_kv[1], page_table, cache_lens, parents, block_of))
    token_count = REQS * DRAFT
    projected = jnp.dot(attended.reshape(token_count, H * HD), out_proj, preferred_element_type=jnp.float32)
    residual = hidden.reshape(token_count, D).astype(jnp.float32) + projected
    mean_sq = lax.optimization_barrier(jnp.mean(residual * residual, axis=1, keepdims=True))
    normed = (residual * lax.rsqrt(mean_sq + EPS_NORM) * norm_gain.astype(jnp.float32)[None, :]).astype(jnp.bfloat16)
    logits = jnp.dot(normed, router, preferred_element_type=jnp.float32)
    chosen = routes.reshape(token_count, TOPK)
    gate_values = jax.nn.sigmoid(jnp.take_along_axis(logits, chosen, axis=1))
    block_rows = RK * DRAFT
    block_count = REQS // RK
    slot_of = jax.vmap(slot_numbers)(chosen.reshape(block_count, block_rows * TOPK))
    owner_rows = jnp.arange(block_count, dtype=jnp.int32)[:, None] * block_rows + jnp.arange(block_rows * TOPK, dtype=jnp.int32)[None, :] // TOPK
    block_ids = jnp.broadcast_to(jnp.arange(block_count, dtype=jnp.int32)[:, None], slot_of.shape)
    token_table = jnp.full((block_count, EXPERTS * CAP), -1, jnp.int32).at[block_ids, slot_of].set(owner_rows)
    gate_table = jnp.zeros((block_count, EXPERTS * CAP), jnp.float32).at[block_ids, slot_of].set(gate_values.reshape(block_count, block_rows * TOPK))
    token_table = jnp.transpose(token_table.reshape(block_count, EXPERTS, CAP), (1, 0, 2)).reshape(EXPERTS, block_count * CAP)
    gate_table = jnp.transpose(gate_table.reshape(block_count, EXPERTS, CAP), (1, 0, 2)).reshape(EXPERTS, block_count * CAP)
    slice_width = FF // SETS

    def expert_step(moe_total, expert_item):
        gate_mat, up_mat, down_mat, token_ids, gate_vals = expert_item
        present = token_ids >= 0
        safe_ids = jnp.maximum(token_ids, 0)
        rows_in = normed[safe_ids]
        gate_pre = jnp.dot(rows_in, gate_mat, preferred_element_type=jnp.float32)
        up_pre = jnp.dot(rows_in, up_mat, preferred_element_type=jnp.float32)
        activity = (jax.nn.silu(gate_pre) * up_pre).astype(jnp.bfloat16)
        contrib = jnp.zeros((rows_in.shape[0], D), jnp.float32)
        for slice_index in range(SETS):
            slice_part = jnp.dot(activity[:, slice_index * slice_width:(slice_index + 1) * slice_width], down_mat[slice_index * slice_width:(slice_index + 1) * slice_width], preferred_element_type=jnp.float32)
            slice_part = lax.optimization_barrier(slice_part.astype(jnp.bfloat16)).astype(jnp.float32)
            contrib = contrib + gate_vals[:, None] * slice_part
        contrib = jnp.where(present[:, None], contrib, 0.0)
        return (moe_total.at[safe_ids].add(contrib), None)
    moe_total, unused = lax.scan(expert_step, jnp.zeros((token_count, D), jnp.float32), (gate_w, up_w, down_w, token_table, gate_table))
    return (residual + moe_total).astype(jnp.bfloat16).reshape(REQS, DRAFT, D)
```

```python
import jax
import jax.numpy as jnp
from jax import lax
from jax.experimental import pallas as pl
from jax.experimental.pallas import tpu as pltpu
from jax.sharding import PartitionSpec as P

D = 2048
H = 16
HD = 128
FF = 1024
EXPERTS = 64
TOPK = 8
DRAFT = 64
PAGE = 16
PPD = 12
SETS = 8
KEYS = PPD * PAGE
ROWS = KEYS + 16
TOK = DRAFT // SETS
WIDE = D + 2 * EXPERTS
STAT = DRAFT + 8
BLK = FF // SETS

NEG_FILL = -1e30
EPS_NORM = 1e-06
VMEM_LIMIT = 56 * 1024 * 1024


def nt(a, b):
    return lax.dot_general(a, b, (((1,), (1,)), ((), ())), preferred_element_type=jnp.float32)


def tn(a, b):
    return lax.dot_general(a, b, (((0,), (0,)), ((), ())), preferred_element_type=jnp.float32)


def nn(a, b):
    return lax.dot_general(a, b, (((1,), (0,)), ((), ())), preferred_element_type=jnp.float32)


def attention_kernel(
    table, info, q_ref, parents_ref, draft_ref, pool_ref, out_ref, kbuf, vbuf, seen_ref, sems
):
    copies = []
    for page in range(PPD):
        slot = table[page]
        rows = pl.ds(page * PAGE, PAGE)
        copies.append(pltpu.make_async_copy(pool_ref.at[0, slot], kbuf.at[rows], sems.at[0, page]))
        copies.append(pltpu.make_async_copy(pool_ref.at[1, slot], vbuf.at[rows], sems.at[1, page]))
    for copy in copies:
        copy.start()
    length = info[0]
    my_set = info[1]
    pad = jnp.zeros((8, D), jnp.float32)
    kbuf[KEYS:ROWS, :] = jnp.concatenate([draft_ref[0, 0].astype(jnp.float32), pad], axis=0).astype(
        jnp.bfloat16
    )
    vbuf[KEYS:ROWS, :] = jnp.concatenate([draft_ref[1, 0].astype(jnp.float32), pad], axis=0).astype(
        jnp.bfloat16
    )
    ancestor = lax.broadcasted_iota(jnp.int32, (DRAFT, 2 * DRAFT), 0)
    token = lax.broadcasted_iota(jnp.int32, (DRAFT, 2 * DRAFT), 1) % DRAFT
    linked = jnp.where((parents_ref[...] == ancestor) | (ancestor == token), 1.0, 0.0)
    for doubling in range((DRAFT - 1).bit_length()):
        narrow = linked.astype(jnp.bfloat16)
        linked = jnp.minimum(nn(narrow[:, :DRAFT], narrow), 1.0)
    seen_ref[...] = linked
    draft_seen = seen_ref[pl.ds(pl.multiple_of(my_set * TOK, TOK), TOK), :]
    key_row = lax.broadcasted_iota(jnp.int32, (KEYS, 2 * DRAFT), 0)
    position = ((key_row // PAGE) * SETS + my_set) * PAGE + key_row % PAGE
    cache_seen = jnp.where(position < length, 1.0, 0.0)
    seen = (
        jnp.concatenate(
            [cache_seen, draft_seen, jnp.zeros((8, 2 * DRAFT), jnp.float32)], axis=0
        )
        > 0.5
    )
    own = (lax.broadcasted_iota(jnp.int32, (2 * DRAFT, 2 * HD), 0) < DRAFT) == (
        lax.broadcasted_iota(jnp.int32, (2 * DRAFT, 2 * HD), 1) < HD
    )
    stat_row = lax.broadcasted_iota(jnp.int32, (8, 2 * DRAFT), 0)
    for copy in copies:
        copy.wait()
    for pair in range(H // 2):
        cols = slice(pair * 2 * HD, (pair + 1) * 2 * HD)
        query = q_ref[0, :, cols]
        query = jnp.where(own, jnp.concatenate([query, query], axis=0), jnp.zeros((), jnp.bfloat16))
        scores = nt(kbuf[:, cols], query) * (HD**-0.5)
        scores = jnp.where(seen, scores, NEG_FILL)
        top = jnp.max(scores, axis=0, keepdims=True).astype(jnp.bfloat16).astype(jnp.float32)
        weights = jnp.where(seen, jnp.exp(scores - top), 0.0)
        total = jnp.sum(weights, axis=0, keepdims=True)
        acc = tn(weights.astype(jnp.bfloat16), vbuf[:, cols])
        total_high = total.astype(jnp.bfloat16).astype(jnp.float32)
        stats = jnp.where(
            stat_row == 0,
            top,
            jnp.where(stat_row == 1, total_high, jnp.where(stat_row == 2, total - total_high, 0.0)),
        )
        out_ref[pair, 0:DRAFT, 0:HD] = acc[:DRAFT, :HD].astype(jnp.bfloat16)
        out_ref[pair, 0:DRAFT, HD : 2 * HD] = acc[DRAFT:, HD:].astype(jnp.bfloat16)
        out_ref[pair, DRAFT:STAT, 0:HD] = stats.astype(jnp.bfloat16)
        out_ref[pair, DRAFT:STAT, HD : 2 * HD] = jnp.zeros((8, HD), jnp.bfloat16)


def attention(table, info, queries, parents, draft_kv, kv_pool):
    vmem = pl.BlockSpec(memory_space=pltpu.VMEM)
    return pl.pallas_call(
        attention_kernel,
        out_shape=jax.ShapeDtypeStruct((SETS, STAT, 2 * HD), jnp.bfloat16),
        in_specs=[
            pl.BlockSpec(memory_space=pltpu.SMEM),
            pl.BlockSpec(memory_space=pltpu.SMEM),
            vmem,
            vmem,
            vmem,
            pl.BlockSpec(memory_space=pl.ANY),
        ],
        out_specs=vmem,
        scratch_shapes=[
            pltpu.VMEM((ROWS, D), jnp.bfloat16),
            pltpu.VMEM((ROWS, D), jnp.bfloat16),
            pltpu.VMEM((DRAFT, 2 * DRAFT), jnp.float32),
            pltpu.SemaphoreType.DMA((2, PPD)),
        ],
        compiler_params=pltpu.CompilerParams(vmem_limit_bytes=VMEM_LIMIT),
        name="attention",
    )(table, info, queries, parents, draft_kv, kv_pool)


def merge_kernel(parts_ref, proj_ref, out_ref):
    stats = parts_ref[:, DRAFT:STAT, 0:HD].astype(jnp.float32)
    tops = stats[:, 0, :]
    totals = stats[:, 1, :] + stats[:, 2, :]
    scale = jnp.exp(tops - jnp.max(tops, axis=0, keepdims=True))
    scale = scale / jnp.sum(scale * totals, axis=0, keepdims=True)
    scale = jnp.transpose(scale)
    heads = []
    for head in range(2):
        joined = jnp.zeros((DRAFT, HD), jnp.float32)
        for source in range(SETS):
            part = parts_ref[source, 0:DRAFT, head * HD : (head + 1) * HD].astype(jnp.float32)
            joined = joined + part * scale[head * DRAFT : (head + 1) * DRAFT, source : source + 1]
        heads.append(joined.astype(jnp.bfloat16))
    out_ref[...] = nn(jnp.concatenate(heads, axis=1), proj_ref[...]).astype(jnp.bfloat16)


def merge(parts, out_proj):
    return pl.pallas_call(
        merge_kernel,
        out_shape=jax.ShapeDtypeStruct((DRAFT, D), jnp.bfloat16),
        compiler_params=pltpu.CompilerParams(vmem_limit_bytes=VMEM_LIMIT),
        name="merge",
    )(parts, out_proj)


def norm_kernel(my_set, parts_ref, hidden_ref, gain_ref, router_ref, routes_ref, residual_ref, row_ref):
    residual = hidden_ref[0].astype(jnp.float32)
    for source in range(SETS):
        residual = residual + parts_ref[source].astype(jnp.float32)
    residual_ref[...] = residual
    mean_sq = jnp.mean(residual * residual, axis=1, keepdims=True)
    normed = (residual * lax.rsqrt(mean_sq + EPS_NORM) * gain_ref[...].astype(jnp.float32)).astype(
        jnp.bfloat16
    )
    logits = nn(normed, router_ref[...])
    gates = 1.0 / (1.0 + jnp.exp(-logits))
    expert = lax.broadcasted_iota(jnp.int32, (TOK, EXPERTS), 1)
    routes = routes_ref[0]
    chosen = routes[:, 0:1] == expert
    for pick in range(1, TOPK):
        chosen = chosen | (routes[:, pick : pick + 1] == expert)
    gates = jnp.where(chosen, gates, 0.0)
    high = gates.astype(jnp.bfloat16).astype(jnp.float32)
    row_ref[:, 0:D] = normed
    row_ref[:, D:WIDE] = jnp.concatenate([high, gates - high], axis=1).astype(jnp.bfloat16)


def norm(my_set, parts, hidden, norm_gain, router, routes):
    whole = lambda *shape: pl.BlockSpec(shape, lambda i, s: (0,) * len(shape))
    return pl.pallas_call(
        norm_kernel,
        out_shape=(
            jax.ShapeDtypeStruct((TOK, D), jnp.float32),
            jax.ShapeDtypeStruct((TOK, WIDE), jnp.bfloat16),
        ),
        grid_spec=pltpu.PrefetchScalarGridSpec(
            num_scalar_prefetch=1,
            grid=(1,),
            in_specs=[
                whole(SETS, TOK, D),
                pl.BlockSpec((1, TOK, D), lambda i, s: (0, s[0], 0)),
                whole(1, D),
                whole(D, EXPERTS),
                pl.BlockSpec((1, TOK, TOPK), lambda i, s: (0, s[0], 0)),
            ],
            out_specs=(whole(TOK, D), whole(TOK, WIDE)),
        ),
        compiler_params=pltpu.CompilerParams(vmem_limit_bytes=VMEM_LIMIT),
        name="norm",
    )(my_set, parts, hidden, norm_gain, router, routes)


def expert_kernel(my_expert, rows_ref, in_ref, down_ref, out_ref, act_ref, gate_ref):
    step = pl.program_id(0)

    @pl.when(step == 0)
    def _():
        gates = rows_ref[:, D:WIDE].astype(jnp.float32)
        lane = lax.broadcasted_iota(jnp.int32, gates.shape, 1) % EXPERTS
        gate_ref[...] = jnp.sum(jnp.where(lane == my_expert[0], gates, 0.0), axis=1, keepdims=True)

    @pl.when(step < SETS)
    def _():
        both = nn(rows_ref[:, 0:D], in_ref[0])
        gate, up = both[:, :BLK], both[:, BLK:]
        act = gate / (1.0 + jnp.exp(-gate)) * up
        act_ref[:, pl.ds(pl.multiple_of(step * BLK, BLK), BLK)] = act.astype(jnp.bfloat16)

    @pl.when(step >= SETS)
    def _():
        down = down_ref[...].reshape(FF, D // SETS)
        out_ref[...] = (nn(act_ref[...], down) * gate_ref[...]).astype(jnp.bfloat16)


def expert(my_expert, rows, weights):
    count = rows.shape[0]
    width = D // SETS
    return pl.pallas_call(
        expert_kernel,
        out_shape=jax.ShapeDtypeStruct((count, D), jnp.bfloat16),
        grid_spec=pltpu.PrefetchScalarGridSpec(
            num_scalar_prefetch=1,
            grid=(2 * SETS,),
            in_specs=[
                pl.BlockSpec((count, WIDE), lambda i, e: (0, 0)),
                pl.BlockSpec((1, D, width), lambda i, e: (jnp.minimum(i, SETS - 1), 0, 0)),
                pl.BlockSpec(
                    (SETS, BLK, width), lambda i, e: (0, D // BLK + jnp.maximum(i - SETS, 0), 0)
                ),
            ],
            out_specs=pl.BlockSpec((count, width), lambda i, e: (0, jnp.maximum(i - SETS, 0))),
            scratch_shapes=[
                pltpu.VMEM((count, FF), jnp.bfloat16),
                pltpu.VMEM((count, 1), jnp.float32),
            ],
        ),
        compiler_params=pltpu.CompilerParams(vmem_limit_bytes=VMEM_LIMIT),
        name="expert",
    )(my_expert, rows, weights, weights)


def local(
    queries,
    draft_kv,
    kv_pool,
    page_table,
    cache_lens,
    parents,
    hidden,
    norm_gain,
    out_proj,
    router,
    routes,
    gate_w,
    up_w,
    down_w,
):
    my_set = lax.axis_index("exp").astype(jnp.int32)
    kv_count = lax.axis_size("kv")
    seq_count = lax.axis_size("seq")
    my_expert = (lax.axis_index("kv") * seq_count + lax.axis_index("seq")).astype(jnp.int32)
    width = D // SETS
    packed = jnp.concatenate(
        [
            jnp.concatenate([gate_w[0], up_w[0]], axis=1),
            jnp.transpose(down_w[0].reshape(BLK, SETS, width), (1, 0, 2)).reshape(SETS * BLK, width),
        ],
        axis=0,
    )
    weights = lax.all_gather(packed, "exp")
    info = jnp.concatenate([cache_lens, my_set.reshape(1)])
    partials = attention(
        page_table.reshape(PPD),
        info,
        queries,
        jnp.concatenate([parents, parents], axis=1),
        draft_kv,
        kv_pool,
    )
    parts = lax.all_to_all(partials, "exp", 0, 0, tiled=True)
    projected = merge(parts, out_proj)
    shares = lax.all_to_all(projected.reshape(SETS, TOK, D), "exp", 0, 0, tiled=True)
    residual, row = norm(
        my_set.reshape(1), shares, hidden, norm_gain.reshape(1, D), router, routes
    )
    along_seq = lax.all_gather(row, "seq").reshape(1, seq_count * TOK, WIDE)
    rows = lax.all_to_all(
        jnp.broadcast_to(along_seq, (kv_count, seq_count * TOK, WIDE)), "kv", 0, 0, tiled=True
    ).reshape(kv_count * seq_count * TOK, WIDE)
    finished = expert(my_expert.reshape(1), rows, weights)
    back = lax.all_to_all(finished.reshape(kv_count, seq_count * TOK, D), "kv", 0, 0, tiled=True)
    back = jnp.sum(back.astype(jnp.float32), axis=0).astype(jnp.bfloat16)
    back = lax.all_to_all(back.reshape(seq_count, TOK, D), "seq", 0, 0, tiled=True)
    total = (residual + jnp.sum(back.astype(jnp.float32), axis=0)).astype(jnp.bfloat16)
    columns = jnp.transpose(total.reshape(TOK, SETS, width), (1, 0, 2))
    return lax.all_to_all(columns, "exp", 0, 0, tiled=True).reshape(1, DRAFT, width)


def solution(mesh):
    in_specs = (
        P(("kv", "seq"), None, None),
        P(None, ("kv", "seq"), "exp", None),
        P(None, ("kv", "seq", "exp"), None, None),
        P(("kv", "seq"), None, "exp"),
        P(("kv", "seq")),
        P(("kv", "seq"), None),
        P(("kv", "seq"), None, None),
        P(),
        P("exp", None),
        P(),
        P(("kv", "seq"), None, None),
        P(("kv", "seq"), None, "exp"),
        P(("kv", "seq"), None, "exp"),
        P(("kv", "seq"), "exp", None),
    )
    out_specs = P(("kv", "seq"), None, "exp")
    return jax.shard_map(local, mesh=mesh, in_specs=in_specs, out_specs=out_specs, check_vma=False)
```

```python
import functools

import jax
import jax.numpy as jnp
from jax import lax
from jax.experimental import pallas as pl
from jax.experimental.pallas import tpu as pltpu
from jax.sharding import PartitionSpec as P

D = 2048
H = 16
HD = 128
FF = 1024
EXPERTS = 64
TOPK = 8
DRAFT = 64
PAGE = 16
PPD = 12
SETS = 8
KEYS = PPD * PAGE
ROWS = KEYS + 16
TOK = DRAFT // SETS
WIDE = D + 2 * EXPERTS
STAT = DRAFT + 8
BLK = FF // SETS

NEG_FILL = -1e30
EPS_NORM = 1e-06
VMEM_LIMIT = 16 * 1024 * 1024
EXPERT_VMEM = 24 * 1024 * 1024


def nt(a, b):
    return lax.dot_general(a, b, (((1,), (1,)), ((), ())), preferred_element_type=jnp.float32)


def tn(a, b):
    return lax.dot_general(a, b, (((0,), (0,)), ((), ())), preferred_element_type=jnp.float32)


def nn(a, b):
    return lax.dot_general(a, b, (((1,), (0,)), ((), ())), preferred_element_type=jnp.float32)


def attention_kernel(
    table, lens, q_ref, parents_ref, draft_ref, pool_ref, out_ref, kbuf, vbuf, seen_ref, sems
):
    copies = []
    for page in range(PPD):
        slot = table[page]
        rows = pl.ds(page * PAGE, PAGE)
        copies.append(pltpu.make_async_copy(pool_ref.at[0, slot], kbuf.at[rows], sems.at[0, page]))
        copies.append(pltpu.make_async_copy(pool_ref.at[1, slot], vbuf.at[rows], sems.at[1, page]))
    for copy in copies:
        copy.start()
    length = lens[0]
    my_set = lax.axis_index("exp")
    pad = jnp.zeros((8, D), jnp.float32)
    kbuf[KEYS:ROWS, :] = jnp.concatenate([draft_ref[0, 0].astype(jnp.float32), pad], axis=0).astype(
        jnp.bfloat16
    )
    vbuf[KEYS:ROWS, :] = jnp.concatenate([draft_ref[1, 0].astype(jnp.float32), pad], axis=0).astype(
        jnp.bfloat16
    )
    ancestor = lax.broadcasted_iota(jnp.int32, (DRAFT, 2 * DRAFT), 0)
    token = lax.broadcasted_iota(jnp.int32, (DRAFT, 2 * DRAFT), 1) % DRAFT
    parents = jnp.concatenate([parents_ref[...], parents_ref[...]], axis=1)
    linked = jnp.where((parents == ancestor) | (ancestor == token), 1.0, 0.0)
    for doubling in range((DRAFT - 1).bit_length()):
        narrow = linked.astype(jnp.bfloat16)
        linked = jnp.minimum(nn(narrow[:, :DRAFT], narrow), 1.0)
    seen_ref[...] = linked
    draft_seen = seen_ref[pl.ds(pl.multiple_of(my_set * TOK, TOK), TOK), :]
    key_row = lax.broadcasted_iota(jnp.int32, (KEYS, 2 * DRAFT), 0)
    position = ((key_row // PAGE) * SETS + my_set) * PAGE + key_row % PAGE
    cache_seen = jnp.where(position < length, 1.0, 0.0)
    seen = (
        jnp.concatenate(
            [cache_seen, draft_seen, jnp.zeros((8, 2 * DRAFT), jnp.float32)], axis=0
        )
        > 0.5
    )
    own = (lax.broadcasted_iota(jnp.int32, (2 * DRAFT, 2 * HD), 0) < DRAFT) == (
        lax.broadcasted_iota(jnp.int32, (2 * DRAFT, 2 * HD), 1) < HD
    )
    stat_row = lax.broadcasted_iota(jnp.int32, (8, 2 * DRAFT), 0)
    for copy in copies:
        copy.wait()
    for pair in range(H // 2):
        cols = slice(pair * 2 * HD, (pair + 1) * 2 * HD)
        query = q_ref[0, :, cols]
        query = jnp.where(own, jnp.concatenate([query, query], axis=0), jnp.zeros((), jnp.bfloat16))
        scores = nt(kbuf[:, cols], query) * (HD**-0.5)
        scores = jnp.where(seen, scores, NEG_FILL)
        top = jnp.max(scores, axis=0, keepdims=True).astype(jnp.bfloat16).astype(jnp.float32)
        weights = jnp.where(seen, jnp.exp(scores - top), 0.0)
        total = jnp.sum(weights, axis=0, keepdims=True)
        acc = tn(weights.astype(jnp.bfloat16), vbuf[:, cols])
        total_high = total.astype(jnp.bfloat16).astype(jnp.float32)
        stats = jnp.where(
            stat_row == 0,
            top,
            jnp.where(stat_row == 1, total_high, jnp.where(stat_row == 2, total - total_high, 0.0)),
        )
        out_ref[pair, 0:DRAFT, 0:HD] = acc[:DRAFT, :HD].astype(jnp.bfloat16)
        out_ref[pair, 0:DRAFT, HD : 2 * HD] = acc[DRAFT:, HD:].astype(jnp.bfloat16)
        out_ref[pair, DRAFT:STAT, 0:HD] = stats.astype(jnp.bfloat16)
        out_ref[pair, DRAFT:STAT, HD : 2 * HD] = jnp.zeros((8, HD), jnp.bfloat16)


def attention(table, lens, queries, parents, draft_kv, kv_pool):
    vmem = pl.BlockSpec(memory_space=pltpu.VMEM)
    return pl.pallas_call(
        attention_kernel,
        out_shape=jax.ShapeDtypeStruct((SETS, STAT, 2 * HD), jnp.bfloat16),
        in_specs=[
            pl.BlockSpec(memory_space=pltpu.SMEM),
            pl.BlockSpec(memory_space=pltpu.SMEM),
            vmem,
            vmem,
            vmem,
            pl.BlockSpec(memory_space=pl.ANY),
        ],
        out_specs=vmem,
        scratch_shapes=[
            pltpu.VMEM((ROWS, D), jnp.bfloat16),
            pltpu.VMEM((ROWS, D), jnp.bfloat16),
            pltpu.VMEM((DRAFT, 2 * DRAFT), jnp.float32),
            pltpu.SemaphoreType.DMA((2, PPD)),
        ],
        compiler_params=pltpu.CompilerParams(vmem_limit_bytes=VMEM_LIMIT),
        name="attention",
    )(table, lens, queries, parents, draft_kv, kv_pool)


def merge_kernel(parts_ref, proj_ref, out_ref):
    stats = parts_ref[:, DRAFT:STAT, 0:HD].astype(jnp.float32)
    tops = stats[:, 0, :]
    totals = stats[:, 1, :] + stats[:, 2, :]
    scale = jnp.exp(tops - jnp.max(tops, axis=0, keepdims=True))
    scale = scale / jnp.sum(scale * totals, axis=0, keepdims=True)
    scale = jnp.transpose(scale)
    heads = []
    for head in range(2):
        joined = jnp.zeros((DRAFT, HD), jnp.float32)
        for source in range(SETS):
            part = parts_ref[source, 0:DRAFT, head * HD : (head + 1) * HD].astype(jnp.float32)
            joined = joined + part * scale[head * DRAFT : (head + 1) * DRAFT, source : source + 1]
        heads.append(joined.astype(jnp.bfloat16))
    out_ref[...] = nn(jnp.concatenate(heads, axis=1), proj_ref[...]).astype(jnp.bfloat16)


def merge(parts, out_proj):
    return pl.pallas_call(
        merge_kernel,
        out_shape=jax.ShapeDtypeStruct((DRAFT, D), jnp.bfloat16),
        compiler_params=pltpu.CompilerParams(vmem_limit_bytes=VMEM_LIMIT),
        name="merge",
    )(parts, out_proj)


def norm_kernel(my_set, parts_ref, hidden_ref, gain_ref, router_ref, routes_ref, residual_ref, row_ref):
    residual = hidden_ref[0].astype(jnp.float32)
    for source in range(SETS):
        residual = residual + parts_ref[source].astype(jnp.float32)
    residual_ref[...] = residual
    mean_sq = jnp.mean(residual * residual, axis=1, keepdims=True)
    normed = (residual * lax.rsqrt(mean_sq + EPS_NORM) * gain_ref[...].astype(jnp.float32)).astype(
        jnp.bfloat16
    )
    logits = nn(normed, router_ref[...])
    gates = 1.0 / (1.0 + jnp.exp(-logits))
    expert = lax.broadcasted_iota(jnp.int32, (TOK, EXPERTS), 1)
    routes = routes_ref[0]
    chosen = routes[:, 0:1] == expert
    for pick in range(1, TOPK):
        chosen = chosen | (routes[:, pick : pick + 1] == expert)
    gates = jnp.where(chosen, gates, 0.0)
    high = gates.astype(jnp.bfloat16).astype(jnp.float32)
    row_ref[:, 0:D] = normed
    row_ref[:, D:WIDE] = jnp.concatenate([high, gates - high], axis=1).astype(jnp.bfloat16)


def norm(my_set, parts, hidden, norm_gain, router, routes):
    whole = lambda *shape: pl.BlockSpec(shape, lambda i, s: (0,) * len(shape))
    return pl.pallas_call(
        norm_kernel,
        out_shape=(
            jax.ShapeDtypeStruct((TOK, D), jnp.float32),
            jax.ShapeDtypeStruct((TOK, WIDE), jnp.bfloat16),
        ),
        grid_spec=pltpu.PrefetchScalarGridSpec(
            num_scalar_prefetch=1,
            grid=(1,),
            in_specs=[
                whole(SETS, TOK, D),
                pl.BlockSpec((1, TOK, D), lambda i, s: (0, s[0], 0)),
                whole(1, D),
                whole(D, EXPERTS),
                pl.BlockSpec((1, TOK, TOPK), lambda i, s: (0, s[0], 0)),
            ],
            out_specs=(whole(TOK, D), whole(TOK, WIDE)),
        ),
        compiler_params=pltpu.CompilerParams(vmem_limit_bytes=VMEM_LIMIT),
        name="norm",
    )(my_set, parts, hidden, norm_gain, router, routes)


def expert_rows(my_expert, rows_ref, weights_ref, out_ref, act_ref, before_block):
    gates = rows_ref[:, D:WIDE].astype(jnp.float32)
    lane = lax.broadcasted_iota(jnp.int32, gates.shape, 1) % EXPERTS
    scale = jnp.sum(jnp.where(lane == my_expert, gates, 0.0), axis=1, keepdims=True)
    for block in range(SETS):
        before_block(block)
        both = nn(rows_ref[:, 0:D], weights_ref[block, 0:D, :])
        gate, up = both[:, :BLK], both[:, BLK:]
        act = gate / (1.0 + jnp.exp(-gate)) * up
        act_ref[:, block * BLK : (block + 1) * BLK] = act.astype(jnp.bfloat16)
    width = D // SETS
    for block in range(SETS):
        down = weights_ref[:, D + block * BLK : D + (block + 1) * BLK, :].reshape(FF, width)
        out = nn(act_ref[...], down) * scale
        out_ref[:, block * width : (block + 1) * width] = out.astype(jnp.bfloat16)


def own_kernel(my_expert, rows_ref, weights_ref, out_ref, kept_ref, act_ref, sems):
    copies = [
        pltpu.make_async_copy(weights_ref.at[block], kept_ref.at[block], sems.at[block])
        for block in range(SETS)
    ]
    for copy in copies:
        copy.start()
    expert_rows(
        my_expert[0], rows_ref, kept_ref, out_ref, act_ref, lambda block: copies[block].wait()
    )


def other_kernel(count, my_expert, *refs):
    rows_refs, weights_ref, out_refs, act_ref = (
        refs[:count],
        refs[count],
        refs[count + 1 : 2 * count + 1],
        refs[2 * count + 1],
    )
    for rows_ref, out_ref in zip(rows_refs, out_refs):
        expert_rows(my_expert[0], rows_ref, weights_ref, out_ref, act_ref, lambda block: None)


def own_expert(my_expert, rows, weights):
    count = rows.shape[0]
    vmem = pl.BlockSpec(memory_space=pltpu.VMEM)
    return pl.pallas_call(
        own_kernel,
        out_shape=(
            jax.ShapeDtypeStruct((count, D), jnp.bfloat16),
            pltpu.VMEM(weights.shape, weights.dtype),
        ),
        in_specs=[
            pl.BlockSpec(memory_space=pltpu.SMEM),
            vmem,
            pl.BlockSpec(memory_space=pl.ANY),
        ],
        out_specs=(vmem, vmem),
        scratch_shapes=[
            pltpu.VMEM((count, FF), jnp.bfloat16),
            pltpu.SemaphoreType.DMA((SETS,)),
        ],
        compiler_params=pltpu.CompilerParams(vmem_limit_bytes=EXPERT_VMEM),
        name="own_expert",
    )(my_expert, rows, pltpu.with_memory_space_constraint(weights, pltpu.HBM))


def other_expert(my_expert, weights, *blocks):
    rows = blocks[0].shape[0]
    vmem = pl.BlockSpec(memory_space=pltpu.VMEM)
    return pl.pallas_call(
        functools.partial(other_kernel, len(blocks)),
        out_shape=tuple(jax.ShapeDtypeStruct((rows, D), jnp.bfloat16) for block in blocks),
        in_specs=[pl.BlockSpec(memory_space=pltpu.SMEM)] + [vmem] * (len(blocks) + 1),
        out_specs=(vmem,) * len(blocks),
        scratch_shapes=[pltpu.VMEM((rows, FF), jnp.bfloat16)],
        compiler_params=pltpu.CompilerParams(vmem_limit_bytes=EXPERT_VMEM),
        name="other_expert",
    )(my_expert, *blocks, pltpu.with_memory_space_constraint(weights, pltpu.VMEM))


def shifted(value, axis, count, by):
    return lax.ppermute(value, axis, [(i, (i + by) % count) for i in range(count)])


def local(
    queries,
    draft_kv,
    kv_pool,
    page_table,
    cache_lens,
    parents,
    hidden,
    norm_gain,
    out_proj,
    router,
    routes,
    gate_w,
    up_w,
    down_w,
):
    my_set = lax.axis_index("exp").astype(jnp.int32)
    kv_count = lax.axis_size("kv")
    seq_count = lax.axis_size("seq")
    my_expert = (lax.axis_index("kv") * seq_count + lax.axis_index("seq")).astype(jnp.int32)
    width = D // SETS
    packed = jnp.concatenate(
        [
            jnp.concatenate([gate_w[0], up_w[0]], axis=1),
            jnp.transpose(down_w[0].reshape(BLK, SETS, width), (1, 0, 2)).reshape(SETS * BLK, width),
        ],
        axis=0,
    )
    weights = lax.all_gather(packed, "exp")
    partials = attention(
        page_table.reshape(PPD), cache_lens, queries, parents, draft_kv, kv_pool
    )
    parts = lax.all_to_all(partials, "exp", 0, 0, tiled=True)
    projected = merge(parts, out_proj)
    shares = lax.all_to_all(projected.reshape(SETS, TOK, D), "exp", 0, 0, tiled=True)
    residual, row = norm(
        my_set.reshape(1), shares, hidden, norm_gain.reshape(1, D), router, routes
    )
    rows = lax.all_gather(row, "seq").reshape(seq_count * TOK, WIDE)
    ident = my_expert.reshape(1)
    arrived = {by: shifted(rows, "kv", kv_count, by) for by in range(1, kv_count)}
    total, kept = own_expert(ident, rows, weights)
    near = other_expert(ident, kept, arrived[1], arrived[kv_count - 1])
    returned = [
        shifted(near[0], "kv", kv_count, -1),
        shifted(near[1], "kv", kv_count, 1),
    ]
    for by in range(2, kv_count - 1):
        (far,) = other_expert(ident, kept, arrived[by])
        returned.append(shifted(far, "kv", kv_count, -by))
    total = total.astype(jnp.float32)
    for part in returned:
        total = total + part.astype(jnp.float32)
    back = total.astype(jnp.bfloat16).reshape(seq_count, TOK, D)
    back = lax.all_to_all(back, "seq", 0, 0, tiled=True)
    output = (residual + jnp.sum(back.astype(jnp.float32), axis=0)).astype(jnp.bfloat16)
    columns = jnp.transpose(output.reshape(TOK, SETS, width), (1, 0, 2))
    return lax.all_to_all(columns, "exp", 0, 0, tiled=True).reshape(1, DRAFT, width)


def solution(mesh):
    in_specs = (
        P(("kv", "seq"), None, None),
        P(None, ("kv", "seq"), "exp", None),
        P(None, ("kv", "seq", "exp"), None, None),
        P(("kv", "seq"), None, "exp"),
        P(("kv", "seq")),
        P(("kv", "seq"), None),
        P(("kv", "seq"), None, None),
        P(),
        P("exp", None),
        P(),
        P(("kv", "seq"), None, None),
        P(("kv", "seq"), None, "exp"),
        P(("kv", "seq"), None, "exp"),
        P(("kv", "seq"), "exp", None),
    )
    out_specs = P(("kv", "seq"), None, "exp")
    return jax.shard_map(local, mesh=mesh, in_specs=in_specs, out_specs=out_specs, check_vma=False)
```

```python
import functools

import jax
import jax.numpy as jnp
from jax import lax
from jax.experimental import pallas as pl
from jax.experimental.pallas import tpu as pltpu
from jax.sharding import PartitionSpec as P

D = 2048
H = 16
HD = 128
FF = 1024
EXPERTS = 64
TOPK = 8
DRAFT = 64
PAGE = 16
PPD = 12
SETS = 8
KEYS = PPD * PAGE
ROWS = KEYS + 16
TOK = DRAFT // SETS
WIDE = D + 2 * EXPERTS
STAT = DRAFT + 8
BLK = FF // SETS

NEG_FILL = -1e30
EPS_NORM = 1e-06
VMEM_LIMIT = 16 * 1024 * 1024
EXPERT_VMEM = 24 * 1024 * 1024


def nt(a, b):
    return lax.dot_general(a, b, (((1,), (1,)), ((), ())), preferred_element_type=jnp.float32)


def tn(a, b):
    return lax.dot_general(a, b, (((0,), (0,)), ((), ())), preferred_element_type=jnp.float32)


def nn(a, b):
    return lax.dot_general(a, b, (((1,), (0,)), ((), ())), preferred_element_type=jnp.float32)


def attention_kernel(
    table, lens, q_ref, parents_ref, draft_ref, pool_ref, out_ref, kbuf, vbuf, seen_ref, sems
):
    copies = []
    for page in range(PPD):
        slot = table[page]
        rows = pl.ds(page * PAGE, PAGE)
        copies.append(pltpu.make_async_copy(pool_ref.at[0, slot], kbuf.at[rows], sems.at[0, page]))
        copies.append(pltpu.make_async_copy(pool_ref.at[1, slot], vbuf.at[rows], sems.at[1, page]))
    for copy in copies:
        copy.start()
    length = lens[0]
    my_set = lax.axis_index("exp")
    pad = jnp.zeros((8, D), jnp.float32)
    kbuf[KEYS:ROWS, :] = jnp.concatenate([draft_ref[0, 0].astype(jnp.float32), pad], axis=0).astype(
        jnp.bfloat16
    )
    vbuf[KEYS:ROWS, :] = jnp.concatenate([draft_ref[1, 0].astype(jnp.float32), pad], axis=0).astype(
        jnp.bfloat16
    )
    ancestor = lax.broadcasted_iota(jnp.int32, (DRAFT, 2 * DRAFT), 0)
    token = lax.broadcasted_iota(jnp.int32, (DRAFT, 2 * DRAFT), 1) % DRAFT
    parents = jnp.concatenate([parents_ref[...], parents_ref[...]], axis=1)
    linked = jnp.where((parents == ancestor) | (ancestor == token), 1.0, 0.0)
    for doubling in range((DRAFT - 1).bit_length()):
        narrow = linked.astype(jnp.bfloat16)
        linked = jnp.minimum(nn(narrow[:, :DRAFT], narrow), 1.0)
    seen_ref[...] = linked
    draft_seen = seen_ref[pl.ds(pl.multiple_of(my_set * TOK, TOK), TOK), :]
    key_row = lax.broadcasted_iota(jnp.int32, (KEYS, 2 * DRAFT), 0)
    position = ((key_row // PAGE) * SETS + my_set) * PAGE + key_row % PAGE
    cache_seen = jnp.where(position < length, 1.0, 0.0)
    seen = (
        jnp.concatenate(
            [cache_seen, draft_seen, jnp.zeros((8, 2 * DRAFT), jnp.float32)], axis=0
        )
        > 0.5
    )
    own = (lax.broadcasted_iota(jnp.int32, (2 * DRAFT, 2 * HD), 0) < DRAFT) == (
        lax.broadcasted_iota(jnp.int32, (2 * DRAFT, 2 * HD), 1) < HD
    )
    stat_row = lax.broadcasted_iota(jnp.int32, (8, 2 * DRAFT), 0)
    for copy in copies:
        copy.wait()
    for pair in range(H // 2):
        cols = slice(pair * 2 * HD, (pair + 1) * 2 * HD)
        query = q_ref[0, :, cols]
        query = jnp.where(own, jnp.concatenate([query, query], axis=0), jnp.zeros((), jnp.bfloat16))
        scores = nt(kbuf[:, cols], query) * (HD**-0.5)
        scores = jnp.where(seen, scores, NEG_FILL)
        top = jnp.max(scores, axis=0, keepdims=True).astype(jnp.bfloat16).astype(jnp.float32)
        weights = jnp.where(seen, jnp.exp(scores - top), 0.0)
        total = jnp.sum(weights, axis=0, keepdims=True)
        acc = tn(weights.astype(jnp.bfloat16), vbuf[:, cols])
        total_high = total.astype(jnp.bfloat16).astype(jnp.float32)
        stats = jnp.where(
            stat_row == 0,
            top,
            jnp.where(stat_row == 1, total_high, jnp.where(stat_row == 2, total - total_high, 0.0)),
        )
        out_ref[pair, 0:DRAFT, 0:HD] = acc[:DRAFT, :HD].astype(jnp.bfloat16)
        out_ref[pair, 0:DRAFT, HD : 2 * HD] = acc[DRAFT:, HD:].astype(jnp.bfloat16)
        out_ref[pair, DRAFT:STAT, 0:HD] = stats.astype(jnp.bfloat16)
        out_ref[pair, DRAFT:STAT, HD : 2 * HD] = jnp.zeros((8, HD), jnp.bfloat16)


def attention(table, lens, queries, parents, draft_kv, kv_pool):
    vmem = pl.BlockSpec(memory_space=pltpu.VMEM)
    return pl.pallas_call(
        attention_kernel,
        out_shape=jax.ShapeDtypeStruct((SETS, STAT, 2 * HD), jnp.bfloat16),
        in_specs=[
            pl.BlockSpec(memory_space=pltpu.SMEM),
            pl.BlockSpec(memory_space=pltpu.SMEM),
            vmem,
            vmem,
            vmem,
            pl.BlockSpec(memory_space=pl.ANY),
        ],
        out_specs=vmem,
        scratch_shapes=[
            pltpu.VMEM((ROWS, D), jnp.bfloat16),
            pltpu.VMEM((ROWS, D), jnp.bfloat16),
            pltpu.VMEM((DRAFT, 2 * DRAFT), jnp.float32),
            pltpu.SemaphoreType.DMA((2, PPD)),
        ],
        compiler_params=pltpu.CompilerParams(vmem_limit_bytes=VMEM_LIMIT),
        name="attention",
    )(table, lens, queries, parents, draft_kv, kv_pool)


def merge_kernel(parts_ref, proj_ref, out_ref):
    stats = parts_ref[:, DRAFT:STAT, 0:HD].astype(jnp.float32)
    tops = stats[:, 0, :]
    totals = stats[:, 1, :] + stats[:, 2, :]
    scale = jnp.exp(tops - jnp.max(tops, axis=0, keepdims=True))
    scale = scale / jnp.sum(scale * totals, axis=0, keepdims=True)
    scale = jnp.transpose(scale)
    heads = []
    for head in range(2):
        joined = jnp.zeros((DRAFT, HD), jnp.float32)
        for source in range(SETS):
            part = parts_ref[source, 0:DRAFT, head * HD : (head + 1) * HD].astype(jnp.float32)
            joined = joined + part * scale[head * DRAFT : (head + 1) * DRAFT, source : source + 1]
        heads.append(joined.astype(jnp.bfloat16))
    out_ref[...] = nn(jnp.concatenate(heads, axis=1), proj_ref[...]).astype(jnp.bfloat16)


def merge(parts, out_proj):
    return pl.pallas_call(
        merge_kernel,
        out_shape=jax.ShapeDtypeStruct((DRAFT, D), jnp.bfloat16),
        compiler_params=pltpu.CompilerParams(vmem_limit_bytes=VMEM_LIMIT),
        name="merge",
    )(parts, out_proj)


def norm_kernel(my_set, parts_ref, hidden_ref, gain_ref, router_ref, routes_ref, residual_ref, row_ref):
    residual = hidden_ref[0].astype(jnp.float32)
    for source in range(SETS):
        residual = residual + parts_ref[source].astype(jnp.float32)
    residual_ref[...] = residual
    mean_sq = jnp.mean(residual * residual, axis=1, keepdims=True)
    normed = (residual * lax.rsqrt(mean_sq + EPS_NORM) * gain_ref[...].astype(jnp.float32)).astype(
        jnp.bfloat16
    )
    logits = nn(normed, router_ref[...])
    gates = 1.0 / (1.0 + jnp.exp(-logits))
    expert = lax.broadcasted_iota(jnp.int32, (TOK, EXPERTS), 1)
    routes = routes_ref[0]
    chosen = routes[:, 0:1] == expert
    for pick in range(1, TOPK):
        chosen = chosen | (routes[:, pick : pick + 1] == expert)
    gates = jnp.where(chosen, gates, 0.0)
    high = gates.astype(jnp.bfloat16).astype(jnp.float32)
    row_ref[:, 0:D] = normed
    row_ref[:, D:WIDE] = jnp.concatenate([high, gates - high], axis=1).astype(jnp.bfloat16)


def norm(my_set, parts, hidden, norm_gain, router, routes):
    whole = lambda *shape: pl.BlockSpec(shape, lambda i, s: (0,) * len(shape))
    return pl.pallas_call(
        norm_kernel,
        out_shape=(
            jax.ShapeDtypeStruct((TOK, D), jnp.float32),
            jax.ShapeDtypeStruct((TOK, WIDE), jnp.bfloat16),
        ),
        grid_spec=pltpu.PrefetchScalarGridSpec(
            num_scalar_prefetch=1,
            grid=(1,),
            in_specs=[
                whole(SETS, TOK, D),
                pl.BlockSpec((1, TOK, D), lambda i, s: (0, s[0], 0)),
                whole(1, D),
                whole(D, EXPERTS),
                pl.BlockSpec((1, TOK, TOPK), lambda i, s: (0, s[0], 0)),
            ],
            out_specs=(whole(TOK, D), whole(TOK, WIDE)),
        ),
        compiler_params=pltpu.CompilerParams(vmem_limit_bytes=VMEM_LIMIT),
        name="norm",
    )(my_set, parts, hidden, norm_gain, router, routes)


def pack_kernel(gate_ref, up_ref, down_ref, out_ref, buf, in_sems, out_sems):
    width = D // SETS
    pieces = []
    part = D // 4
    for piece in range(4):
        rows = pl.ds(piece * part, part)
        pieces.append(
            (
                [
                    (gate_ref.at[0, rows], buf.at[rows, pl.ds(0, BLK)]),
                    (up_ref.at[0, rows], buf.at[rows, pl.ds(BLK, BLK)]),
                ],
                rows,
            )
        )
    for half in range(2):
        blocks = range(half * SETS // 2, (half + 1) * SETS // 2)
        pieces.append(
            (
                [
                    (
                        down_ref.at[0, :, pl.ds(block * width, width)],
                        buf.at[pl.ds(D + block * BLK, BLK)],
                    )
                    for block in blocks
                ],
                pl.ds(D + half * FF // 2, FF // 2),
            )
        )
    loads = []
    count = 0
    for moves, rows in pieces:
        group = []
        for source, target in moves:
            group.append(pltpu.make_async_copy(source, target, in_sems.at[count]))
            count += 1
        loads.append((group, rows))
    for group, rows in loads:
        for copy in group:
            copy.start()
    stores = []
    for index, (group, rows) in enumerate(loads):
        for copy in group:
            copy.wait()
        store = pltpu.make_async_copy(buf.at[rows], out_ref.at[rows], out_sems.at[index])
        store.start()
        stores.append(store)
    for store in stores:
        store.wait()


def pack(gate_w, up_w, down_w):
    hbm = pl.BlockSpec(memory_space=pltpu.HBM)
    width = D // SETS
    return pl.pallas_call(
        pack_kernel,
        out_shape=jax.ShapeDtypeStruct((D + FF, width), gate_w.dtype),
        in_specs=[hbm] * 3,
        out_specs=hbm,
        scratch_shapes=[
            pltpu.VMEM((D + FF, width), jnp.bfloat16),
            pltpu.SemaphoreType.DMA((16,)),
            pltpu.SemaphoreType.DMA((6,)),
        ],
        compiler_params=pltpu.CompilerParams(vmem_limit_bytes=VMEM_LIMIT),
        name="pack",
    )(*(pltpu.with_memory_space_constraint(x, pltpu.HBM) for x in (gate_w, up_w, down_w)))


def expert_rows(my_expert, rows_ref, weights_ref, store, act_ref, before_block):
    gates = rows_ref[:, D:WIDE].astype(jnp.float32)
    lane = lax.broadcasted_iota(jnp.int32, gates.shape, 1) % EXPERTS
    scale = jnp.sum(jnp.where(lane == my_expert, gates, 0.0), axis=1, keepdims=True)
    for block in range(SETS):
        before_block(block)
        both = nn(rows_ref[:, 0:D], weights_ref[block, 0:D, :])
        gate, up = both[:, :BLK], both[:, BLK:]
        act = gate / (1.0 + jnp.exp(-gate)) * up
        act_ref[:, block * BLK : (block + 1) * BLK] = act.astype(jnp.bfloat16)
    width = D // SETS
    for block in range(SETS):
        down = weights_ref[:, D + block * BLK : D + (block + 1) * BLK, :].reshape(FF, width)
        store(block, (nn(act_ref[...], down) * scale).astype(jnp.bfloat16))


def own_kernel(place, rows_ref, residual_ref, weights_ref, out_ref, kept_ref, act_ref, sems):
    copies = [
        pltpu.make_async_copy(weights_ref.at[block], kept_ref.at[block], sems.at[block])
        for block in range(SETS)
    ]
    for copy in copies:
        copy.start()
    width = D // SETS
    mine = pl.ds(pl.multiple_of(place[2] * TOK, TOK), TOK)

    def store(block, value):
        out_ref[block] = value

    expert_rows(
        place[0], rows_ref, kept_ref, store, act_ref, lambda block: copies[block].wait()
    )
    for block in range(SETS):
        own = out_ref[block, mine, :].astype(jnp.float32)
        own = own + residual_ref[:, block * width : (block + 1) * width]
        out_ref[block, mine, :] = own.astype(jnp.bfloat16)


def other_kernel(count, place, *refs):
    rows_refs, own_ref, weights_ref, out_ref, act_ref = (
        refs[:count],
        refs[count],
        refs[count + 1],
        refs[count + 2],
        refs[count + 3],
    )
    out_ref[place[1]] = own_ref[...]
    for by, rows_ref in enumerate(rows_refs, 1):
        target = lax.rem(place[1] + (count + 1 - by), count + 1)

        def store(block, value, target=target):
            out_ref[target, block] = value

        expert_rows(place[0], rows_ref, weights_ref, store, act_ref, lambda block: None)


def own_expert(place, rows, residual, weights):
    count = rows.shape[0]
    vmem = pl.BlockSpec(memory_space=pltpu.VMEM)
    return pl.pallas_call(
        own_kernel,
        out_shape=(
            pltpu.VMEM((SETS, count, D // SETS), jnp.bfloat16),
            pltpu.VMEM(weights.shape, weights.dtype),
        ),
        in_specs=[
            pl.BlockSpec(memory_space=pltpu.SMEM),
            vmem,
            vmem,
            pl.BlockSpec(memory_space=pl.ANY),
        ],
        out_specs=(vmem, vmem),
        scratch_shapes=[
            pltpu.VMEM((count, FF), jnp.bfloat16),
            pltpu.SemaphoreType.DMA((SETS,)),
        ],
        compiler_params=pltpu.CompilerParams(vmem_limit_bytes=EXPERT_VMEM),
        name="own_expert",
    )(place, rows, residual, pltpu.with_memory_space_constraint(weights, pltpu.HBM))


def other_expert(place, own, weights, blocks):
    rows = blocks[0].shape[0]
    vmem = pl.BlockSpec(memory_space=pltpu.VMEM)
    held = [pltpu.with_memory_space_constraint(x, pltpu.VMEM) for x in (*blocks, own, weights)]
    return pl.pallas_call(
        functools.partial(other_kernel, len(blocks)),
        out_shape=jax.ShapeDtypeStruct((len(blocks) + 1, SETS, rows, D // SETS), jnp.bfloat16),
        in_specs=[pl.BlockSpec(memory_space=pltpu.SMEM)] + [vmem] * len(held),
        out_specs=vmem,
        scratch_shapes=[pltpu.VMEM((rows, FF), jnp.bfloat16)],
        compiler_params=pltpu.CompilerParams(vmem_limit_bytes=EXPERT_VMEM),
        name="other_expert",
    )(place, *held)


def fold_kernel(parts_ref, out_ref):
    seq_count = out_ref.shape[0]
    width = out_ref.shape[2]
    for source in range(SETS):
        total = parts_ref[source].astype(jnp.float32)
        for block in range(1, parts_ref.shape[0] // SETS):
            total = total + parts_ref[block * SETS + source].astype(jnp.float32)
        total = total.astype(jnp.bfloat16).reshape(seq_count, TOK, width)
        out_ref[:, source * TOK : (source + 1) * TOK, :] = total


def fold(parts, seq_count):
    vmem = pl.BlockSpec(memory_space=pltpu.VMEM)
    return pl.pallas_call(
        fold_kernel,
        out_shape=pltpu.VMEM((seq_count, DRAFT, parts.shape[2]), parts.dtype),
        in_specs=[vmem],
        out_specs=vmem,
        compiler_params=pltpu.CompilerParams(vmem_limit_bytes=VMEM_LIMIT),
        name="fold",
    )(pltpu.with_memory_space_constraint(parts, pltpu.VMEM))


def total_kernel(parts_ref, out_ref):
    total = parts_ref[0].astype(jnp.float32)
    for source in range(1, parts_ref.shape[0]):
        total = total + parts_ref[source].astype(jnp.float32)
    out_ref[0] = total.astype(jnp.bfloat16)


def total(parts):
    vmem = pl.BlockSpec(memory_space=pltpu.VMEM)
    return pl.pallas_call(
        total_kernel,
        out_shape=jax.ShapeDtypeStruct((1,) + parts.shape[1:], parts.dtype),
        in_specs=[vmem],
        out_specs=vmem,
        compiler_params=pltpu.CompilerParams(vmem_limit_bytes=VMEM_LIMIT),
        name="total",
    )(pltpu.with_memory_space_constraint(parts, pltpu.VMEM))


def shifted(value, axis, count, by):
    return lax.ppermute(value, axis, [(i, (i + by) % count) for i in range(count)])


def local(
    queries,
    draft_kv,
    kv_pool,
    page_table,
    cache_lens,
    parents,
    hidden,
    norm_gain,
    out_proj,
    router,
    routes,
    gate_w,
    up_w,
    down_w,
):
    my_set = lax.axis_index("exp").astype(jnp.int32)
    my_kv = lax.axis_index("kv").astype(jnp.int32)
    my_seq = lax.axis_index("seq").astype(jnp.int32)
    kv_count = lax.axis_size("kv")
    seq_count = lax.axis_size("seq")
    width = D // SETS
    weights = lax.all_gather(pack(gate_w, up_w, down_w), "exp")
    partials = attention(
        page_table.reshape(PPD), cache_lens, queries, parents, draft_kv, kv_pool
    )
    parts = lax.all_to_all(partials, "exp", 0, 0, tiled=True)
    projected = merge(parts, out_proj)
    shares = lax.all_to_all(projected.reshape(SETS, TOK, D), "exp", 0, 0, tiled=True)
    residual, row = norm(
        my_set.reshape(1), shares, hidden, norm_gain.reshape(1, D), router, routes
    )
    rows = lax.all_gather(row, "seq").reshape(seq_count * TOK, WIDE)
    place = jnp.stack([my_kv * seq_count + my_seq, my_kv, my_seq])
    arrived = [shifted(rows, "kv", kv_count, by) for by in range(1, kv_count)]
    own, kept = own_expert(place, rows, residual, weights)
    finished = other_expert(place, own, kept, arrived)
    back = finished.reshape(kv_count * SETS, seq_count * TOK, width)
    back = lax.all_to_all(back, ("kv", "exp"), 0, 0, tiled=True)
    back = lax.all_to_all(fold(back, seq_count), "seq", 0, 0, tiled=True)
    return total(back)


def solution(mesh):
    in_specs = (
        P(("kv", "seq"), None, None),
        P(None, ("kv", "seq"), "exp", None),
        P(None, ("kv", "seq", "exp"), None, None),
        P(("kv", "seq"), None, "exp"),
        P(("kv", "seq")),
        P(("kv", "seq"), None),
        P(("kv", "seq"), None, None),
        P(),
        P("exp", None),
        P(),
        P(("kv", "seq"), None, None),
        P(("kv", "seq"), None, "exp"),
        P(("kv", "seq"), None, "exp"),
        P(("kv", "seq"), "exp", None),
    )
    out_specs = P(("kv", "seq"), None, "exp")
    return jax.shard_map(local, mesh=mesh, in_specs=in_specs, out_specs=out_specs, check_vma=False)
```

```python
import functools

import jax
import jax.numpy as jnp
from jax import lax
from jax.experimental import pallas as pl
from jax.experimental.pallas import tpu as pltpu
from jax.sharding import PartitionSpec as P

D = 2048
H = 16
HD = 128
FF = 1024
EXPERTS = 64
TOPK = 8
DRAFT = 64
PAGE = 16
PPD = 12
SETS = 8
KEYS = PPD * PAGE
ROWS = KEYS + 16
TOK = DRAFT // SETS
WIDE = D + 2 * EXPERTS
STAT = DRAFT + 8
BLK = FF // SETS

NEG_FILL = -1e30
EPS_NORM = 1e-06
VMEM_LIMIT = 16 * 1024 * 1024
EXPERT_VMEM = 24 * 1024 * 1024


def nt(a, b):
    return lax.dot_general(a, b, (((1,), (1,)), ((), ())), preferred_element_type=jnp.float32)


def tn(a, b):
    return lax.dot_general(a, b, (((0,), (0,)), ((), ())), preferred_element_type=jnp.float32)


def nn(a, b):
    return lax.dot_general(a, b, (((1,), (0,)), ((), ())), preferred_element_type=jnp.float32)


def attention_kernel(
    table, lens, q_ref, parents_ref, draft_ref, pool_ref, out_ref, kbuf, vbuf, seen_ref, sems
):
    copies = []
    for page in range(PPD):
        slot = table[page]
        rows = pl.ds(page * PAGE, PAGE)
        copies.append(pltpu.make_async_copy(pool_ref.at[0, slot], kbuf.at[rows], sems.at[0, page]))
        copies.append(pltpu.make_async_copy(pool_ref.at[1, slot], vbuf.at[rows], sems.at[1, page]))
    for copy in copies:
        copy.start()
    length = lens[0]
    my_set = lax.axis_index("exp")
    pad = jnp.zeros((8, D), jnp.float32)
    kbuf[KEYS:ROWS, :] = jnp.concatenate([draft_ref[0, 0].astype(jnp.float32), pad], axis=0).astype(
        jnp.bfloat16
    )
    vbuf[KEYS:ROWS, :] = jnp.concatenate([draft_ref[1, 0].astype(jnp.float32), pad], axis=0).astype(
        jnp.bfloat16
    )
    ancestor = lax.broadcasted_iota(jnp.int32, (DRAFT, 2 * DRAFT), 0)
    token = lax.broadcasted_iota(jnp.int32, (DRAFT, 2 * DRAFT), 1) % DRAFT
    parents = jnp.concatenate([parents_ref[...], parents_ref[...]], axis=1)
    linked = jnp.where((parents == ancestor) | (ancestor == token), 1.0, 0.0)
    for doubling in range((DRAFT - 1).bit_length()):
        narrow = linked.astype(jnp.bfloat16)
        linked = jnp.minimum(nn(narrow[:, :DRAFT], narrow), 1.0)
    seen_ref[...] = linked
    draft_seen = seen_ref[pl.ds(pl.multiple_of(my_set * TOK, TOK), TOK), :]
    key_row = lax.broadcasted_iota(jnp.int32, (KEYS, 2 * DRAFT), 0)
    position = ((key_row // PAGE) * SETS + my_set) * PAGE + key_row % PAGE
    cache_seen = jnp.where(position < length, 1.0, 0.0)
    seen = (
        jnp.concatenate(
            [cache_seen, draft_seen, jnp.zeros((8, 2 * DRAFT), jnp.float32)], axis=0
        )
        > 0.5
    )
    own = (lax.broadcasted_iota(jnp.int32, (2 * DRAFT, 2 * HD), 0) < DRAFT) == (
        lax.broadcasted_iota(jnp.int32, (2 * DRAFT, 2 * HD), 1) < HD
    )
    stat_row = lax.broadcasted_iota(jnp.int32, (8, 2 * DRAFT), 0)
    for copy in copies:
        copy.wait()
    for pair in range(H // 2):
        cols = slice(pair * 2 * HD, (pair + 1) * 2 * HD)
        query = q_ref[0, :, cols]
        query = jnp.where(own, jnp.concatenate([query, query], axis=0), jnp.zeros((), jnp.bfloat16))
        scores = nt(kbuf[:, cols], query) * (HD**-0.5)
        scores = jnp.where(seen, scores, NEG_FILL)
        top = jnp.max(scores, axis=0, keepdims=True).astype(jnp.bfloat16).astype(jnp.float32)
        weights = jnp.where(seen, jnp.exp(scores - top), 0.0)
        total = jnp.sum(weights, axis=0, keepdims=True)
        acc = tn(weights.astype(jnp.bfloat16), vbuf[:, cols])
        total_high = total.astype(jnp.bfloat16).astype(jnp.float32)
        stats = jnp.where(
            stat_row == 0,
            top,
            jnp.where(stat_row == 1, total_high, jnp.where(stat_row == 2, total - total_high, 0.0)),
        )
        out_ref[pair, 0:DRAFT, 0:HD] = acc[:DRAFT, :HD].astype(jnp.bfloat16)
        out_ref[pair, 0:DRAFT, HD : 2 * HD] = acc[DRAFT:, HD:].astype(jnp.bfloat16)
        out_ref[pair, DRAFT:STAT, 0:HD] = stats.astype(jnp.bfloat16)
        out_ref[pair, DRAFT:STAT, HD : 2 * HD] = jnp.zeros((8, HD), jnp.bfloat16)


def attention(table, lens, queries, parents, draft_kv, kv_pool):
    vmem = pl.BlockSpec(memory_space=pltpu.VMEM)
    return pl.pallas_call(
        attention_kernel,
        out_shape=jax.ShapeDtypeStruct((SETS, STAT, 2 * HD), jnp.bfloat16),
        in_specs=[
            pl.BlockSpec(memory_space=pltpu.SMEM),
            pl.BlockSpec(memory_space=pltpu.SMEM),
            vmem,
            vmem,
            vmem,
            pl.BlockSpec(memory_space=pl.ANY),
        ],
        out_specs=vmem,
        scratch_shapes=[
            pltpu.VMEM((ROWS, D), jnp.bfloat16),
            pltpu.VMEM((ROWS, D), jnp.bfloat16),
            pltpu.VMEM((DRAFT, 2 * DRAFT), jnp.float32),
            pltpu.SemaphoreType.DMA((2, PPD)),
        ],
        compiler_params=pltpu.CompilerParams(vmem_limit_bytes=VMEM_LIMIT),
        name="attention",
    )(table, lens, queries, parents, draft_kv, kv_pool)


def merge_kernel(parts_ref, proj_ref, out_ref):
    stats = parts_ref[:, DRAFT:STAT, 0:HD].astype(jnp.float32)
    tops = stats[:, 0, :]
    totals = stats[:, 1, :] + stats[:, 2, :]
    scale = jnp.exp(tops - jnp.max(tops, axis=0, keepdims=True))
    scale = scale / jnp.sum(scale * totals, axis=0, keepdims=True)
    scale = jnp.transpose(scale)
    heads = []
    for head in range(2):
        joined = jnp.zeros((DRAFT, HD), jnp.float32)
        for source in range(SETS):
            part = parts_ref[source, 0:DRAFT, head * HD : (head + 1) * HD].astype(jnp.float32)
            joined = joined + part * scale[head * DRAFT : (head + 1) * DRAFT, source : source + 1]
        heads.append(joined.astype(jnp.bfloat16))
    out_ref[...] = nn(jnp.concatenate(heads, axis=1), proj_ref[...]).astype(jnp.bfloat16)


def merge(parts, out_proj):
    return pl.pallas_call(
        merge_kernel,
        out_shape=jax.ShapeDtypeStruct((DRAFT, D), jnp.bfloat16),
        compiler_params=pltpu.CompilerParams(vmem_limit_bytes=VMEM_LIMIT),
        name="merge",
    )(parts, out_proj)


def norm_kernel(my_set, parts_ref, hidden_ref, gain_ref, router_ref, routes_ref, residual_ref, row_ref):
    residual = hidden_ref[0].astype(jnp.float32)
    for source in range(SETS):
        residual = residual + parts_ref[source].astype(jnp.float32)
    residual_ref[...] = residual
    mean_sq = jnp.mean(residual * residual, axis=1, keepdims=True)
    normed = (residual * lax.rsqrt(mean_sq + EPS_NORM) * gain_ref[...].astype(jnp.float32)).astype(
        jnp.bfloat16
    )
    logits = nn(normed, router_ref[...])
    gates = 1.0 / (1.0 + jnp.exp(-logits))
    expert = lax.broadcasted_iota(jnp.int32, (TOK, EXPERTS), 1)
    routes = routes_ref[0]
    chosen = routes[:, 0:1] == expert
    for pick in range(1, TOPK):
        chosen = chosen | (routes[:, pick : pick + 1] == expert)
    gates = jnp.where(chosen, gates, 0.0)
    high = gates.astype(jnp.bfloat16).astype(jnp.float32)
    row_ref[:, 0:D] = normed
    row_ref[:, D:WIDE] = jnp.concatenate([high, gates - high], axis=1).astype(jnp.bfloat16)


def norm(my_set, parts, hidden, norm_gain, router, routes):
    whole = lambda *shape: pl.BlockSpec(shape, lambda i, s: (0,) * len(shape))
    return pl.pallas_call(
        norm_kernel,
        out_shape=(
            jax.ShapeDtypeStruct((TOK, D), jnp.float32),
            jax.ShapeDtypeStruct((TOK, WIDE), jnp.bfloat16),
        ),
        grid_spec=pltpu.PrefetchScalarGridSpec(
            num_scalar_prefetch=1,
            grid=(1,),
            in_specs=[
                whole(SETS, TOK, D),
                pl.BlockSpec((1, TOK, D), lambda i, s: (0, s[0], 0)),
                whole(1, D),
                whole(D, EXPERTS),
                pl.BlockSpec((1, TOK, TOPK), lambda i, s: (0, s[0], 0)),
            ],
            out_specs=(whole(TOK, D), whole(TOK, WIDE)),
        ),
        compiler_params=pltpu.CompilerParams(vmem_limit_bytes=VMEM_LIMIT),
        name="norm",
    )(my_set, parts, hidden, norm_gain, router, routes)


def pack_kernel(gate_ref, up_ref, down_ref, out_ref, buf, in_sems, out_sems):
    width = D // SETS
    pieces = []
    part = D // 4
    for piece in range(4):
        rows = pl.ds(piece * part, part)
        pieces.append(
            (
                [
                    (gate_ref.at[0, rows], buf.at[rows, pl.ds(0, BLK)]),
                    (up_ref.at[0, rows], buf.at[rows, pl.ds(BLK, BLK)]),
                ],
                rows,
            )
        )
    for half in range(2):
        blocks = range(half * SETS // 2, (half + 1) * SETS // 2)
        pieces.append(
            (
                [
                    (
                        down_ref.at[0, :, pl.ds(block * width, width)],
                        buf.at[pl.ds(D + block * BLK, BLK)],
                    )
                    for block in blocks
                ],
                pl.ds(D + half * FF // 2, FF // 2),
            )
        )
    loads = []
    count = 0
    for moves, rows in pieces:
        group = []
        for source, target in moves:
            group.append(pltpu.make_async_copy(source, target, in_sems.at[count]))
            count += 1
        loads.append((group, rows))
    for group, rows in loads:
        for copy in group:
            copy.start()
    stores = []
    for index, (group, rows) in enumerate(loads):
        for copy in group:
            copy.wait()
        store = pltpu.make_async_copy(buf.at[rows], out_ref.at[rows], out_sems.at[index])
        store.start()
        stores.append(store)
    for store in stores:
        store.wait()


def pack(gate_w, up_w, down_w):
    hbm = pl.BlockSpec(memory_space=pltpu.HBM)
    width = D // SETS
    return pl.pallas_call(
        pack_kernel,
        out_shape=jax.ShapeDtypeStruct((D + FF, width), gate_w.dtype),
        in_specs=[hbm] * 3,
        out_specs=hbm,
        scratch_shapes=[
            pltpu.VMEM((D + FF, width), jnp.bfloat16),
            pltpu.SemaphoreType.DMA((16,)),
            pltpu.SemaphoreType.DMA((6,)),
        ],
        compiler_params=pltpu.CompilerParams(vmem_limit_bytes=VMEM_LIMIT),
        name="pack",
    )(*(pltpu.with_memory_space_constraint(x, pltpu.HBM) for x in (gate_w, up_w, down_w)))


def expert_rows(my_expert, rows_ref, weights_ref, store, act_ref, before_block):
    gates = rows_ref[:, D:WIDE].astype(jnp.float32)
    lane = lax.broadcasted_iota(jnp.int32, gates.shape, 1) % EXPERTS
    scale = jnp.sum(jnp.where(lane == my_expert, gates, 0.0), axis=1, keepdims=True)
    for block in range(SETS):
        before_block(block)
        both = nn(rows_ref[:, 0:D], weights_ref[block, 0:D, :])
        gate, up = both[:, :BLK], both[:, BLK:]
        act = gate / (1.0 + jnp.exp(-gate)) * up
        act_ref[:, block * BLK : (block + 1) * BLK] = act.astype(jnp.bfloat16)
    width = D // SETS
    for block in range(SETS):
        down = weights_ref[:, D + block * BLK : D + (block + 1) * BLK, :].reshape(FF, width)
        store(block, (nn(act_ref[...], down) * scale).astype(jnp.bfloat16))


def columns_of(out_ref):
    width = D // SETS

    def store(block, value):
        out_ref[:, block * width : (block + 1) * width] = value

    return store


def own_kernel(place, rows_ref, weights_ref, out_ref, kept_ref, act_ref, sems):
    copies = [
        pltpu.make_async_copy(weights_ref.at[block], kept_ref.at[block], sems.at[block])
        for block in range(SETS)
    ]
    for copy in copies:
        copy.start()
    expert_rows(
        place[0],
        rows_ref,
        kept_ref,
        columns_of(out_ref),
        act_ref,
        lambda block: copies[block].wait(),
    )


def other_kernel(count, place, *refs):
    rows_refs, weights_ref, out_refs, act_ref = (
        refs[:count],
        refs[count],
        refs[count + 1 : 2 * count + 1],
        refs[2 * count + 1],
    )
    for rows_ref, out_ref in zip(rows_refs, out_refs):
        expert_rows(
            place[0], rows_ref, weights_ref, columns_of(out_ref), act_ref, lambda block: None
        )


def own_expert(place, rows, weights):
    count = rows.shape[0]
    vmem = pl.BlockSpec(memory_space=pltpu.VMEM)
    return pl.pallas_call(
        own_kernel,
        out_shape=(
            pltpu.VMEM((count, D), jnp.bfloat16),
            pltpu.VMEM(weights.shape, weights.dtype),
        ),
        in_specs=[
            pl.BlockSpec(memory_space=pltpu.SMEM),
            vmem,
            pl.BlockSpec(memory_space=pl.ANY),
        ],
        out_specs=(vmem, vmem),
        scratch_shapes=[
            pltpu.VMEM((count, FF), jnp.bfloat16),
            pltpu.SemaphoreType.DMA((SETS,)),
        ],
        compiler_params=pltpu.CompilerParams(vmem_limit_bytes=EXPERT_VMEM),
        name="own_expert",
    )(place, rows, pltpu.with_memory_space_constraint(weights, pltpu.HBM))


def in_vmem(*arrays):
    return [pltpu.with_memory_space_constraint(x, pltpu.VMEM) for x in arrays]


def other_expert(place, weights, *blocks):
    rows = blocks[0].shape[0]
    vmem = pl.BlockSpec(memory_space=pltpu.VMEM)
    return pl.pallas_call(
        functools.partial(other_kernel, len(blocks)),
        out_shape=tuple(jax.ShapeDtypeStruct((rows, D), jnp.bfloat16) for block in blocks),
        in_specs=[pl.BlockSpec(memory_space=pltpu.SMEM)] + [vmem] * (len(blocks) + 1),
        out_specs=(vmem,) * len(blocks),
        scratch_shapes=[pltpu.VMEM((rows, FF), jnp.bfloat16)],
        compiler_params=pltpu.CompilerParams(vmem_limit_bytes=EXPERT_VMEM),
        name="other_expert",
    )(place, *in_vmem(*blocks, weights))


def summed(refs, rows):
    total = refs[0][rows].astype(jnp.float32)
    for ref in refs[1:]:
        total = total + ref[rows].astype(jnp.float32)
    return total


def join_kernel(place, residual_ref, *refs):
    parts_refs, out_ref, work_ref = refs[:-2], refs[-2], refs[-1]
    near = out_ref.shape[0]
    rows = work_ref.shape[0]
    step = 2 * TOK
    for start in range(0, rows, step):
        work_ref[start : start + step, :] = summed(parts_refs, slice(start, start + step))
    mine = pl.ds(pl.multiple_of(place[2] * TOK, TOK), TOK)
    work_ref[mine, :] = work_ref[mine, :] + residual_ref[...]
    for seq in range(rows // TOK):
        far = seq // near
        out_ref[seq % near, far * TOK : (far + 1) * TOK, :] = work_ref[
            seq * TOK : (seq + 1) * TOK, :
        ].astype(jnp.bfloat16)


def join(place, residual, parts, near):
    rows = parts[0].shape[0]
    vmem = pl.BlockSpec(memory_space=pltpu.VMEM)
    return pl.pallas_call(
        join_kernel,
        out_shape=pltpu.VMEM((near, rows // near, D), jnp.bfloat16),
        in_specs=[pl.BlockSpec(memory_space=pltpu.SMEM)] + [vmem] * (len(parts) + 1),
        out_specs=vmem,
        scratch_shapes=[pltpu.VMEM((rows, D), jnp.float32)],
        compiler_params=pltpu.CompilerParams(vmem_limit_bytes=VMEM_LIMIT),
        name="join",
    )(place, *in_vmem(residual, *parts))


def fold_kernel(parts_ref, out_ref):
    width = D // SETS
    for far in range(parts_ref.shape[1] // TOK):
        for block in range(SETS):
            cols = slice(block * width, (block + 1) * width)
            total = parts_ref[0, far * TOK : (far + 1) * TOK, cols].astype(jnp.float32)
            for source in range(1, parts_ref.shape[0]):
                total = total + parts_ref[
                    source, far * TOK : (far + 1) * TOK, cols
                ].astype(jnp.float32)
            out_ref[far * SETS + block] = total.astype(jnp.bfloat16)


def fold(parts):
    far = parts.shape[1] // TOK
    vmem = pl.BlockSpec(memory_space=pltpu.VMEM)
    return pl.pallas_call(
        fold_kernel,
        out_shape=pltpu.VMEM((far * SETS, TOK, D // SETS), parts.dtype),
        in_specs=[vmem],
        out_specs=vmem,
        compiler_params=pltpu.CompilerParams(vmem_limit_bytes=VMEM_LIMIT),
        name="fold",
    )(*in_vmem(parts))


def total_kernel(parts_ref, out_ref):
    for source in range(SETS):
        total = parts_ref[source].astype(jnp.float32)
        for far in range(1, parts_ref.shape[0] // SETS):
            total = total + parts_ref[far * SETS + source].astype(jnp.float32)
        out_ref[0, source * TOK : (source + 1) * TOK, :] = total.astype(jnp.bfloat16)


def total(parts):
    vmem = pl.BlockSpec(memory_space=pltpu.VMEM)
    return pl.pallas_call(
        total_kernel,
        out_shape=jax.ShapeDtypeStruct((1, DRAFT, parts.shape[2]), parts.dtype),
        in_specs=[vmem],
        out_specs=vmem,
        compiler_params=pltpu.CompilerParams(vmem_limit_bytes=VMEM_LIMIT),
        name="total",
    )(*in_vmem(parts))


def shifted(value, axis, count, by):
    return lax.ppermute(value, axis, [(i, (i + by) % count) for i in range(count)])


def local(
    queries,
    draft_kv,
    kv_pool,
    page_table,
    cache_lens,
    parents,
    hidden,
    norm_gain,
    out_proj,
    router,
    routes,
    gate_w,
    up_w,
    down_w,
):
    my_set = lax.axis_index("exp").astype(jnp.int32)
    my_kv = lax.axis_index("kv").astype(jnp.int32)
    my_seq = lax.axis_index("seq").astype(jnp.int32)
    kv_count = lax.axis_size("kv")
    seq_count = lax.axis_size("seq")
    width = D // SETS
    weights = lax.all_gather(pack(gate_w, up_w, down_w), "exp")
    partials = attention(
        page_table.reshape(PPD), cache_lens, queries, parents, draft_kv, kv_pool
    )
    parts = lax.all_to_all(partials, "exp", 0, 0, tiled=True)
    projected = merge(parts, out_proj)
    shares = lax.all_to_all(projected.reshape(SETS, TOK, D), "exp", 0, 0, tiled=True)
    residual, row = norm(
        my_set.reshape(1), shares, hidden, norm_gain.reshape(1, D), router, routes
    )
    rows = lax.all_gather(row, "seq").reshape(seq_count * TOK, WIDE)
    place = jnp.stack([my_kv * seq_count + my_seq, my_kv, my_seq])
    arrived = {by: shifted(rows, "kv", kv_count, by) for by in range(1, kv_count)}
    own, kept = own_expert(place, rows, weights)
    near = other_expert(place, kept, arrived[1], arrived[kv_count - 1])
    parts = [
        own,
        shifted(near[0], "kv", kv_count, -1),
        shifted(near[1], "kv", kv_count, 1),
    ]
    for by in range(2, kv_count - 1):
        (far,) = other_expert(place, kept, arrived[by])
        parts.append(shifted(far, "kv", kv_count, -by))
    run = 4
    far_count = seq_count // run
    runs = [[far * run + near for near in range(run)] for far in range(far_count)]
    strides = [
        [
            (far * run + near) * SETS + block
            for far in range(far_count)
            for block in range(SETS)
        ]
        for near in range(run)
    ]
    back = join(place, residual, parts, run)
    back = lax.all_to_all(back, "seq", 0, 0, tiled=True, axis_index_groups=runs)
    back = lax.all_to_all(
        fold(back), ("seq", "exp"), 0, 0, tiled=True, axis_index_groups=strides
    )
    return total(back)


def solution(mesh):
    in_specs = (
        P(("kv", "seq"), None, None),
        P(None, ("kv", "seq"), "exp", None),
        P(None, ("kv", "seq", "exp"), None, None),
        P(("kv", "seq"), None, "exp"),
        P(("kv", "seq")),
        P(("kv", "seq"), None),
        P(("kv", "seq"), None, None),
        P(),
        P("exp", None),
        P(),
        P(("kv", "seq"), None, None),
        P(("kv", "seq"), None, "exp"),
        P(("kv", "seq"), None, "exp"),
        P(("kv", "seq"), "exp", None),
    )
    out_specs = P(("kv", "seq"), None, "exp")
    return jax.shard_map(local, mesh=mesh, in_specs=in_specs, out_specs=out_specs, check_vma=False)
```

```python
import functools

import jax
import jax.numpy as jnp
from jax import lax
from jax.experimental import pallas as pl
from jax.experimental.pallas import tpu as pltpu
from jax.sharding import PartitionSpec as P

D = 2048
H = 16
HD = 128
FF = 1024
EXPERTS = 64
TOPK = 8
DRAFT = 64
PAGE = 16
PPD = 12
SETS = 8
KEYS = PPD * PAGE
ROWS = KEYS + 16
TOK = DRAFT // SETS
WIDE = D + 2 * EXPERTS
STAT = DRAFT + 8
BLK = FF // SETS

NEG_FILL = -1e30
EPS_NORM = 1e-06
VMEM_LIMIT = 16 * 1024 * 1024
EXPERT_VMEM = 24 * 1024 * 1024


def nt(a, b):
    return lax.dot_general(a, b, (((1,), (1,)), ((), ())), preferred_element_type=jnp.float32)


def tn(a, b):
    return lax.dot_general(a, b, (((0,), (0,)), ((), ())), preferred_element_type=jnp.float32)


def nn(a, b):
    return lax.dot_general(a, b, (((1,), (0,)), ((), ())), preferred_element_type=jnp.float32)


def in_vmem(*arrays):
    return [pltpu.with_memory_space_constraint(x, pltpu.VMEM) for x in arrays]


def expert_index():
    return lax.axis_index("kv") * lax.axis_size("seq") + lax.axis_index("seq")


def attention_kernel(
    table,
    lens,
    q_hbm,
    parents_hbm,
    draft_hbm,
    pool_ref,
    proj_ref,
    out_ref,
    kept_ref,
    kbuf,
    vbuf,
    q_ref,
    draft_ref,
    parents_ref,
    seen_ref,
    score_ref,
    weight_ref,
    sems,
    more_sems,
):
    keys, values = [], []
    for page in range(PPD):
        slot = table[page]
        rows = pl.ds(page * PAGE, PAGE)
        keys.append(pltpu.make_async_copy(pool_ref.at[0, slot], kbuf.at[rows], sems.at[0, page]))
        values.append(pltpu.make_async_copy(pool_ref.at[1, slot], vbuf.at[rows], sems.at[1, page]))
    query_copy = pltpu.make_async_copy(q_hbm.at[0], q_ref, more_sems.at[0])
    draft_copy = pltpu.make_async_copy(draft_hbm.at[:, 0], draft_ref, more_sems.at[1])
    proj_copy = pltpu.make_async_copy(proj_ref, kept_ref, more_sems.at[2])
    parents_copy = pltpu.make_async_copy(parents_hbm, parents_ref, more_sems.at[3])
    for copy in [parents_copy, draft_copy, query_copy] + keys + values + [proj_copy]:
        copy.start()
    length = lens[0]
    my_set = lax.axis_index("exp")
    ancestor = lax.broadcasted_iota(jnp.int32, (DRAFT, 2 * DRAFT), 0)
    token = lax.broadcasted_iota(jnp.int32, (DRAFT, 2 * DRAFT), 1) % DRAFT
    parents_copy.wait()
    parents = jnp.concatenate([parents_ref[...], parents_ref[...]], axis=1)
    linked = jnp.where((parents == ancestor) | (ancestor == token), 1.0, 0.0)
    for doubling in range((DRAFT - 1).bit_length()):
        narrow = linked.astype(jnp.bfloat16)
        linked = jnp.minimum(nn(narrow[:, :DRAFT], narrow), 1.0)
    seen_ref[0:DRAFT, :] = linked
    draft_seen = seen_ref[pl.ds(pl.multiple_of(my_set * TOK, TOK), TOK), :]
    key_row = lax.broadcasted_iota(jnp.int32, (KEYS, 2 * DRAFT), 0)
    position = ((key_row // PAGE) * SETS + my_set) * PAGE + key_row % PAGE
    cache_seen = jnp.where(position < length, 1.0, 0.0)
    seen_ref[0:ROWS, :] = jnp.concatenate(
        [cache_seen, draft_seen, jnp.zeros((8, 2 * DRAFT), jnp.float32)], axis=0
    )
    own = (lax.broadcasted_iota(jnp.int32, (2 * DRAFT, 2 * HD), 0) < DRAFT) == (
        lax.broadcasted_iota(jnp.int32, (2 * DRAFT, 2 * HD), 1) < HD
    )
    stat_row = lax.broadcasted_iota(jnp.int32, (8, 2 * DRAFT), 0)
    pad = jnp.zeros((8, D), jnp.float32)
    draft_copy.wait()
    for place, buf in ((0, kbuf), (1, vbuf)):
        rows = jnp.concatenate([draft_ref[place].astype(jnp.float32), pad], axis=0)
        buf[KEYS:ROWS, :] = rows.astype(jnp.bfloat16)
    query_copy.wait()
    for copy in keys:
        copy.wait()
    for pair in range(H // 2):
        cols = slice(pair * 2 * HD, (pair + 1) * 2 * HD)
        query = q_ref[:, cols]
        query = jnp.where(own, jnp.concatenate([query, query], axis=0), jnp.zeros((), jnp.bfloat16))
        score_ref[pair] = nt(kbuf[:, cols], query) * (HD**-0.5)
    for pair in range(H // 2):
        seen = seen_ref[0:ROWS, :] > 0.5
        scores = jnp.where(seen, score_ref[pair], NEG_FILL)
        top = jnp.max(scores, axis=0, keepdims=True).astype(jnp.bfloat16).astype(jnp.float32)
        weights = jnp.where(seen, jnp.exp(scores - top), 0.0)
        total = jnp.sum(weights, axis=0, keepdims=True)
        weight_ref[pair] = weights.astype(jnp.bfloat16)
        total_high = total.astype(jnp.bfloat16).astype(jnp.float32)
        stats = jnp.where(
            stat_row == 0,
            top,
            jnp.where(stat_row == 1, total_high, jnp.where(stat_row == 2, total - total_high, 0.0)),
        )
        out_ref[pair, DRAFT:STAT, 0:HD] = stats.astype(jnp.bfloat16)
        out_ref[pair, DRAFT:STAT, HD : 2 * HD] = jnp.zeros((8, HD), jnp.bfloat16)
    for copy in values:
        copy.wait()
    for pair in range(H // 2):
        cols = slice(pair * 2 * HD, (pair + 1) * 2 * HD)
        acc = tn(weight_ref[pair], vbuf[:, cols])
        out_ref[pair, 0:DRAFT, 0:HD] = acc[:DRAFT, :HD].astype(jnp.bfloat16)
        out_ref[pair, 0:DRAFT, HD : 2 * HD] = acc[DRAFT:, HD:].astype(jnp.bfloat16)
    proj_copy.wait()


def attention(table, lens, queries, parents, draft_kv, kv_pool, out_proj):
    smem = pl.BlockSpec(memory_space=pltpu.SMEM)
    vmem = pl.BlockSpec(memory_space=pltpu.VMEM)
    hbm = pl.BlockSpec(memory_space=pltpu.HBM)
    queries, parents, draft_kv, kv_pool, out_proj = (
        pltpu.with_memory_space_constraint(x, pltpu.HBM)
        for x in (queries, parents, draft_kv, kv_pool, out_proj)
    )
    return pl.pallas_call(
        attention_kernel,
        out_shape=(
            jax.ShapeDtypeStruct((SETS, STAT, 2 * HD), jnp.bfloat16),
            pltpu.VMEM(out_proj.shape, out_proj.dtype),
        ),
        in_specs=[smem, smem, hbm, hbm, hbm, hbm, hbm],
        out_specs=(vmem, vmem),
        scratch_shapes=[
            pltpu.VMEM((ROWS, D), jnp.bfloat16),
            pltpu.VMEM((ROWS, D), jnp.bfloat16),
            pltpu.VMEM((DRAFT, D), jnp.bfloat16),
            pltpu.VMEM((2, TOK, D), jnp.bfloat16),
            pltpu.VMEM((1, DRAFT), jnp.int32),
            pltpu.VMEM((ROWS, 2 * DRAFT), jnp.float32),
            pltpu.VMEM((H // 2, ROWS, 2 * DRAFT), jnp.float32),
            pltpu.VMEM((H // 2, ROWS, 2 * DRAFT), jnp.bfloat16),
            pltpu.SemaphoreType.DMA((2, PPD)),
            pltpu.SemaphoreType.DMA((4,)),
        ],
        compiler_params=pltpu.CompilerParams(vmem_limit_bytes=VMEM_LIMIT),
        name="attention",
    )(table, lens, queries, parents, draft_kv, kv_pool, out_proj)


def merge_kernel(parts_ref, proj_ref, out_ref):
    stats = parts_ref[:, DRAFT:STAT, 0:HD].astype(jnp.float32)
    tops = stats[:, 0, :]
    totals = stats[:, 1, :] + stats[:, 2, :]
    scale = jnp.exp(tops - jnp.max(tops, axis=0, keepdims=True))
    scale = scale / jnp.sum(scale * totals, axis=0, keepdims=True)
    scale = jnp.transpose(scale)
    heads = []
    for head in range(2):
        joined = jnp.zeros((DRAFT, HD), jnp.float32)
        for source in range(SETS):
            part = parts_ref[source, 0:DRAFT, head * HD : (head + 1) * HD].astype(jnp.float32)
            joined = joined + part * scale[head * DRAFT : (head + 1) * DRAFT, source : source + 1]
        heads.append(joined.astype(jnp.bfloat16))
    out_ref[...] = nn(jnp.concatenate(heads, axis=1), proj_ref[...]).astype(jnp.bfloat16)


def merge(parts, out_proj):
    return pl.pallas_call(
        merge_kernel,
        out_shape=jax.ShapeDtypeStruct((DRAFT, D), jnp.bfloat16),
        compiler_params=pltpu.CompilerParams(vmem_limit_bytes=VMEM_LIMIT),
        name="merge",
    )(parts, *in_vmem(out_proj))


def norm_kernel(
    parts_ref, hidden_ref, gain_ref, router_ref, routes_ref, residual_ref, row_ref, own_ref, sem
):
    mine = pl.ds(pl.multiple_of(lax.axis_index("exp") * TOK, TOK), TOK)
    copy = pltpu.make_async_copy(hidden_ref.at[0, mine], own_ref, sem)
    copy.start()
    residual = parts_ref[0].astype(jnp.float32)
    for source in range(1, SETS):
        residual = residual + parts_ref[source].astype(jnp.float32)
    expert = lax.broadcasted_iota(jnp.int32, (TOK, EXPERTS), 1)
    routes = routes_ref[0, mine, :]
    chosen = routes[:, 0:1] == expert
    for pick in range(1, TOPK):
        chosen = chosen | (routes[:, pick : pick + 1] == expert)
    copy.wait()
    residual = own_ref[...].astype(jnp.float32) + residual
    residual_ref[...] = residual
    mean_sq = jnp.mean(residual * residual, axis=1, keepdims=True)
    normed = (residual * lax.rsqrt(mean_sq + EPS_NORM) * gain_ref[...].astype(jnp.float32)).astype(
        jnp.bfloat16
    )
    logits = nn(normed, router_ref[...])
    gates = jnp.where(chosen, 1.0 / (1.0 + jnp.exp(-logits)), 0.0)
    high = gates.astype(jnp.bfloat16).astype(jnp.float32)
    row_ref[:, 0:D] = normed
    row_ref[:, D:WIDE] = jnp.concatenate([high, gates - high], axis=1).astype(jnp.bfloat16)


def norm(parts, hidden, norm_gain, router, routes):
    vmem = pl.BlockSpec(memory_space=pltpu.VMEM)
    return pl.pallas_call(
        norm_kernel,
        out_shape=(
            pltpu.VMEM((TOK, D), jnp.float32),
            jax.ShapeDtypeStruct((TOK, WIDE), jnp.bfloat16),
        ),
        in_specs=[vmem, pl.BlockSpec(memory_space=pltpu.HBM), vmem, vmem, vmem],
        out_specs=(vmem, vmem),
        scratch_shapes=[pltpu.VMEM((TOK, D), jnp.bfloat16), pltpu.SemaphoreType.DMA],
        compiler_params=pltpu.CompilerParams(vmem_limit_bytes=VMEM_LIMIT),
        name="norm",
    )(
        *in_vmem(parts),
        pltpu.with_memory_space_constraint(hidden, pltpu.HBM),
        *in_vmem(norm_gain, router, routes),
    )


def pack_kernel(gate_ref, up_ref, down_ref, out_ref, buf, in_sems, out_sems):
    width = D // SETS
    pieces = []
    part = D // 4
    for piece in range(4):
        rows = pl.ds(piece * part, part)
        pieces.append(
            (
                [
                    (gate_ref.at[0, rows], buf.at[rows, pl.ds(0, BLK)]),
                    (up_ref.at[0, rows], buf.at[rows, pl.ds(BLK, BLK)]),
                ],
                rows,
            )
        )
    for half in range(2):
        blocks = range(half * SETS // 2, (half + 1) * SETS // 2)
        pieces.append(
            (
                [
                    (
                        down_ref.at[0, :, pl.ds(block * width, width)],
                        buf.at[pl.ds(D + block * BLK, BLK)],
                    )
                    for block in blocks
                ],
                pl.ds(D + half * FF // 2, FF // 2),
            )
        )
    loads = []
    count = 0
    for moves, rows in pieces:
        group = []
        for source, target in moves:
            group.append(pltpu.make_async_copy(source, target, in_sems.at[count]))
            count += 1
        loads.append((group, rows))
    for group, rows in loads:
        for copy in group:
            copy.start()
    stores = []
    for index, (group, rows) in enumerate(loads):
        for copy in group:
            copy.wait()
        store = pltpu.make_async_copy(buf.at[rows], out_ref.at[rows], out_sems.at[index])
        store.start()
        stores.append(store)
    for store in stores:
        store.wait()


def pack(gate_w, up_w, down_w):
    hbm = pl.BlockSpec(memory_space=pltpu.HBM)
    width = D // SETS
    return pl.pallas_call(
        pack_kernel,
        out_shape=jax.ShapeDtypeStruct((D + FF, width), gate_w.dtype),
        in_specs=[hbm] * 3,
        out_specs=hbm,
        scratch_shapes=[
            pltpu.VMEM((D + FF, width), jnp.bfloat16),
            pltpu.SemaphoreType.DMA((16,)),
            pltpu.SemaphoreType.DMA((6,)),
        ],
        compiler_params=pltpu.CompilerParams(vmem_limit_bytes=VMEM_LIMIT),
        name="pack",
    )(*(pltpu.with_memory_space_constraint(x, pltpu.HBM) for x in (gate_w, up_w, down_w)))


def expert_rows(my_expert, rows_ref, weights_ref, store, act_ref, before_block):
    gates = rows_ref[:, D:WIDE].astype(jnp.float32)
    lane = lax.broadcasted_iota(jnp.int32, gates.shape, 1) % EXPERTS
    scale = jnp.sum(jnp.where(lane == my_expert, gates, 0.0), axis=1, keepdims=True)
    for block in range(SETS):
        before_block(block)
        both = nn(rows_ref[:, 0:D], weights_ref[block, 0:D, :])
        gate, up = both[:, :BLK], both[:, BLK:]
        act = gate / (1.0 + jnp.exp(-gate)) * up
        act_ref[:, block * BLK : (block + 1) * BLK] = act.astype(jnp.bfloat16)
    width = D // SETS
    for block in range(SETS):
        down = weights_ref[:, D + block * BLK : D + (block + 1) * BLK, :].reshape(FF, width)
        store(block, (nn(act_ref[...], down) * scale).astype(jnp.bfloat16))


def columns_of(out_ref):
    width = D // SETS

    def store(block, value):
        out_ref[:, block * width : (block + 1) * width] = value

    return store


def own_kernel(rows_ref, weights_ref, out_ref, kept_ref, act_ref, sems):
    copies = [
        pltpu.make_async_copy(weights_ref.at[block], kept_ref.at[block], sems.at[block])
        for block in range(SETS)
    ]
    for copy in copies:
        copy.start()
    expert_rows(
        expert_index(),
        rows_ref,
        kept_ref,
        columns_of(out_ref),
        act_ref,
        lambda block: copies[block].wait(),
    )


def other_kernel(count, *refs):
    rows_refs, weights_ref, out_refs, act_ref = (
        refs[:count],
        refs[count],
        refs[count + 1 : 2 * count + 1],
        refs[2 * count + 1],
    )
    for rows_ref, out_ref in zip(rows_refs, out_refs):
        expert_rows(
            expert_index(), rows_ref, weights_ref, columns_of(out_ref), act_ref, lambda block: None
        )


def own_expert(rows, weights):
    count = rows.shape[0]
    vmem = pl.BlockSpec(memory_space=pltpu.VMEM)
    return pl.pallas_call(
        own_kernel,
        out_shape=(
            pltpu.VMEM((count, D), jnp.bfloat16),
            pltpu.VMEM(weights.shape, weights.dtype),
        ),
        in_specs=[vmem, pl.BlockSpec(memory_space=pltpu.HBM)],
        out_specs=(vmem, vmem),
        scratch_shapes=[
            pltpu.VMEM((count, FF), jnp.bfloat16),
            pltpu.SemaphoreType.DMA((SETS,)),
        ],
        compiler_params=pltpu.CompilerParams(vmem_limit_bytes=EXPERT_VMEM),
        name="own_expert",
    )(*in_vmem(rows), pltpu.with_memory_space_constraint(weights, pltpu.HBM))


def other_expert(weights, *blocks):
    rows = blocks[0].shape[0]
    vmem = pl.BlockSpec(memory_space=pltpu.VMEM)
    return pl.pallas_call(
        functools.partial(other_kernel, len(blocks)),
        out_shape=tuple(jax.ShapeDtypeStruct((rows, D), jnp.bfloat16) for block in blocks),
        in_specs=[vmem] * (len(blocks) + 1),
        out_specs=(vmem,) * len(blocks),
        scratch_shapes=[pltpu.VMEM((rows, FF), jnp.bfloat16)],
        compiler_params=pltpu.CompilerParams(vmem_limit_bytes=EXPERT_VMEM),
        name="other_expert",
    )(*in_vmem(*blocks, weights))


def summed(refs, rows):
    total = refs[0][rows].astype(jnp.float32)
    for ref in refs[1:]:
        total = total + ref[rows].astype(jnp.float32)
    return total


def join_kernel(residual_ref, *refs):
    parts_refs, out_ref, work_ref = refs[:-2], refs[-2], refs[-1]
    near = out_ref.shape[0]
    rows = work_ref.shape[0]
    step = 2 * TOK
    for start in range(0, rows, step):
        work_ref[start : start + step, :] = summed(parts_refs, slice(start, start + step))
    mine = pl.ds(pl.multiple_of(lax.axis_index("seq") * TOK, TOK), TOK)
    work_ref[mine, :] = work_ref[mine, :] + residual_ref[...]
    for seq in range(rows // TOK):
        far = seq // near
        out_ref[seq % near, far * TOK : (far + 1) * TOK, :] = work_ref[
            seq * TOK : (seq + 1) * TOK, :
        ].astype(jnp.bfloat16)


def join(residual, parts, near):
    rows = parts[0].shape[0]
    vmem = pl.BlockSpec(memory_space=pltpu.VMEM)
    return pl.pallas_call(
        join_kernel,
        out_shape=pltpu.VMEM((near, rows // near, D), jnp.bfloat16),
        in_specs=[vmem] * (len(parts) + 1),
        out_specs=vmem,
        scratch_shapes=[pltpu.VMEM((rows, D), jnp.float32)],
        compiler_params=pltpu.CompilerParams(vmem_limit_bytes=VMEM_LIMIT),
        name="join",
    )(*in_vmem(residual, *parts))


def fold_kernel(parts_ref, out_ref):
    width = D // SETS
    for far in range(parts_ref.shape[1] // TOK):
        for block in range(SETS):
            cols = slice(block * width, (block + 1) * width)
            total = parts_ref[0, far * TOK : (far + 1) * TOK, cols].astype(jnp.float32)
            for source in range(1, parts_ref.shape[0]):
                total = total + parts_ref[
                    source, far * TOK : (far + 1) * TOK, cols
                ].astype(jnp.float32)
            out_ref[far * SETS + block] = total.astype(jnp.bfloat16)


def fold(parts):
    far = parts.shape[1] // TOK
    vmem = pl.BlockSpec(memory_space=pltpu.VMEM)
    return pl.pallas_call(
        fold_kernel,
        out_shape=pltpu.VMEM((far * SETS, TOK, D // SETS), parts.dtype),
        in_specs=[vmem],
        out_specs=vmem,
        compiler_params=pltpu.CompilerParams(vmem_limit_bytes=VMEM_LIMIT),
        name="fold",
    )(*in_vmem(parts))


def total_kernel(parts_ref, out_ref):
    for source in range(SETS):
        total = parts_ref[source].astype(jnp.float32)
        for far in range(1, parts_ref.shape[0] // SETS):
            total = total + parts_ref[far * SETS + source].astype(jnp.float32)
        out_ref[0, source * TOK : (source + 1) * TOK, :] = total.astype(jnp.bfloat16)


def total(parts):
    vmem = pl.BlockSpec(memory_space=pltpu.VMEM)
    return pl.pallas_call(
        total_kernel,
        out_shape=jax.ShapeDtypeStruct((1, DRAFT, parts.shape[2]), parts.dtype),
        in_specs=[vmem],
        out_specs=vmem,
        compiler_params=pltpu.CompilerParams(vmem_limit_bytes=VMEM_LIMIT),
        name="total",
    )(*in_vmem(parts))


def shifted(value, axis, count, by):
    return lax.ppermute(value, axis, [(i, (i + by) % count) for i in range(count)])


def local(
    queries,
    draft_kv,
    kv_pool,
    page_table,
    cache_lens,
    parents,
    hidden,
    norm_gain,
    out_proj,
    router,
    routes,
    gate_w,
    up_w,
    down_w,
):
    kv_count = lax.axis_size("kv")
    seq_count = lax.axis_size("seq")
    weights = lax.all_gather(pack(gate_w, up_w, down_w), "exp")
    partials, out_proj = attention(
        page_table.reshape(PPD), cache_lens, queries, parents, draft_kv, kv_pool, out_proj
    )
    parts = lax.all_to_all(partials, "exp", 0, 0, tiled=True)
    projected = merge(parts, out_proj)
    shares = lax.all_to_all(projected.reshape(SETS, TOK, D), "exp", 0, 0, tiled=True)
    residual, row = norm(shares, hidden, norm_gain.reshape(1, D), router, routes)
    rows = lax.all_gather(row, "seq").reshape(seq_count * TOK, WIDE)
    arrived = {by: shifted(rows, "kv", kv_count, by) for by in range(1, kv_count)}
    own, kept = own_expert(rows, weights)
    near = other_expert(kept, arrived[1], arrived[kv_count - 1])
    parts = [
        own,
        shifted(near[0], "kv", kv_count, -1),
        shifted(near[1], "kv", kv_count, 1),
    ]
    for by in range(2, kv_count - 1):
        (far,) = other_expert(kept, arrived[by])
        parts.append(shifted(far, "kv", kv_count, -by))
    run = 4
    far_count = seq_count // run
    runs = [[far * run + near for near in range(run)] for far in range(far_count)]
    strides = [
        [
            (far * run + near) * SETS + block
            for far in range(far_count)
            for block in range(SETS)
        ]
        for near in range(run)
    ]
    back = join(residual, parts, run)
    back = lax.all_to_all(back, "seq", 0, 0, tiled=True, axis_index_groups=runs)
    back = lax.all_to_all(
        fold(back), ("seq", "exp"), 0, 0, tiled=True, axis_index_groups=strides
    )
    return total(back)


def solution(mesh):
    in_specs = (
        P(("kv", "seq"), None, None),
        P(None, ("kv", "seq"), "exp", None),
        P(None, ("kv", "seq", "exp"), None, None),
        P(("kv", "seq"), None, "exp"),
        P(("kv", "seq")),
        P(("kv", "seq"), None),
        P(("kv", "seq"), None, None),
        P(),
        P("exp", None),
        P(),
        P(("kv", "seq"), None, None),
        P(("kv", "seq"), None, "exp"),
        P(("kv", "seq"), None, "exp"),
        P(("kv", "seq"), "exp", None),
    )
    out_specs = P(("kv", "seq"), None, "exp")
    return jax.shard_map(local, mesh=mesh, in_specs=in_specs, out_specs=out_specs, check_vma=False)
```

```python
import functools

import jax
import jax.numpy as jnp
from jax import lax
from jax.experimental import pallas as pl
from jax.experimental.pallas import tpu as pltpu
from jax.sharding import PartitionSpec as P

D = 2048
H = 16
HD = 128
FF = 1024
EXPERTS = 64
TOPK = 8
DRAFT = 64
PAGE = 16
PPD = 12
SETS = 8
KEYS = PPD * PAGE
ROWS = KEYS + 16
TOK = DRAFT // SETS
WIDE = D + 2 * EXPERTS
STAT = DRAFT + 8
BLK = FF // SETS

NEG_FILL = -1e30
EPS_NORM = 1e-06
VMEM_LIMIT = 16 * 1024 * 1024
EXPERT_VMEM = 24 * 1024 * 1024


def nt(a, b):
    return lax.dot_general(a, b, (((1,), (1,)), ((), ())), preferred_element_type=jnp.float32)


def tn(a, b):
    return lax.dot_general(a, b, (((0,), (0,)), ((), ())), preferred_element_type=jnp.float32)


def nn(a, b):
    return lax.dot_general(a, b, (((1,), (0,)), ((), ())), preferred_element_type=jnp.float32)


def in_vmem(*arrays):
    return [pltpu.with_memory_space_constraint(x, pltpu.VMEM) for x in arrays]


def expert_index():
    return lax.axis_index("kv") * lax.axis_size("seq") + lax.axis_index("seq")


def attention_kernel(
    table,
    lens,
    q_hbm,
    parents_hbm,
    draft_hbm,
    pool_ref,
    proj_ref,
    routes_hbm,
    out_ref,
    kept_ref,
    chosen_ref,
    kbuf,
    vbuf,
    q_ref,
    draft_ref,
    parents_ref,
    routes_ref,
    mask_ref,
    seen_ref,
    score_ref,
    weight_ref,
    sems,
    more_sems,
):
    keys, values = [], []
    for page in range(PPD):
        slot = table[page]
        rows = pl.ds(page * PAGE, PAGE)
        keys.append(pltpu.make_async_copy(pool_ref.at[0, slot], kbuf.at[rows], sems.at[0, page]))
        values.append(pltpu.make_async_copy(pool_ref.at[1, slot], vbuf.at[rows], sems.at[1, page]))
    query_copy = pltpu.make_async_copy(q_hbm.at[0], q_ref, more_sems.at[0])
    draft_copy = pltpu.make_async_copy(draft_hbm.at[:, 0], draft_ref, more_sems.at[1])
    proj_copy = pltpu.make_async_copy(proj_ref, kept_ref, more_sems.at[2])
    parents_copy = pltpu.make_async_copy(parents_hbm, parents_ref, more_sems.at[3])
    routes_copy = pltpu.make_async_copy(routes_hbm.at[0], routes_ref, more_sems.at[4])
    for copy in [parents_copy, routes_copy, draft_copy, query_copy] + keys + values + [proj_copy]:
        copy.start()
    length = lens[0]
    my_set = lax.axis_index("exp")
    ancestor = lax.broadcasted_iota(jnp.int32, (DRAFT, 2 * DRAFT), 0)
    token = lax.broadcasted_iota(jnp.int32, (DRAFT, 2 * DRAFT), 1) % DRAFT
    parents_copy.wait()
    parents = jnp.concatenate([parents_ref[...], parents_ref[...]], axis=1)
    linked = jnp.where((parents == ancestor) | (ancestor == token), 1.0, 0.0)
    for doubling in range((DRAFT - 1).bit_length()):
        narrow = linked.astype(jnp.bfloat16)
        linked = jnp.minimum(nn(narrow[:, :DRAFT], narrow), 1.0)
    seen_ref[0:DRAFT, :] = linked
    draft_seen = seen_ref[pl.ds(pl.multiple_of(my_set * TOK, TOK), TOK), :]
    key_row = lax.broadcasted_iota(jnp.int32, (KEYS, 2 * DRAFT), 0)
    position = ((key_row // PAGE) * SETS + my_set) * PAGE + key_row % PAGE
    cache_seen = jnp.where(position < length, 1.0, 0.0)
    seen_ref[0:ROWS, :] = jnp.concatenate(
        [cache_seen, draft_seen, jnp.zeros((8, 2 * DRAFT), jnp.float32)], axis=0
    )
    own = (lax.broadcasted_iota(jnp.int32, (2 * DRAFT, 2 * HD), 0) < DRAFT) == (
        lax.broadcasted_iota(jnp.int32, (2 * DRAFT, 2 * HD), 1) < HD
    )
    stat_row = lax.broadcasted_iota(jnp.int32, (8, 2 * DRAFT), 0)
    routes_copy.wait()
    expert = lax.broadcasted_iota(jnp.int32, (EXPERTS, DRAFT), 0)
    chosen = routes_ref[0:1, :] == expert
    for pick in range(1, TOPK):
        chosen = chosen | (routes_ref[pick : pick + 1, :] == expert)
    mask_ref[...] = jnp.transpose(jnp.where(chosen, 1.0, 0.0))
    chosen_ref[...] = mask_ref[pl.ds(pl.multiple_of(my_set * TOK, TOK), TOK), :]
    pad = jnp.zeros((8, D), jnp.float32)
    draft_copy.wait()
    for place, buf in ((0, kbuf), (1, vbuf)):
        rows = jnp.concatenate([draft_ref[place].astype(jnp.float32), pad], axis=0)
        buf[KEYS:ROWS, :] = rows.astype(jnp.bfloat16)
    query_copy.wait()
    for copy in keys:
        copy.wait()
    for pair in range(H // 2):
        cols = slice(pair * 2 * HD, (pair + 1) * 2 * HD)
        query = q_ref[:, cols]
        query = jnp.where(own, jnp.concatenate([query, query], axis=0), jnp.zeros((), jnp.bfloat16))
        score_ref[pair] = nt(kbuf[:, cols], query) * (HD**-0.5)
    for pair in range(H // 2):
        seen = seen_ref[0:ROWS, :] > 0.5
        scores = jnp.where(seen, score_ref[pair], NEG_FILL)
        top = jnp.max(scores, axis=0, keepdims=True).astype(jnp.bfloat16).astype(jnp.float32)
        weights = jnp.where(seen, jnp.exp(scores - top), 0.0)
        total = jnp.sum(weights, axis=0, keepdims=True)
        weight_ref[pair] = weights.astype(jnp.bfloat16)
        total_high = total.astype(jnp.bfloat16).astype(jnp.float32)
        stats = jnp.where(
            stat_row == 0,
            top,
            jnp.where(stat_row == 1, total_high, jnp.where(stat_row == 2, total - total_high, 0.0)),
        )
        out_ref[pair, DRAFT:STAT, 0:HD] = stats.astype(jnp.bfloat16)
        out_ref[pair, DRAFT:STAT, HD : 2 * HD] = jnp.zeros((8, HD), jnp.bfloat16)
    for copy in values:
        copy.wait()
    for pair in range(H // 2):
        cols = slice(pair * 2 * HD, (pair + 1) * 2 * HD)
        acc = tn(weight_ref[pair], vbuf[:, cols])
        out_ref[pair, 0:DRAFT, 0:HD] = acc[:DRAFT, :HD].astype(jnp.bfloat16)
        out_ref[pair, 0:DRAFT, HD : 2 * HD] = acc[DRAFT:, HD:].astype(jnp.bfloat16)
    proj_copy.wait()


def attention(table, lens, queries, parents, draft_kv, kv_pool, out_proj, routes):
    smem = pl.BlockSpec(memory_space=pltpu.SMEM)
    vmem = pl.BlockSpec(memory_space=pltpu.VMEM)
    hbm = pl.BlockSpec(memory_space=pltpu.HBM)
    queries, parents, draft_kv, kv_pool, out_proj, routes = (
        pltpu.with_memory_space_constraint(x, pltpu.HBM)
        for x in (queries, parents, draft_kv, kv_pool, out_proj, routes)
    )
    return pl.pallas_call(
        attention_kernel,
        out_shape=(
            jax.ShapeDtypeStruct((SETS, STAT, 2 * HD), jnp.bfloat16),
            pltpu.VMEM(out_proj.shape, out_proj.dtype),
            pltpu.VMEM((TOK, EXPERTS), jnp.float32),
        ),
        in_specs=[smem, smem, hbm, hbm, hbm, hbm, hbm, hbm],
        out_specs=(vmem, vmem, vmem),
        scratch_shapes=[
            pltpu.VMEM((ROWS, D), jnp.bfloat16),
            pltpu.VMEM((ROWS, D), jnp.bfloat16),
            pltpu.VMEM((DRAFT, D), jnp.bfloat16),
            pltpu.VMEM((2, TOK, D), jnp.bfloat16),
            pltpu.VMEM((1, DRAFT), jnp.int32),
            pltpu.VMEM((TOPK, DRAFT), jnp.int32),
            pltpu.VMEM((DRAFT, EXPERTS), jnp.float32),
            pltpu.VMEM((ROWS, 2 * DRAFT), jnp.float32),
            pltpu.VMEM((H // 2, ROWS, 2 * DRAFT), jnp.float32),
            pltpu.VMEM((H // 2, ROWS, 2 * DRAFT), jnp.bfloat16),
            pltpu.SemaphoreType.DMA((2, PPD)),
            pltpu.SemaphoreType.DMA((5,)),
        ],
        compiler_params=pltpu.CompilerParams(vmem_limit_bytes=VMEM_LIMIT),
        name="attention",
    )(table, lens, queries, parents, draft_kv, kv_pool, out_proj, routes)


def merge_kernel(parts_ref, proj_ref, out_ref):
    stats = parts_ref[:, DRAFT:STAT, 0:HD].astype(jnp.float32)
    tops = stats[:, 0, :]
    totals = stats[:, 1, :] + stats[:, 2, :]
    scale = jnp.exp(tops - jnp.max(tops, axis=0, keepdims=True))
    scale = scale / jnp.sum(scale * totals, axis=0, keepdims=True)
    scale = jnp.transpose(scale)
    heads = []
    for head in range(2):
        joined = jnp.zeros((DRAFT, HD), jnp.float32)
        for source in range(SETS):
            part = parts_ref[source, 0:DRAFT, head * HD : (head + 1) * HD].astype(jnp.float32)
            joined = joined + part * scale[head * DRAFT : (head + 1) * DRAFT, source : source + 1]
        heads.append(joined.astype(jnp.bfloat16))
    out_ref[...] = nn(jnp.concatenate(heads, axis=1), proj_ref[...]).astype(jnp.bfloat16)


def merge(parts, out_proj):
    return pl.pallas_call(
        merge_kernel,
        out_shape=jax.ShapeDtypeStruct((DRAFT, D), jnp.bfloat16),
        compiler_params=pltpu.CompilerParams(vmem_limit_bytes=VMEM_LIMIT),
        name="merge",
    )(parts, *in_vmem(out_proj))


def norm_kernel(
    parts_ref,
    hidden_ref,
    gain_hbm,
    router_hbm,
    chosen_ref,
    residual_ref,
    row_ref,
    own_ref,
    gain_ref,
    router_ref,
    sems,
):
    mine = pl.ds(pl.multiple_of(lax.axis_index("exp") * TOK, TOK), TOK)
    copies = [
        pltpu.make_async_copy(hidden_ref.at[0, mine], own_ref, sems.at[0]),
        pltpu.make_async_copy(gain_hbm, gain_ref, sems.at[1]),
        pltpu.make_async_copy(router_hbm, router_ref, sems.at[2]),
    ]
    for copy in copies:
        copy.start()
    residual = parts_ref[0].astype(jnp.float32)
    for source in range(1, SETS):
        residual = residual + parts_ref[source].astype(jnp.float32)
    for copy in copies:
        copy.wait()
    residual = own_ref[...].astype(jnp.float32) + residual
    residual_ref[...] = residual
    mean_sq = jnp.mean(residual * residual, axis=1, keepdims=True)
    gain = gain_ref[...].astype(jnp.float32).reshape(1, D)
    normed = (residual * lax.rsqrt(mean_sq + EPS_NORM) * gain).astype(jnp.bfloat16)
    logits = nt(normed, router_ref[...])
    gates = jnp.where(chosen_ref[...] > 0.5, 1.0 / (1.0 + jnp.exp(-logits)), 0.0)
    high = gates.astype(jnp.bfloat16).astype(jnp.float32)
    row_ref[:, 0:D] = normed
    row_ref[:, D:WIDE] = jnp.concatenate([high, gates - high], axis=1).astype(jnp.bfloat16)


def norm(parts, hidden, norm_gain, router, chosen):
    vmem = pl.BlockSpec(memory_space=pltpu.VMEM)
    hbm = pl.BlockSpec(memory_space=pltpu.HBM)
    held = [
        pltpu.with_memory_space_constraint(x, pltpu.HBM) for x in (hidden, norm_gain, router)
    ]
    return pl.pallas_call(
        norm_kernel,
        out_shape=(
            pltpu.VMEM((TOK, D), jnp.float32),
            jax.ShapeDtypeStruct((TOK, WIDE), jnp.bfloat16),
        ),
        in_specs=[vmem, hbm, hbm, hbm, vmem],
        out_specs=(vmem, vmem),
        scratch_shapes=[
            pltpu.VMEM((TOK, D), jnp.bfloat16),
            pltpu.VMEM(norm_gain.shape, jnp.bfloat16),
            pltpu.VMEM((EXPERTS, D), jnp.bfloat16),
            pltpu.SemaphoreType.DMA((3,)),
        ],
        compiler_params=pltpu.CompilerParams(vmem_limit_bytes=VMEM_LIMIT),
        name="norm",
    )(*in_vmem(parts), *held, *in_vmem(chosen))


def pack_kernel(gate_ref, up_ref, down_ref, out_ref, buf, in_sems, out_sems):
    width = D // SETS
    pieces = []
    part = D // 4
    for piece in range(4):
        rows = pl.ds(piece * part, part)
        pieces.append(
            (
                [
                    (gate_ref.at[0, rows], buf.at[rows, pl.ds(0, BLK)]),
                    (up_ref.at[0, rows], buf.at[rows, pl.ds(BLK, BLK)]),
                ],
                rows,
            )
        )
    for half in range(2):
        blocks = range(half * SETS // 2, (half + 1) * SETS // 2)
        pieces.append(
            (
                [
                    (
                        down_ref.at[0, :, pl.ds(block * width, width)],
                        buf.at[pl.ds(D + block * BLK, BLK)],
                    )
                    for block in blocks
                ],
                pl.ds(D + half * FF // 2, FF // 2),
            )
        )
    loads = []
    count = 0
    for moves, rows in pieces:
        group = []
        for source, target in moves:
            group.append(pltpu.make_async_copy(source, target, in_sems.at[count]))
            count += 1
        loads.append((group, rows))
    for group, rows in loads:
        for copy in group:
            copy.start()
    stores = []
    for index, (group, rows) in enumerate(loads):
        for copy in group:
            copy.wait()
        store = pltpu.make_async_copy(buf.at[rows], out_ref.at[rows], out_sems.at[index])
        store.start()
        stores.append(store)
    for store in stores:
        store.wait()


def pack(gate_w, up_w, down_w):
    hbm = pl.BlockSpec(memory_space=pltpu.HBM)
    width = D // SETS
    return pl.pallas_call(
        pack_kernel,
        out_shape=jax.ShapeDtypeStruct((D + FF, width), gate_w.dtype),
        in_specs=[hbm] * 3,
        out_specs=hbm,
        scratch_shapes=[
            pltpu.VMEM((D + FF, width), jnp.bfloat16),
            pltpu.SemaphoreType.DMA((16,)),
            pltpu.SemaphoreType.DMA((6,)),
        ],
        compiler_params=pltpu.CompilerParams(vmem_limit_bytes=VMEM_LIMIT),
        name="pack",
    )(*(pltpu.with_memory_space_constraint(x, pltpu.HBM) for x in (gate_w, up_w, down_w)))


def expert_rows(my_expert, rows_ref, weights_ref, store, act_ref, before_block):
    gates = rows_ref[:, D:WIDE].astype(jnp.float32)
    lane = lax.broadcasted_iota(jnp.int32, gates.shape, 1) % EXPERTS
    scale = jnp.sum(jnp.where(lane == my_expert, gates, 0.0), axis=1, keepdims=True)
    for block in range(SETS):
        before_block(block)
        both = nn(rows_ref[:, 0:D], weights_ref[block, 0:D, :])
        gate, up = both[:, :BLK], both[:, BLK:]
        act = gate / (1.0 + jnp.exp(-gate)) * up
        act_ref[:, block * BLK : (block + 1) * BLK] = act.astype(jnp.bfloat16)
    width = D // SETS
    for block in range(SETS):
        down = weights_ref[:, D + block * BLK : D + (block + 1) * BLK, :].reshape(FF, width)
        store(block, (nn(act_ref[...], down) * scale).astype(jnp.bfloat16))


def columns_of(out_ref):
    width = D // SETS

    def store(block, value):
        out_ref[:, block * width : (block + 1) * width] = value

    return store


def own_kernel(rows_ref, weights_ref, out_ref, kept_ref, act_ref, sems):
    copies = [
        pltpu.make_async_copy(weights_ref.at[block], kept_ref.at[block], sems.at[block])
        for block in range(SETS)
    ]
    for copy in copies:
        copy.start()
    expert_rows(
        expert_index(),
        rows_ref,
        kept_ref,
        columns_of(out_ref),
        act_ref,
        lambda block: copies[block].wait(),
    )


def other_kernel(count, *refs):
    rows_refs, weights_ref, out_refs, act_ref = (
        refs[:count],
        refs[count],
        refs[count + 1 : 2 * count + 1],
        refs[2 * count + 1],
    )
    for rows_ref, out_ref in zip(rows_refs, out_refs):
        expert_rows(
            expert_index(), rows_ref, weights_ref, columns_of(out_ref), act_ref, lambda block: None
        )


def own_expert(rows, weights):
    count = rows.shape[0]
    vmem = pl.BlockSpec(memory_space=pltpu.VMEM)
    return pl.pallas_call(
        own_kernel,
        out_shape=(
            pltpu.VMEM((count, D), jnp.bfloat16),
            pltpu.VMEM(weights.shape, weights.dtype),
        ),
        in_specs=[vmem, pl.BlockSpec(memory_space=pltpu.HBM)],
        out_specs=(vmem, vmem),
        scratch_shapes=[
            pltpu.VMEM((count, FF), jnp.bfloat16),
            pltpu.SemaphoreType.DMA((SETS,)),
        ],
        compiler_params=pltpu.CompilerParams(vmem_limit_bytes=EXPERT_VMEM),
        name="own_expert",
    )(*in_vmem(rows), pltpu.with_memory_space_constraint(weights, pltpu.HBM))


def other_expert(weights, *blocks):
    rows = blocks[0].shape[0]
    vmem = pl.BlockSpec(memory_space=pltpu.VMEM)
    return pl.pallas_call(
        functools.partial(other_kernel, len(blocks)),
        out_shape=tuple(jax.ShapeDtypeStruct((rows, D), jnp.bfloat16) for block in blocks),
        in_specs=[vmem] * (len(blocks) + 1),
        out_specs=(vmem,) * len(blocks),
        scratch_shapes=[pltpu.VMEM((rows, FF), jnp.bfloat16)],
        compiler_params=pltpu.CompilerParams(vmem_limit_bytes=EXPERT_VMEM),
        name="other_expert",
    )(*in_vmem(*blocks, weights))


def summed(refs, rows):
    total = refs[0][rows].astype(jnp.float32)
    for ref in refs[1:]:
        total = total + ref[rows].astype(jnp.float32)
    return total


def join_kernel(residual_ref, *refs):
    parts_refs, out_ref, work_ref = refs[:-2], refs[-2], refs[-1]
    near = out_ref.shape[0] // SETS
    width = out_ref.shape[2]
    rows = work_ref.shape[0]
    step = 2 * TOK
    for start in range(0, rows, step):
        work_ref[start : start + step, :] = summed(parts_refs, slice(start, start + step))
    mine = pl.ds(pl.multiple_of(lax.axis_index("seq") * TOK, TOK), TOK)
    work_ref[mine, :] = work_ref[mine, :] + residual_ref[...]
    for seq in range(rows // TOK):
        far = seq // near
        for block in range(SETS):
            out_ref[(seq % near) * SETS + block, far * TOK : (far + 1) * TOK, :] = work_ref[
                seq * TOK : (seq + 1) * TOK, block * width : (block + 1) * width
            ].astype(jnp.bfloat16)


def join(residual, parts, near):
    rows = parts[0].shape[0]
    vmem = pl.BlockSpec(memory_space=pltpu.VMEM)
    return pl.pallas_call(
        join_kernel,
        out_shape=pltpu.VMEM((near * SETS, rows // near, D // SETS), jnp.bfloat16),
        in_specs=[vmem] * (len(parts) + 1),
        out_specs=vmem,
        scratch_shapes=[pltpu.VMEM((rows, D), jnp.float32)],
        compiler_params=pltpu.CompilerParams(vmem_limit_bytes=VMEM_LIMIT),
        name="join",
    )(*in_vmem(residual, *parts))


def fold_kernel(parts_ref, out_ref):
    for source in range(SETS):
        total = summed([parts_ref.at[near * SETS + source] for near in range(parts_ref.shape[0] // SETS)], ...)
        total = total.astype(jnp.bfloat16)
        for far in range(out_ref.shape[0]):
            out_ref[far, source * TOK : (source + 1) * TOK, :] = total[
                far * TOK : (far + 1) * TOK, :
            ]


def fold(parts):
    vmem = pl.BlockSpec(memory_space=pltpu.VMEM)
    return pl.pallas_call(
        fold_kernel,
        out_shape=pltpu.VMEM((parts.shape[1] // TOK, DRAFT, parts.shape[2]), parts.dtype),
        in_specs=[vmem],
        out_specs=vmem,
        compiler_params=pltpu.CompilerParams(vmem_limit_bytes=VMEM_LIMIT),
        name="fold",
    )(*in_vmem(parts))


def total_kernel(parts_ref, out_ref):
    total = summed([parts_ref.at[far] for far in range(parts_ref.shape[0])], ...)
    out_ref[0] = total.astype(jnp.bfloat16)


def total(parts):
    vmem = pl.BlockSpec(memory_space=pltpu.VMEM)
    return pl.pallas_call(
        total_kernel,
        out_shape=jax.ShapeDtypeStruct((1,) + parts.shape[1:], parts.dtype),
        in_specs=[vmem],
        out_specs=vmem,
        compiler_params=pltpu.CompilerParams(vmem_limit_bytes=VMEM_LIMIT),
        name="total",
    )(*in_vmem(parts))


def shifted(value, axis, count, by):
    return lax.ppermute(value, axis, [(i, (i + by) % count) for i in range(count)])


def local(
    queries,
    draft_kv,
    kv_pool,
    page_table,
    cache_lens,
    parents,
    hidden,
    norm_gain,
    out_proj,
    router,
    routes,
    gate_w,
    up_w,
    down_w,
):
    kv_count = lax.axis_size("kv")
    seq_count = lax.axis_size("seq")
    weights = lax.all_gather(pack(gate_w, up_w, down_w), "exp")
    partials, out_proj, chosen = attention(
        page_table.reshape(PPD),
        cache_lens,
        queries,
        parents,
        draft_kv,
        kv_pool,
        out_proj,
        jnp.transpose(routes, (0, 2, 1)),
    )
    parts = lax.all_to_all(partials, "exp", 0, 0, tiled=True)
    projected = merge(parts, out_proj)
    shares = lax.all_to_all(projected.reshape(SETS, TOK, D), "exp", 0, 0, tiled=True)
    residual, row = norm(shares, hidden, norm_gain, jnp.transpose(router), chosen)
    rows = lax.all_gather(row, "seq").reshape(seq_count * TOK, WIDE)
    arrived = {by: shifted(rows, "kv", kv_count, by) for by in range(1, kv_count)}
    own, kept = own_expert(rows, weights)
    near = other_expert(kept, arrived[1], arrived[kv_count - 1])
    parts = [
        own,
        shifted(near[0], "kv", kv_count, -1),
        shifted(near[1], "kv", kv_count, 1),
    ]
    for by in range(2, kv_count - 1):
        (far,) = other_expert(kept, arrived[by])
        parts.append(shifted(far, "kv", kv_count, -by))
    run = 4
    far_count = seq_count // run
    runs = [
        [(far * run + near) * SETS + block for near in range(run) for block in range(SETS)]
        for far in range(far_count)
    ]
    strides = [[far * run + near for far in range(far_count)] for near in range(run)]
    back = join(residual, parts, run)
    back = lax.all_to_all(back, ("seq", "exp"), 0, 0, tiled=True, axis_index_groups=runs)
    back = lax.all_to_all(fold(back), "seq", 0, 0, tiled=True, axis_index_groups=strides)
    return total(back)


def solution(mesh):
    in_specs = (
        P(("kv", "seq"), None, None),
        P(None, ("kv", "seq"), "exp", None),
        P(None, ("kv", "seq", "exp"), None, None),
        P(("kv", "seq"), None, "exp"),
        P(("kv", "seq")),
        P(("kv", "seq"), None),
        P(("kv", "seq"), None, None),
        P(),
        P("exp", None),
        P(),
        P(("kv", "seq"), None, None),
        P(("kv", "seq"), None, "exp"),
        P(("kv", "seq"), None, "exp"),
        P(("kv", "seq"), "exp", None),
    )
    out_specs = P(("kv", "seq"), None, "exp")
    return jax.shard_map(local, mesh=mesh, in_specs=in_specs, out_specs=out_specs, check_vma=False)
```

```python
import functools

import jax
import jax.numpy as jnp
from jax import lax
from jax.experimental import pallas as pl
from jax.experimental.pallas import tpu as pltpu
from jax.sharding import PartitionSpec as P

D = 2048
H = 16
HD = 128
FF = 1024
EXPERTS = 64
TOPK = 8
DRAFT = 64
PAGE = 16
PPD = 12
SETS = 8
KEYS = PPD * PAGE
ROWS = KEYS + 16
TOK = DRAFT // SETS
WIDE = D + 2 * EXPERTS
STAT = DRAFT + 8
BLK = FF // SETS

NEG_FILL = -1e30
EPS_NORM = 1e-06
VMEM_LIMIT = 16 * 1024 * 1024
EXPERT_VMEM = 24 * 1024 * 1024


def nt(a, b):
    return lax.dot_general(a, b, (((1,), (1,)), ((), ())), preferred_element_type=jnp.float32)


def tn(a, b):
    return lax.dot_general(a, b, (((0,), (0,)), ((), ())), preferred_element_type=jnp.float32)


def nn(a, b):
    return lax.dot_general(a, b, (((1,), (0,)), ((), ())), preferred_element_type=jnp.float32)


def in_vmem(*arrays):
    return [pltpu.with_memory_space_constraint(x, pltpu.VMEM) for x in arrays]


def expert_index():
    return lax.axis_index("kv") * lax.axis_size("seq") + lax.axis_index("seq")


def attention_kernel(
    table,
    lens,
    q_hbm,
    parents_hbm,
    draft_hbm,
    pool_ref,
    proj_ref,
    routes_hbm,
    out_ref,
    kept_ref,
    chosen_ref,
    kbuf,
    vbuf,
    q_ref,
    draft_ref,
    parents_ref,
    routes_ref,
    mask_ref,
    seen_ref,
    score_ref,
    weight_ref,
    sems,
    more_sems,
):
    keys, values = [], []
    for page in range(PPD):
        slot = table[page]
        rows = pl.ds(page * PAGE, PAGE)
        keys.append(pltpu.make_async_copy(pool_ref.at[0, slot], kbuf.at[rows], sems.at[0, page]))
        values.append(pltpu.make_async_copy(pool_ref.at[1, slot], vbuf.at[rows], sems.at[1, page]))
    query_copy = pltpu.make_async_copy(q_hbm.at[0], q_ref, more_sems.at[0])
    draft_copy = pltpu.make_async_copy(draft_hbm.at[:, 0], draft_ref, more_sems.at[1])
    proj_copy = pltpu.make_async_copy(proj_ref, kept_ref, more_sems.at[2])
    parents_copy = pltpu.make_async_copy(parents_hbm, parents_ref, more_sems.at[3])
    routes_copy = pltpu.make_async_copy(routes_hbm.at[0], routes_ref, more_sems.at[4])
    for copy in [parents_copy, routes_copy, draft_copy, query_copy] + keys + values + [proj_copy]:
        copy.start()
    length = lens[0]
    my_set = lax.axis_index("exp")
    ancestor = lax.broadcasted_iota(jnp.int32, (DRAFT, 2 * DRAFT), 0)
    token = lax.broadcasted_iota(jnp.int32, (DRAFT, 2 * DRAFT), 1) % DRAFT
    parents_copy.wait()
    parents = jnp.concatenate([parents_ref[...], parents_ref[...]], axis=1)
    linked = jnp.where((parents == ancestor) | (ancestor == token), 1.0, 0.0)
    for doubling in range((DRAFT - 1).bit_length()):
        narrow = linked.astype(jnp.bfloat16)
        linked = jnp.minimum(nn(narrow[:, :DRAFT], narrow), 1.0)
    seen_ref[0:DRAFT, :] = linked
    draft_seen = seen_ref[pl.ds(pl.multiple_of(my_set * TOK, TOK), TOK), :]
    key_row = lax.broadcasted_iota(jnp.int32, (KEYS, 2 * DRAFT), 0)
    position = ((key_row // PAGE) * SETS + my_set) * PAGE + key_row % PAGE
    cache_seen = jnp.where(position < length, 1.0, 0.0)
    seen_ref[0:ROWS, :] = jnp.concatenate(
        [cache_seen, draft_seen, jnp.zeros((8, 2 * DRAFT), jnp.float32)], axis=0
    )
    own = (lax.broadcasted_iota(jnp.int32, (2 * DRAFT, 2 * HD), 0) < DRAFT) == (
        lax.broadcasted_iota(jnp.int32, (2 * DRAFT, 2 * HD), 1) < HD
    )
    stat_row = lax.broadcasted_iota(jnp.int32, (8, 2 * DRAFT), 0)
    routes_copy.wait()
    expert = lax.broadcasted_iota(jnp.int32, (EXPERTS, DRAFT), 0)
    chosen = routes_ref[0:1, :] == expert
    for pick in range(1, TOPK):
        chosen = chosen | (routes_ref[pick : pick + 1, :] == expert)
    mask_ref[...] = jnp.transpose(jnp.where(chosen, 1.0, 0.0))
    chosen_ref[...] = mask_ref[pl.ds(pl.multiple_of(my_set * TOK, TOK), TOK), :]
    pad = jnp.zeros((8, D), jnp.float32)
    draft_copy.wait()
    for place, buf in ((0, kbuf), (1, vbuf)):
        rows = jnp.concatenate([draft_ref[place].astype(jnp.float32), pad], axis=0)
        buf[KEYS:ROWS, :] = rows.astype(jnp.bfloat16)
    query_copy.wait()
    for copy in keys:
        copy.wait()
    for pair in range(H // 2):
        cols = slice(pair * 2 * HD, (pair + 1) * 2 * HD)
        query = q_ref[:, cols]
        query = jnp.where(own, jnp.concatenate([query, query], axis=0), jnp.zeros((), jnp.bfloat16))
        score_ref[pair] = nt(kbuf[:, cols], query) * (HD**-0.5)
    for pair in range(H // 2):
        seen = seen_ref[0:ROWS, :] > 0.5
        scores = jnp.where(seen, score_ref[pair], NEG_FILL)
        top = jnp.max(scores, axis=0, keepdims=True).astype(jnp.bfloat16).astype(jnp.float32)
        weights = jnp.where(seen, jnp.exp(scores - top), 0.0)
        total = jnp.sum(weights, axis=0, keepdims=True)
        weight_ref[pair] = weights.astype(jnp.bfloat16)
        total_high = total.astype(jnp.bfloat16).astype(jnp.float32)
        stats = jnp.where(
            stat_row == 0,
            top,
            jnp.where(stat_row == 1, total_high, jnp.where(stat_row == 2, total - total_high, 0.0)),
        )
        out_ref[pair, DRAFT:STAT, 0:HD] = stats.astype(jnp.bfloat16)
        out_ref[pair, DRAFT:STAT, HD : 2 * HD] = jnp.zeros((8, HD), jnp.bfloat16)
    for copy in values:
        copy.wait()
    for pair in range(H // 2):
        cols = slice(pair * 2 * HD, (pair + 1) * 2 * HD)
        acc = tn(weight_ref[pair], vbuf[:, cols])
        out_ref[pair, 0:DRAFT, 0:HD] = acc[:DRAFT, :HD].astype(jnp.bfloat16)
        out_ref[pair, 0:DRAFT, HD : 2 * HD] = acc[DRAFT:, HD:].astype(jnp.bfloat16)
    proj_copy.wait()


def attention(table, lens, queries, parents, draft_kv, kv_pool, out_proj, routes):
    smem = pl.BlockSpec(memory_space=pltpu.SMEM)
    vmem = pl.BlockSpec(memory_space=pltpu.VMEM)
    hbm = pl.BlockSpec(memory_space=pltpu.HBM)
    queries, parents, draft_kv, kv_pool, out_proj, routes = (
        pltpu.with_memory_space_constraint(x, pltpu.HBM)
        for x in (queries, parents, draft_kv, kv_pool, out_proj, routes)
    )
    return pl.pallas_call(
        attention_kernel,
        out_shape=(
            jax.ShapeDtypeStruct((SETS, STAT, 2 * HD), jnp.bfloat16),
            pltpu.VMEM(out_proj.shape, out_proj.dtype),
            pltpu.VMEM((TOK, EXPERTS), jnp.float32),
        ),
        in_specs=[smem, smem, hbm, hbm, hbm, hbm, hbm, hbm],
        out_specs=(vmem, vmem, vmem),
        scratch_shapes=[
            pltpu.VMEM((ROWS, D), jnp.bfloat16),
            pltpu.VMEM((ROWS, D), jnp.bfloat16),
            pltpu.VMEM((DRAFT, D), jnp.bfloat16),
            pltpu.VMEM((2, TOK, D), jnp.bfloat16),
            pltpu.VMEM((1, DRAFT), jnp.int32),
            pltpu.VMEM((TOPK, DRAFT), jnp.int32),
            pltpu.VMEM((DRAFT, EXPERTS), jnp.float32),
            pltpu.VMEM((ROWS, 2 * DRAFT), jnp.float32),
            pltpu.VMEM((H // 2, ROWS, 2 * DRAFT), jnp.float32),
            pltpu.VMEM((H // 2, ROWS, 2 * DRAFT), jnp.bfloat16),
            pltpu.SemaphoreType.DMA((2, PPD)),
            pltpu.SemaphoreType.DMA((5,)),
        ],
        compiler_params=pltpu.CompilerParams(vmem_limit_bytes=VMEM_LIMIT),
        name="attention",
    )(table, lens, queries, parents, draft_kv, kv_pool, out_proj, routes)


def merge_kernel(parts_ref, proj_ref, out_ref):
    stats = parts_ref[:, DRAFT:STAT, 0:HD].astype(jnp.float32)
    tops = stats[:, 0, :]
    totals = stats[:, 1, :] + stats[:, 2, :]
    scale = jnp.exp(tops - jnp.max(tops, axis=0, keepdims=True))
    scale = scale / jnp.sum(scale * totals, axis=0, keepdims=True)
    scale = jnp.transpose(scale)
    heads = []
    for head in range(2):
        joined = jnp.zeros((DRAFT, HD), jnp.float32)
        for source in range(SETS):
            part = parts_ref[source, 0:DRAFT, head * HD : (head + 1) * HD].astype(jnp.float32)
            joined = joined + part * scale[head * DRAFT : (head + 1) * DRAFT, source : source + 1]
        heads.append(joined.astype(jnp.bfloat16))
    out_ref[...] = nn(jnp.concatenate(heads, axis=1), proj_ref[...]).astype(jnp.bfloat16)


def merge(parts, out_proj):
    return pl.pallas_call(
        merge_kernel,
        out_shape=jax.ShapeDtypeStruct((DRAFT, D), jnp.bfloat16),
        compiler_params=pltpu.CompilerParams(vmem_limit_bytes=VMEM_LIMIT),
        name="merge",
    )(parts, *in_vmem(out_proj))


def norm_kernel(
    parts_ref,
    hidden_ref,
    gain_hbm,
    router_hbm,
    chosen_ref,
    residual_ref,
    row_ref,
    own_ref,
    gain_ref,
    router_ref,
    sems,
):
    mine = pl.ds(pl.multiple_of(lax.axis_index("exp") * TOK, TOK), TOK)
    copies = [
        pltpu.make_async_copy(hidden_ref.at[0, mine], own_ref, sems.at[0]),
        pltpu.make_async_copy(gain_hbm, gain_ref, sems.at[1]),
        pltpu.make_async_copy(router_hbm, router_ref, sems.at[2]),
    ]
    for copy in copies:
        copy.start()
    residual = parts_ref[0].astype(jnp.float32)
    for source in range(1, SETS):
        residual = residual + parts_ref[source].astype(jnp.float32)
    for copy in copies:
        copy.wait()
    residual = own_ref[...].astype(jnp.float32) + residual
    residual_ref[...] = residual
    mean_sq = jnp.mean(residual * residual, axis=1, keepdims=True)
    gain = gain_ref[...].astype(jnp.float32).reshape(1, D)
    normed = (residual * lax.rsqrt(mean_sq + EPS_NORM) * gain).astype(jnp.bfloat16)
    logits = nt(normed, router_ref[...])
    gates = jnp.where(chosen_ref[...] > 0.5, 1.0 / (1.0 + jnp.exp(-logits)), 0.0)
    high = gates.astype(jnp.bfloat16).astype(jnp.float32)
    row_ref[:, 0:D] = normed
    row_ref[:, D:WIDE] = jnp.concatenate([high, gates - high], axis=1).astype(jnp.bfloat16)


def norm(parts, hidden, norm_gain, router, chosen):
    vmem = pl.BlockSpec(memory_space=pltpu.VMEM)
    hbm = pl.BlockSpec(memory_space=pltpu.HBM)
    held = [
        pltpu.with_memory_space_constraint(x, pltpu.HBM) for x in (hidden, norm_gain, router)
    ]
    return pl.pallas_call(
        norm_kernel,
        out_shape=(
            pltpu.VMEM((TOK, D), jnp.float32),
            jax.ShapeDtypeStruct((TOK, WIDE), jnp.bfloat16),
        ),
        in_specs=[vmem, hbm, hbm, hbm, vmem],
        out_specs=(vmem, vmem),
        scratch_shapes=[
            pltpu.VMEM((TOK, D), jnp.bfloat16),
            pltpu.VMEM(norm_gain.shape, jnp.bfloat16),
            pltpu.VMEM((EXPERTS, D), jnp.bfloat16),
            pltpu.SemaphoreType.DMA((3,)),
        ],
        compiler_params=pltpu.CompilerParams(vmem_limit_bytes=VMEM_LIMIT),
        name="norm",
    )(*in_vmem(parts), *held, *in_vmem(chosen))


def pack_kernel(gate_ref, up_ref, down_ref, out_ref, buf, in_sems, out_sems):
    width = D // SETS
    pieces = []
    part = D // 4
    for piece in range(4):
        rows = pl.ds(piece * part, part)
        pieces.append(
            (
                [
                    (gate_ref.at[0, rows], buf.at[rows, pl.ds(0, BLK)]),
                    (up_ref.at[0, rows], buf.at[rows, pl.ds(BLK, BLK)]),
                ],
                rows,
            )
        )
    for half in range(2):
        blocks = range(half * SETS // 2, (half + 1) * SETS // 2)
        pieces.append(
            (
                [
                    (
                        down_ref.at[0, :, pl.ds(block * width, width)],
                        buf.at[pl.ds(D + block * BLK, BLK)],
                    )
                    for block in blocks
                ],
                pl.ds(D + half * FF // 2, FF // 2),
            )
        )
    loads = []
    count = 0
    for moves, rows in pieces:
        group = []
        for source, target in moves:
            group.append(pltpu.make_async_copy(source, target, in_sems.at[count]))
            count += 1
        loads.append((group, rows))
    for group, rows in loads:
        for copy in group:
            copy.start()
    stores = []
    for index, (group, rows) in enumerate(loads):
        for copy in group:
            copy.wait()
        store = pltpu.make_async_copy(buf.at[rows], out_ref.at[rows], out_sems.at[index])
        store.start()
        stores.append(store)
    for store in stores:
        store.wait()


def pack(gate_w, up_w, down_w):
    hbm = pl.BlockSpec(memory_space=pltpu.HBM)
    width = D // SETS
    return pl.pallas_call(
        pack_kernel,
        out_shape=jax.ShapeDtypeStruct((D + FF, width), gate_w.dtype),
        in_specs=[hbm] * 3,
        out_specs=hbm,
        scratch_shapes=[
            pltpu.VMEM((D + FF, width), jnp.bfloat16),
            pltpu.SemaphoreType.DMA((16,)),
            pltpu.SemaphoreType.DMA((6,)),
        ],
        compiler_params=pltpu.CompilerParams(vmem_limit_bytes=VMEM_LIMIT),
        name="pack",
    )(*(pltpu.with_memory_space_constraint(x, pltpu.HBM) for x in (gate_w, up_w, down_w)))


def expert_rows(my_expert, rows_ref, weights_ref, store, act_ref, before_block):
    gates = rows_ref[:, D:WIDE].astype(jnp.float32)
    lane = lax.broadcasted_iota(jnp.int32, gates.shape, 1) % EXPERTS
    scale = jnp.sum(jnp.where(lane == my_expert, gates, 0.0), axis=1, keepdims=True)
    for block in range(SETS):
        before_block(block)
        both = nn(rows_ref[:, 0:D], weights_ref[block, 0:D, :])
        gate, up = both[:, :BLK], both[:, BLK:]
        act = gate / (1.0 + jnp.exp(-gate)) * up
        act_ref[:, block * BLK : (block + 1) * BLK] = act.astype(jnp.bfloat16)
    width = D // SETS
    for block in range(SETS):
        down = weights_ref[:, D + block * BLK : D + (block + 1) * BLK, :].reshape(FF, width)
        store(block, (nn(act_ref[...], down) * scale).astype(jnp.bfloat16))


def columns_of(out_ref):
    width = D // SETS

    def store(block, value):
        out_ref[:, block * width : (block + 1) * width] = value

    return store


def own_kernel(rows_ref, weights_ref, out_ref, kept_ref, act_ref, sems):
    copies = [
        pltpu.make_async_copy(weights_ref.at[block], kept_ref.at[block], sems.at[block])
        for block in range(SETS)
    ]
    for copy in copies:
        copy.start()
    expert_rows(
        expert_index(),
        rows_ref,
        kept_ref,
        columns_of(out_ref),
        act_ref,
        lambda block: copies[block].wait(),
    )


def other_kernel(count, *refs):
    rows_refs, weights_ref, out_refs, act_ref = (
        refs[:count],
        refs[count],
        refs[count + 1 : 2 * count + 1],
        refs[2 * count + 1],
    )
    for rows_ref, out_ref in zip(rows_refs, out_refs):
        expert_rows(
            expert_index(), rows_ref, weights_ref, columns_of(out_ref), act_ref, lambda block: None
        )


def own_expert(rows, weights):
    count = rows.shape[0]
    vmem = pl.BlockSpec(memory_space=pltpu.VMEM)
    return pl.pallas_call(
        own_kernel,
        out_shape=(
            pltpu.VMEM((count, D), jnp.bfloat16),
            pltpu.VMEM(weights.shape, weights.dtype),
        ),
        in_specs=[vmem, pl.BlockSpec(memory_space=pltpu.HBM)],
        out_specs=(vmem, vmem),
        scratch_shapes=[
            pltpu.VMEM((count, FF), jnp.bfloat16),
            pltpu.SemaphoreType.DMA((SETS,)),
        ],
        compiler_params=pltpu.CompilerParams(vmem_limit_bytes=EXPERT_VMEM),
        name="own_expert",
    )(*in_vmem(rows), pltpu.with_memory_space_constraint(weights, pltpu.HBM))


def other_expert(weights, *blocks):
    rows = blocks[0].shape[0]
    vmem = pl.BlockSpec(memory_space=pltpu.VMEM)
    return pl.pallas_call(
        functools.partial(other_kernel, len(blocks)),
        out_shape=tuple(jax.ShapeDtypeStruct((rows, D), jnp.bfloat16) for block in blocks),
        in_specs=[vmem] * (len(blocks) + 1),
        out_specs=(vmem,) * len(blocks),
        scratch_shapes=[pltpu.VMEM((rows, FF), jnp.bfloat16)],
        compiler_params=pltpu.CompilerParams(vmem_limit_bytes=EXPERT_VMEM),
        name="other_expert",
    )(*in_vmem(*blocks, weights))


def summed(refs, rows):
    total = refs[0][rows].astype(jnp.float32)
    for ref in refs[1:]:
        total = total + ref[rows].astype(jnp.float32)
    return total


def join_kernel(residual_ref, *refs):
    parts_refs, out_ref, work_ref = refs[:-2], refs[-2], refs[-1]
    near = out_ref.shape[0]
    rows = work_ref.shape[0]
    step = 2 * TOK
    for start in range(0, rows, step):
        work_ref[start : start + step, :] = summed(parts_refs, slice(start, start + step))
    mine = pl.ds(pl.multiple_of(lax.axis_index("seq") * TOK, TOK), TOK)
    work_ref[mine, :] = work_ref[mine, :] + residual_ref[...]
    for seq in range(rows // TOK):
        far = seq // near
        out_ref[seq % near, far * TOK : (far + 1) * TOK, :] = work_ref[
            seq * TOK : (seq + 1) * TOK, :
        ].astype(jnp.bfloat16)


def join(residual, parts, near):
    rows = parts[0].shape[0]
    vmem = pl.BlockSpec(memory_space=pltpu.VMEM)
    return pl.pallas_call(
        join_kernel,
        out_shape=pltpu.VMEM((near, rows // near, D), jnp.bfloat16),
        in_specs=[vmem] * (len(parts) + 1),
        out_specs=vmem,
        scratch_shapes=[pltpu.VMEM((rows, D), jnp.float32)],
        compiler_params=pltpu.CompilerParams(vmem_limit_bytes=VMEM_LIMIT),
        name="join",
    )(*in_vmem(residual, *parts))


def fold_kernel(parts_ref, out_ref):
    width = D // SETS
    for far in range(parts_ref.shape[1] // TOK):
        for block in range(SETS):
            cols = slice(block * width, (block + 1) * width)
            total = parts_ref[0, far * TOK : (far + 1) * TOK, cols].astype(jnp.float32)
            for source in range(1, parts_ref.shape[0]):
                total = total + parts_ref[
                    source, far * TOK : (far + 1) * TOK, cols
                ].astype(jnp.float32)
            out_ref[far * SETS + block] = total.astype(jnp.bfloat16)


def fold(parts):
    far = parts.shape[1] // TOK
    vmem = pl.BlockSpec(memory_space=pltpu.VMEM)
    return pl.pallas_call(
        fold_kernel,
        out_shape=pltpu.VMEM((far * SETS, TOK, D // SETS), parts.dtype),
        in_specs=[vmem],
        out_specs=vmem,
        compiler_params=pltpu.CompilerParams(vmem_limit_bytes=VMEM_LIMIT),
        name="fold",
    )(*in_vmem(parts))


def total_kernel(parts_ref, out_ref):
    for source in range(SETS):
        total = parts_ref[source].astype(jnp.float32)
        for far in range(1, parts_ref.shape[0] // SETS):
            total = total + parts_ref[far * SETS + source].astype(jnp.float32)
        out_ref[0, source * TOK : (source + 1) * TOK, :] = total.astype(jnp.bfloat16)


def total(parts):
    vmem = pl.BlockSpec(memory_space=pltpu.VMEM)
    return pl.pallas_call(
        total_kernel,
        out_shape=jax.ShapeDtypeStruct((1, DRAFT, parts.shape[2]), parts.dtype),
        in_specs=[vmem],
        out_specs=vmem,
        compiler_params=pltpu.CompilerParams(vmem_limit_bytes=VMEM_LIMIT),
        name="total",
    )(*in_vmem(parts))


def shifted(value, axis, count, by):
    return lax.ppermute(value, axis, [(i, (i + by) % count) for i in range(count)])


def local(
    queries,
    draft_kv,
    kv_pool,
    page_table,
    cache_lens,
    parents,
    hidden,
    norm_gain,
    out_proj,
    router,
    routes,
    gate_w,
    up_w,
    down_w,
):
    kv_count = lax.axis_size("kv")
    seq_count = lax.axis_size("seq")
    weights = lax.all_gather(pack(gate_w, up_w, down_w), "exp")
    partials, out_proj, chosen = attention(
        page_table.reshape(PPD),
        cache_lens,
        queries,
        parents,
        draft_kv,
        kv_pool,
        out_proj,
        jnp.transpose(routes, (0, 2, 1)),
    )
    parts = lax.all_to_all(partials, "exp", 0, 0, tiled=True)
    projected = merge(parts, out_proj)
    shares = lax.all_to_all(projected.reshape(SETS, TOK, D), "exp", 0, 0, tiled=True)
    residual, row = norm(shares, hidden, norm_gain, jnp.transpose(router), chosen)
    rows = lax.all_gather(row, "seq").reshape(seq_count * TOK, WIDE)
    arrived = {by: shifted(rows, "kv", kv_count, by) for by in range(1, kv_count)}
    own, kept = own_expert(rows, weights)
    near = other_expert(kept, arrived[1], arrived[kv_count - 1])
    parts = [
        own,
        shifted(near[0], "kv", kv_count, -1),
        shifted(near[1], "kv", kv_count, 1),
    ]
    for by in range(2, kv_count - 1):
        (far,) = other_expert(kept, arrived[by])
        parts.append(shifted(far, "kv", kv_count, -by))
    run = 4
    far_count = seq_count // run
    runs = [[far * run + near for near in range(run)] for far in range(far_count)]
    strides = [
        [
            (far * run + near) * SETS + block
            for far in range(far_count)
            for block in range(SETS)
        ]
        for near in range(run)
    ]
    back = join(residual, parts, run)
    back = lax.all_to_all(back, "seq", 0, 0, tiled=True, axis_index_groups=runs)
    back = lax.all_to_all(
        fold(back), ("seq", "exp"), 0, 0, tiled=True, axis_index_groups=strides
    )
    return total(back)


def solution(mesh):
    in_specs = (
        P(("kv", "seq"), None, None),
        P(None, ("kv", "seq"), "exp", None),
        P(None, ("kv", "seq", "exp"), None, None),
        P(("kv", "seq"), None, "exp"),
        P(("kv", "seq")),
        P(("kv", "seq"), None),
        P(("kv", "seq"), None, None),
        P(),
        P("exp", None),
        P(),
        P(("kv", "seq"), None, None),
        P(("kv", "seq"), None, "exp"),
        P(("kv", "seq"), None, "exp"),
        P(("kv", "seq"), "exp", None),
    )
    out_specs = P(("kv", "seq"), None, "exp")
    return jax.shard_map(local, mesh=mesh, in_specs=in_specs, out_specs=out_specs, check_vma=False)
```

```python
import functools

import jax
import jax.numpy as jnp
from jax import lax
from jax.experimental import pallas as pl
from jax.experimental.pallas import tpu as pltpu
from jax.sharding import PartitionSpec as P

D = 2048
H = 16
HD = 128
FF = 1024
EXPERTS = 64
TOPK = 8
DRAFT = 64
PAGE = 16
PPD = 12
SETS = 8
KEYS = PPD * PAGE
ROWS = KEYS + 16
TOK = DRAFT // SETS
WIDE = D + 2 * EXPERTS
STAT = DRAFT + 8
BLK = FF // SETS

NEG_FILL = -1e30
EPS_NORM = 1e-06
VMEM_LIMIT = 16 * 1024 * 1024
EXPERT_VMEM = 24 * 1024 * 1024


def nt(a, b):
    return lax.dot_general(a, b, (((1,), (1,)), ((), ())), preferred_element_type=jnp.float32)


def tn(a, b):
    return lax.dot_general(a, b, (((0,), (0,)), ((), ())), preferred_element_type=jnp.float32)


def nn(a, b):
    return lax.dot_general(a, b, (((1,), (0,)), ((), ())), preferred_element_type=jnp.float32)


def in_vmem(*arrays):
    return [pltpu.with_memory_space_constraint(x, pltpu.VMEM) for x in arrays]


def expert_index():
    return lax.axis_index("kv") * lax.axis_size("seq") + lax.axis_index("seq")


def attention_kernel(
    table,
    lens,
    q_hbm,
    parents_hbm,
    draft_hbm,
    pool_ref,
    proj_ref,
    routes_hbm,
    out_ref,
    kept_ref,
    chosen_ref,
    kbuf,
    vbuf,
    q_ref,
    draft_ref,
    parents_ref,
    routes_ref,
    mask_ref,
    seen_ref,
    score_ref,
    weight_ref,
    sems,
    more_sems,
):
    keys, values = [], []
    for page in range(PPD):
        slot = table[page]
        rows = pl.ds(page * PAGE, PAGE)
        keys.append(pltpu.make_async_copy(pool_ref.at[0, slot], kbuf.at[rows], sems.at[0, page]))
        values.append(pltpu.make_async_copy(pool_ref.at[1, slot], vbuf.at[rows], sems.at[1, page]))
    query_copy = pltpu.make_async_copy(q_hbm.at[0], q_ref, more_sems.at[0])
    draft_copy = pltpu.make_async_copy(draft_hbm.at[:, 0], draft_ref, more_sems.at[1])
    proj_copy = pltpu.make_async_copy(proj_ref, kept_ref, more_sems.at[2])
    parents_copy = pltpu.make_async_copy(parents_hbm, parents_ref, more_sems.at[3])
    routes_copy = pltpu.make_async_copy(routes_hbm.at[0], routes_ref, more_sems.at[4])
    for copy in [parents_copy, routes_copy, draft_copy, query_copy] + keys + values + [proj_copy]:
        copy.start()
    length = lens[0]
    my_set = lax.axis_index("exp")
    ancestor = lax.broadcasted_iota(jnp.int32, (DRAFT, 2 * DRAFT), 0)
    token = lax.broadcasted_iota(jnp.int32, (DRAFT, 2 * DRAFT), 1) % DRAFT
    parents_copy.wait()
    parents = jnp.concatenate([parents_ref[...], parents_ref[...]], axis=1)
    linked = jnp.where((parents == ancestor) | (ancestor == token), 1.0, 0.0)
    for doubling in range((DRAFT - 1).bit_length()):
        narrow = linked.astype(jnp.bfloat16)
        linked = jnp.minimum(nn(narrow[:, :DRAFT], narrow), 1.0)
    seen_ref[0:DRAFT, :] = linked
    draft_seen = seen_ref[pl.ds(pl.multiple_of(my_set * TOK, TOK), TOK), :]
    key_row = lax.broadcasted_iota(jnp.int32, (KEYS, 2 * DRAFT), 0)
    position = ((key_row // PAGE) * SETS + my_set) * PAGE + key_row % PAGE
    cache_seen = jnp.where(position < length, 1.0, 0.0)
    seen_ref[0:ROWS, :] = jnp.concatenate(
        [cache_seen, draft_seen, jnp.zeros((8, 2 * DRAFT), jnp.float32)], axis=0
    )
    own = (lax.broadcasted_iota(jnp.int32, (2 * DRAFT, 2 * HD), 0) < DRAFT) == (
        lax.broadcasted_iota(jnp.int32, (2 * DRAFT, 2 * HD), 1) < HD
    )
    stat_row = lax.broadcasted_iota(jnp.int32, (8, 2 * DRAFT), 0)
    routes_copy.wait()
    expert = lax.broadcasted_iota(jnp.int32, (EXPERTS, DRAFT), 0)
    chosen = routes_ref[0:1, :] == expert
    for pick in range(1, TOPK):
        chosen = chosen | (routes_ref[pick : pick + 1, :] == expert)
    mask_ref[...] = jnp.transpose(jnp.where(chosen, 1.0, 0.0))
    chosen_ref[...] = mask_ref[pl.ds(pl.multiple_of(my_set * TOK, TOK), TOK), :]
    pad = jnp.zeros((8, D), jnp.float32)
    draft_copy.wait()
    for place, buf in ((0, kbuf), (1, vbuf)):
        rows = jnp.concatenate([draft_ref[place].astype(jnp.float32), pad], axis=0)
        buf[KEYS:ROWS, :] = rows.astype(jnp.bfloat16)
    query_copy.wait()
    for copy in keys:
        copy.wait()
    for pair in range(H // 2):
        cols = slice(pair * 2 * HD, (pair + 1) * 2 * HD)
        query = q_ref[:, cols]
        query = jnp.where(own, jnp.concatenate([query, query], axis=0), jnp.zeros((), jnp.bfloat16))
        score_ref[pair] = nt(kbuf[:, cols], query) * (HD**-0.5)
    for pair in range(H // 2):
        seen = seen_ref[0:ROWS, :] > 0.5
        scores = jnp.where(seen, score_ref[pair], NEG_FILL)
        top = jnp.max(scores, axis=0, keepdims=True).astype(jnp.bfloat16).astype(jnp.float32)
        weights = jnp.where(seen, jnp.exp(scores - top), 0.0)
        total = jnp.sum(weights, axis=0, keepdims=True)
        weight_ref[pair] = weights.astype(jnp.bfloat16)
        total_high = total.astype(jnp.bfloat16).astype(jnp.float32)
        stats = jnp.where(
            stat_row == 0,
            top,
            jnp.where(stat_row == 1, total_high, jnp.where(stat_row == 2, total - total_high, 0.0)),
        )
        out_ref[pair, DRAFT:STAT, 0:HD] = stats.astype(jnp.bfloat16)
        out_ref[pair, DRAFT:STAT, HD : 2 * HD] = jnp.zeros((8, HD), jnp.bfloat16)
    for copy in values:
        copy.wait()
    for pair in range(H // 2):
        cols = slice(pair * 2 * HD, (pair + 1) * 2 * HD)
        acc = tn(weight_ref[pair], vbuf[:, cols])
        out_ref[pair, 0:DRAFT, 0:HD] = acc[:DRAFT, :HD].astype(jnp.bfloat16)
        out_ref[pair, 0:DRAFT, HD : 2 * HD] = acc[DRAFT:, HD:].astype(jnp.bfloat16)
    proj_copy.wait()


def attention(table, lens, queries, parents, draft_kv, kv_pool, out_proj, routes):
    smem = pl.BlockSpec(memory_space=pltpu.SMEM)
    vmem = pl.BlockSpec(memory_space=pltpu.VMEM)
    hbm = pl.BlockSpec(memory_space=pltpu.HBM)
    queries, parents, draft_kv, kv_pool, out_proj, routes = (
        pltpu.with_memory_space_constraint(x, pltpu.HBM)
        for x in (queries, parents, draft_kv, kv_pool, out_proj, routes)
    )
    return pl.pallas_call(
        attention_kernel,
        out_shape=(
            jax.ShapeDtypeStruct((SETS, STAT, 2 * HD), jnp.bfloat16),
            pltpu.VMEM(out_proj.shape, out_proj.dtype),
            pltpu.VMEM((TOK, EXPERTS), jnp.float32),
        ),
        in_specs=[smem, smem, hbm, hbm, hbm, hbm, hbm, hbm],
        out_specs=(vmem, vmem, vmem),
        scratch_shapes=[
            pltpu.VMEM((ROWS, D), jnp.bfloat16),
            pltpu.VMEM((ROWS, D), jnp.bfloat16),
            pltpu.VMEM((DRAFT, D), jnp.bfloat16),
            pltpu.VMEM((2, TOK, D), jnp.bfloat16),
            pltpu.VMEM((1, DRAFT), jnp.int32),
            pltpu.VMEM((TOPK, DRAFT), jnp.int32),
            pltpu.VMEM((DRAFT, EXPERTS), jnp.float32),
            pltpu.VMEM((ROWS, 2 * DRAFT), jnp.float32),
            pltpu.VMEM((H // 2, ROWS, 2 * DRAFT), jnp.float32),
            pltpu.VMEM((H // 2, ROWS, 2 * DRAFT), jnp.bfloat16),
            pltpu.SemaphoreType.DMA((2, PPD)),
            pltpu.SemaphoreType.DMA((5,)),
        ],
        compiler_params=pltpu.CompilerParams(vmem_limit_bytes=VMEM_LIMIT),
        name="attention",
    )(table, lens, queries, parents, draft_kv, kv_pool, out_proj, routes)


def merge_kernel(parts_ref, proj_ref, out_ref):
    stats = parts_ref[:, DRAFT:STAT, 0:HD].astype(jnp.float32)
    tops = stats[:, 0, :]
    totals = stats[:, 1, :] + stats[:, 2, :]
    scale = jnp.exp(tops - jnp.max(tops, axis=0, keepdims=True))
    scale = scale / jnp.sum(scale * totals, axis=0, keepdims=True)
    scale = jnp.transpose(scale)
    heads = []
    for head in range(2):
        joined = jnp.zeros((DRAFT, HD), jnp.float32)
        for source in range(SETS):
            part = parts_ref[source, 0:DRAFT, head * HD : (head + 1) * HD].astype(jnp.float32)
            joined = joined + part * scale[head * DRAFT : (head + 1) * DRAFT, source : source + 1]
        heads.append(joined.astype(jnp.bfloat16))
    out_ref[...] = nn(jnp.concatenate(heads, axis=1), proj_ref[...]).astype(jnp.bfloat16)


def merge(parts, out_proj):
    return pl.pallas_call(
        merge_kernel,
        out_shape=jax.ShapeDtypeStruct((DRAFT, D), jnp.bfloat16),
        compiler_params=pltpu.CompilerParams(vmem_limit_bytes=VMEM_LIMIT),
        name="merge",
    )(parts, *in_vmem(out_proj))


def norm_kernel(
    parts_ref,
    hidden_ref,
    gain_hbm,
    router_hbm,
    chosen_ref,
    residual_ref,
    row_ref,
    own_ref,
    gain_ref,
    router_ref,
    sems,
):
    mine = pl.ds(pl.multiple_of(lax.axis_index("exp") * TOK, TOK), TOK)
    copies = [
        pltpu.make_async_copy(hidden_ref.at[0, mine], own_ref, sems.at[0]),
        pltpu.make_async_copy(gain_hbm, gain_ref, sems.at[1]),
        pltpu.make_async_copy(router_hbm, router_ref, sems.at[2]),
    ]
    for copy in copies:
        copy.start()
    residual = parts_ref[0].astype(jnp.float32)
    for source in range(1, SETS):
        residual = residual + parts_ref[source].astype(jnp.float32)
    for copy in copies:
        copy.wait()
    residual = own_ref[...].astype(jnp.float32) + residual
    residual_ref[...] = residual
    mean_sq = jnp.mean(residual * residual, axis=1, keepdims=True)
    gain = gain_ref[...].astype(jnp.float32).reshape(1, D)
    normed = (residual * lax.rsqrt(mean_sq + EPS_NORM) * gain).astype(jnp.bfloat16)
    logits = nt(normed, router_ref[...])
    gates = jnp.where(chosen_ref[...] > 0.5, 1.0 / (1.0 + jnp.exp(-logits)), 0.0)
    high = gates.astype(jnp.bfloat16).astype(jnp.float32)
    row_ref[:, 0:D] = normed
    row_ref[:, D:WIDE] = jnp.concatenate([high, gates - high], axis=1).astype(jnp.bfloat16)


def norm(parts, hidden, norm_gain, router, chosen):
    vmem = pl.BlockSpec(memory_space=pltpu.VMEM)
    hbm = pl.BlockSpec(memory_space=pltpu.HBM)
    held = [
        pltpu.with_memory_space_constraint(x, pltpu.HBM) for x in (hidden, norm_gain, router)
    ]
    return pl.pallas_call(
        norm_kernel,
        out_shape=(
            pltpu.VMEM((TOK, D), jnp.float32),
            jax.ShapeDtypeStruct((TOK, WIDE), jnp.bfloat16),
        ),
        in_specs=[vmem, hbm, hbm, hbm, vmem],
        out_specs=(vmem, vmem),
        scratch_shapes=[
            pltpu.VMEM((TOK, D), jnp.bfloat16),
            pltpu.VMEM(norm_gain.shape, jnp.bfloat16),
            pltpu.VMEM((EXPERTS, D), jnp.bfloat16),
            pltpu.SemaphoreType.DMA((3,)),
        ],
        compiler_params=pltpu.CompilerParams(vmem_limit_bytes=VMEM_LIMIT),
        name="norm",
    )(*in_vmem(parts), *held, *in_vmem(chosen))


def pack_kernel(gate_ref, up_ref, down_ref, out_ref, buf, in_sems, out_sems):
    width = D // SETS
    pieces = []
    part = D // 4
    for piece in range(4):
        rows = pl.ds(piece * part, part)
        pieces.append(
            (
                [
                    (gate_ref.at[0, rows], buf.at[rows, pl.ds(0, BLK)]),
                    (up_ref.at[0, rows], buf.at[rows, pl.ds(BLK, BLK)]),
                ],
                rows,
            )
        )
    for half in range(2):
        blocks = range(half * SETS // 2, (half + 1) * SETS // 2)
        pieces.append(
            (
                [
                    (
                        down_ref.at[0, :, pl.ds(block * width, width)],
                        buf.at[pl.ds(D + block * BLK, BLK)],
                    )
                    for block in blocks
                ],
                pl.ds(D + half * FF // 2, FF // 2),
            )
        )
    loads = []
    count = 0
    for moves, rows in pieces:
        group = []
        for source, target in moves:
            group.append(pltpu.make_async_copy(source, target, in_sems.at[count]))
            count += 1
        loads.append((group, rows))
    for group, rows in loads:
        for copy in group:
            copy.start()
    stores = []
    for index, (group, rows) in enumerate(loads):
        for copy in group:
            copy.wait()
        store = pltpu.make_async_copy(buf.at[rows], out_ref.at[rows], out_sems.at[index])
        store.start()
        stores.append(store)
    for store in stores:
        store.wait()


def pack(gate_w, up_w, down_w):
    hbm = pl.BlockSpec(memory_space=pltpu.HBM)
    width = D // SETS
    return pl.pallas_call(
        pack_kernel,
        out_shape=jax.ShapeDtypeStruct((D + FF, width), gate_w.dtype),
        in_specs=[hbm] * 3,
        out_specs=hbm,
        scratch_shapes=[
            pltpu.VMEM((D + FF, width), jnp.bfloat16),
            pltpu.SemaphoreType.DMA((16,)),
            pltpu.SemaphoreType.DMA((6,)),
        ],
        compiler_params=pltpu.CompilerParams(vmem_limit_bytes=VMEM_LIMIT),
        name="pack",
    )(*(pltpu.with_memory_space_constraint(x, pltpu.HBM) for x in (gate_w, up_w, down_w)))


def expert_rows(my_expert, rows_ref, weights_ref, store, act_ref, before_block):
    gates = rows_ref[:, D:WIDE].astype(jnp.float32)
    lane = lax.broadcasted_iota(jnp.int32, gates.shape, 1) % EXPERTS
    scale = jnp.sum(jnp.where(lane == my_expert, gates, 0.0), axis=1, keepdims=True)
    for block in range(SETS):
        before_block(block)
        both = nn(rows_ref[:, 0:D], weights_ref[block, 0:D, :])
        gate, up = both[:, :BLK], both[:, BLK:]
        act = gate / (1.0 + jnp.exp(-gate)) * up
        act_ref[:, block * BLK : (block + 1) * BLK] = act.astype(jnp.bfloat16)
    width = D // SETS
    for block in range(SETS):
        down = weights_ref[:, D + block * BLK : D + (block + 1) * BLK, :].reshape(FF, width)
        store(block, (nn(act_ref[...], down) * scale).astype(jnp.bfloat16))


def columns_of(out_ref):
    width = D // SETS

    def store(block, value):
        out_ref[:, block * width : (block + 1) * width] = value

    return store


def own_kernel(rows_ref, weights_ref, out_ref, kept_ref, act_ref, sems):
    copies = [
        pltpu.make_async_copy(weights_ref.at[block], kept_ref.at[block], sems.at[block])
        for block in range(SETS)
    ]
    for copy in copies:
        copy.start()
    expert_rows(
        expert_index(),
        rows_ref,
        kept_ref,
        columns_of(out_ref),
        act_ref,
        lambda block: copies[block].wait(),
    )


def other_kernel(count, *refs):
    rows_refs, weights_ref, out_refs, act_ref = (
        refs[:count],
        refs[count],
        refs[count + 1 : 2 * count + 1],
        refs[2 * count + 1],
    )
    for rows_ref, out_ref in zip(rows_refs, out_refs):
        expert_rows(
            expert_index(), rows_ref, weights_ref, columns_of(out_ref), act_ref, lambda block: None
        )


def own_expert(rows, weights):
    count = rows.shape[0]
    vmem = pl.BlockSpec(memory_space=pltpu.VMEM)
    return pl.pallas_call(
        own_kernel,
        out_shape=(
            pltpu.VMEM((count, D), jnp.bfloat16),
            pltpu.VMEM(weights.shape, weights.dtype),
        ),
        in_specs=[vmem, pl.BlockSpec(memory_space=pltpu.HBM)],
        out_specs=(vmem, vmem),
        scratch_shapes=[
            pltpu.VMEM((count, FF), jnp.bfloat16),
            pltpu.SemaphoreType.DMA((SETS,)),
        ],
        compiler_params=pltpu.CompilerParams(vmem_limit_bytes=EXPERT_VMEM),
        name="own_expert",
    )(*in_vmem(rows), pltpu.with_memory_space_constraint(weights, pltpu.HBM))


def other_expert(weights, *blocks):
    rows = blocks[0].shape[0]
    vmem = pl.BlockSpec(memory_space=pltpu.VMEM)
    return pl.pallas_call(
        functools.partial(other_kernel, len(blocks)),
        out_shape=tuple(jax.ShapeDtypeStruct((rows, D), jnp.bfloat16) for block in blocks),
        in_specs=[vmem] * (len(blocks) + 1),
        out_specs=(vmem,) * len(blocks),
        scratch_shapes=[pltpu.VMEM((rows, FF), jnp.bfloat16)],
        compiler_params=pltpu.CompilerParams(vmem_limit_bytes=EXPERT_VMEM),
        name="other_expert",
    )(*in_vmem(*blocks, weights))


def summed(refs, rows):
    total = refs[0][rows].astype(jnp.float32)
    for ref in refs[1:]:
        total = total + ref[rows].astype(jnp.float32)
    return total


def join_kernel(residual_ref, *refs):
    parts_refs, out_ref, work_ref = refs[:-2], refs[-2], refs[-1]
    near = out_ref.shape[0]
    rows = work_ref.shape[0]
    step = 2 * TOK
    for start in range(0, rows, step):
        work_ref[start : start + step, :] = summed(parts_refs, slice(start, start + step))
    mine = pl.ds(pl.multiple_of(lax.axis_index("seq") * TOK, TOK), TOK)
    work_ref[mine, :] = work_ref[mine, :] + residual_ref[...]
    for seq in range(rows // TOK):
        far = seq // near
        out_ref[seq % near, far * TOK : (far + 1) * TOK, :] = work_ref[
            seq * TOK : (seq + 1) * TOK, :
        ].astype(jnp.bfloat16)


def join(residual, parts, near):
    rows = parts[0].shape[0]
    vmem = pl.BlockSpec(memory_space=pltpu.VMEM)
    return pl.pallas_call(
        join_kernel,
        out_shape=pltpu.VMEM((near, rows // near, D), jnp.bfloat16),
        in_specs=[vmem] * (len(parts) + 1),
        out_specs=vmem,
        scratch_shapes=[pltpu.VMEM((rows, D), jnp.float32)],
        compiler_params=pltpu.CompilerParams(vmem_limit_bytes=VMEM_LIMIT),
        name="join",
    )(*in_vmem(residual, *parts))


def fold_kernel(parts_ref, out_ref):
    width = D // SETS
    for far in range(parts_ref.shape[1] // TOK):
        for block in range(SETS):
            cols = slice(block * width, (block + 1) * width)
            total = parts_ref[0, far * TOK : (far + 1) * TOK, cols].astype(jnp.float32)
            for source in range(1, parts_ref.shape[0]):
                total = total + parts_ref[
                    source, far * TOK : (far + 1) * TOK, cols
                ].astype(jnp.float32)
            out_ref[far * SETS + block] = total.astype(jnp.bfloat16)


def fold(parts):
    far = parts.shape[1] // TOK
    vmem = pl.BlockSpec(memory_space=pltpu.VMEM)
    return pl.pallas_call(
        fold_kernel,
        out_shape=pltpu.VMEM((far * SETS, TOK, D // SETS), parts.dtype),
        in_specs=[vmem],
        out_specs=vmem,
        compiler_params=pltpu.CompilerParams(vmem_limit_bytes=VMEM_LIMIT),
        name="fold",
    )(*in_vmem(parts))


def total_kernel(parts_ref, out_ref):
    for source in range(SETS):
        total = parts_ref[source].astype(jnp.float32)
        for far in range(1, parts_ref.shape[0] // SETS):
            total = total + parts_ref[far * SETS + source].astype(jnp.float32)
        out_ref[0, source * TOK : (source + 1) * TOK, :] = total.astype(jnp.bfloat16)


def total(parts):
    vmem = pl.BlockSpec(memory_space=pltpu.VMEM)
    return pl.pallas_call(
        total_kernel,
        out_shape=jax.ShapeDtypeStruct((1, DRAFT, parts.shape[2]), parts.dtype),
        in_specs=[vmem],
        out_specs=vmem,
        compiler_params=pltpu.CompilerParams(vmem_limit_bytes=VMEM_LIMIT),
        name="total",
    )(*in_vmem(parts))


def shifted(value, axis, count, by):
    return lax.ppermute(value, axis, [(i, (i + by) % count) for i in range(count)])


def local(
    queries,
    draft_kv,
    kv_pool,
    page_table,
    cache_lens,
    parents,
    hidden,
    norm_gain,
    out_proj,
    router,
    routes,
    gate_w,
    up_w,
    down_w,
):
    kv_count = lax.axis_size("kv")
    seq_count = lax.axis_size("seq")
    weights = lax.all_gather(pack(gate_w, up_w, down_w), "exp")
    partials, out_proj, chosen = attention(
        page_table.reshape(PPD),
        cache_lens,
        queries,
        parents,
        draft_kv,
        kv_pool,
        out_proj,
        jnp.transpose(routes, (0, 2, 1)),
    )
    parts = lax.all_to_all(partials, "exp", 0, 0, tiled=True)
    projected = merge(parts, out_proj)
    shares = lax.all_to_all(projected.reshape(SETS, TOK, D), "exp", 0, 0, tiled=True)
    residual, row = norm(shares, hidden, norm_gain, jnp.transpose(router), chosen)
    rows = lax.all_gather(row, "seq").reshape(seq_count * TOK, WIDE)
    arrived = {by: shifted(rows, "kv", kv_count, by) for by in (1, kv_count - 1)}
    own, kept = own_expert(rows, weights)
    later, one, last, own = lax.optimization_barrier(
        (rows, arrived[1], arrived[kv_count - 1], own)
    )
    arrived.update({by: shifted(later, "kv", kv_count, by) for by in range(2, kv_count - 1)})
    near = other_expert(kept, one, last)
    parts = [
        own,
        shifted(near[0], "kv", kv_count, -1),
        shifted(near[1], "kv", kv_count, 1),
    ]
    for by in range(2, kv_count - 1):
        (far,) = other_expert(kept, arrived[by])
        parts.append(shifted(far, "kv", kv_count, -by))
    run = 4
    far_count = seq_count // run
    runs = [[far * run + near for near in range(run)] for far in range(far_count)]
    strides = [
        [
            (far * run + near) * SETS + block
            for far in range(far_count)
            for block in range(SETS)
        ]
        for near in range(run)
    ]
    back = join(residual, parts, run)
    back = lax.all_to_all(back, "seq", 0, 0, tiled=True, axis_index_groups=runs)
    back = lax.all_to_all(
        fold(back), ("seq", "exp"), 0, 0, tiled=True, axis_index_groups=strides
    )
    return total(back)


def solution(mesh):
    in_specs = (
        P(("kv", "seq"), None, None),
        P(None, ("kv", "seq"), "exp", None),
        P(None, ("kv", "seq", "exp"), None, None),
        P(("kv", "seq"), None, "exp"),
        P(("kv", "seq")),
        P(("kv", "seq"), None),
        P(("kv", "seq"), None, None),
        P(),
        P("exp", None),
        P(),
        P(("kv", "seq"), None, None),
        P(("kv", "seq"), None, "exp"),
        P(("kv", "seq"), None, "exp"),
        P(("kv", "seq"), "exp", None),
    )
    out_specs = P(("kv", "seq"), None, "exp")
    return jax.shard_map(local, mesh=mesh, in_specs=in_specs, out_specs=out_specs, check_vma=False)
```

```python
import functools

import jax
import jax.numpy as jnp
from jax import lax
from jax.experimental import pallas as pl
from jax.experimental.pallas import tpu as pltpu
from jax.sharding import PartitionSpec as P

D = 2048
H = 16
HD = 128
FF = 1024
EXPERTS = 64
TOPK = 8
DRAFT = 64
PAGE = 16
PPD = 12
SETS = 8
KEYS = PPD * PAGE
ROWS = KEYS + 16
TOK = DRAFT // SETS
WIDE = D + 2 * EXPERTS
STAT = DRAFT + 8
BLK = FF // SETS

NEG_FILL = -1e30
EPS_NORM = 1e-06
VMEM_LIMIT = 16 * 1024 * 1024
EXPERT_VMEM = 24 * 1024 * 1024


def nt(a, b):
    return lax.dot_general(a, b, (((1,), (1,)), ((), ())), preferred_element_type=jnp.float32)


def tn(a, b):
    return lax.dot_general(a, b, (((0,), (0,)), ((), ())), preferred_element_type=jnp.float32)


def nn(a, b):
    return lax.dot_general(a, b, (((1,), (0,)), ((), ())), preferred_element_type=jnp.float32)


def in_vmem(*arrays):
    return [pltpu.with_memory_space_constraint(x, pltpu.VMEM) for x in arrays]


def expert_index():
    return lax.axis_index("kv") * lax.axis_size("seq") + lax.axis_index("seq")


def attention_kernel(
    table,
    lens,
    q_hbm,
    parents_hbm,
    draft_hbm,
    pool_ref,
    proj_ref,
    routes_hbm,
    out_ref,
    kept_ref,
    chosen_ref,
    kbuf,
    vbuf,
    q_ref,
    draft_ref,
    parents_ref,
    routes_ref,
    mask_ref,
    seen_ref,
    score_ref,
    weight_ref,
    sems,
    more_sems,
):
    keys, values = [], []
    for page in range(PPD):
        slot = table[page]
        rows = pl.ds(page * PAGE, PAGE)
        keys.append(pltpu.make_async_copy(pool_ref.at[0, slot], kbuf.at[rows], sems.at[0, page]))
        values.append(pltpu.make_async_copy(pool_ref.at[1, slot], vbuf.at[rows], sems.at[1, page]))
    query_copy = pltpu.make_async_copy(q_hbm.at[0], q_ref, more_sems.at[0])
    draft_copy = pltpu.make_async_copy(draft_hbm.at[:, 0], draft_ref, more_sems.at[1])
    proj_copy = pltpu.make_async_copy(proj_ref, kept_ref, more_sems.at[2])
    parents_copy = pltpu.make_async_copy(parents_hbm, parents_ref, more_sems.at[3])
    routes_copy = pltpu.make_async_copy(routes_hbm.at[0], routes_ref, more_sems.at[4])
    for copy in [parents_copy, routes_copy, draft_copy, query_copy] + keys + values + [proj_copy]:
        copy.start()
    length = lens[0]
    my_set = lax.axis_index("exp")
    ancestor = lax.broadcasted_iota(jnp.int32, (DRAFT, 2 * DRAFT), 0)
    token = lax.broadcasted_iota(jnp.int32, (DRAFT, 2 * DRAFT), 1) % DRAFT
    parents_copy.wait()
    parents = jnp.concatenate([parents_ref[...], parents_ref[...]], axis=1)
    linked = jnp.where((parents == ancestor) | (ancestor == token), 1.0, 0.0)
    for doubling in range((DRAFT - 1).bit_length()):
        narrow = linked.astype(jnp.bfloat16)
        linked = jnp.minimum(nn(narrow[:, :DRAFT], narrow), 1.0)
    seen_ref[0:DRAFT, :] = linked
    draft_seen = seen_ref[pl.ds(pl.multiple_of(my_set * TOK, TOK), TOK), :]
    key_row = lax.broadcasted_iota(jnp.int32, (KEYS, 2 * DRAFT), 0)
    position = ((key_row // PAGE) * SETS + my_set) * PAGE + key_row % PAGE
    cache_seen = jnp.where(position < length, 1.0, 0.0)
    seen_ref[0:ROWS, :] = jnp.concatenate(
        [cache_seen, draft_seen, jnp.zeros((8, 2 * DRAFT), jnp.float32)], axis=0
    )
    own = (lax.broadcasted_iota(jnp.int32, (2 * DRAFT, 2 * HD), 0) < DRAFT) == (
        lax.broadcasted_iota(jnp.int32, (2 * DRAFT, 2 * HD), 1) < HD
    )
    stat_row = lax.broadcasted_iota(jnp.int32, (8, 2 * DRAFT), 0)
    routes_copy.wait()
    expert = lax.broadcasted_iota(jnp.int32, (EXPERTS, DRAFT), 0)
    chosen = routes_ref[0:1, :] == expert
    for pick in range(1, TOPK):
        chosen = chosen | (routes_ref[pick : pick + 1, :] == expert)
    mask_ref[...] = jnp.transpose(jnp.where(chosen, 1.0, 0.0))
    chosen_ref[...] = mask_ref[pl.ds(pl.multiple_of(my_set * TOK, TOK), TOK), :]
    pad = jnp.zeros((8, D), jnp.float32)
    draft_copy.wait()
    for place, buf in ((0, kbuf), (1, vbuf)):
        rows = jnp.concatenate([draft_ref[place].astype(jnp.float32), pad], axis=0)
        buf[KEYS:ROWS, :] = rows.astype(jnp.bfloat16)
    query_copy.wait()
    for copy in keys:
        copy.wait()
    for pair in range(H // 2):
        cols = slice(pair * 2 * HD, (pair + 1) * 2 * HD)
        query = q_ref[:, cols]
        query = jnp.where(own, jnp.concatenate([query, query], axis=0), jnp.zeros((), jnp.bfloat16))
        score_ref[pair] = nt(kbuf[:, cols], query) * (HD**-0.5)
    for pair in range(H // 2):
        seen = seen_ref[0:ROWS, :] > 0.5
        scores = jnp.where(seen, score_ref[pair], NEG_FILL)
        top = jnp.max(scores, axis=0, keepdims=True).astype(jnp.bfloat16).astype(jnp.float32)
        weights = jnp.where(seen, jnp.exp(scores - top), 0.0)
        total = jnp.sum(weights, axis=0, keepdims=True)
        weight_ref[pair] = weights.astype(jnp.bfloat16)
        total_high = total.astype(jnp.bfloat16).astype(jnp.float32)
        stats = jnp.where(
            stat_row == 0,
            top,
            jnp.where(stat_row == 1, total_high, jnp.where(stat_row == 2, total - total_high, 0.0)),
        )
        out_ref[pair, DRAFT:STAT, 0:HD] = stats.astype(jnp.bfloat16)
        out_ref[pair, DRAFT:STAT, HD : 2 * HD] = jnp.zeros((8, HD), jnp.bfloat16)
    for copy in values:
        copy.wait()
    for pair in range(H // 2):
        cols = slice(pair * 2 * HD, (pair + 1) * 2 * HD)
        acc = tn(weight_ref[pair], vbuf[:, cols])
        out_ref[pair, 0:DRAFT, 0:HD] = acc[:DRAFT, :HD].astype(jnp.bfloat16)
        out_ref[pair, 0:DRAFT, HD : 2 * HD] = acc[DRAFT:, HD:].astype(jnp.bfloat16)
    proj_copy.wait()


def attention(table, lens, queries, parents, draft_kv, kv_pool, out_proj, routes):
    smem = pl.BlockSpec(memory_space=pltpu.SMEM)
    vmem = pl.BlockSpec(memory_space=pltpu.VMEM)
    hbm = pl.BlockSpec(memory_space=pltpu.HBM)
    queries, parents, draft_kv, kv_pool, out_proj, routes = (
        pltpu.with_memory_space_constraint(x, pltpu.HBM)
        for x in (queries, parents, draft_kv, kv_pool, out_proj, routes)
    )
    return pl.pallas_call(
        attention_kernel,
        out_shape=(
            jax.ShapeDtypeStruct((SETS, STAT, 2 * HD), jnp.bfloat16),
            pltpu.VMEM(out_proj.shape, out_proj.dtype),
            pltpu.VMEM((TOK, EXPERTS), jnp.float32),
        ),
        in_specs=[smem, smem, hbm, hbm, hbm, hbm, hbm, hbm],
        out_specs=(vmem, vmem, vmem),
        scratch_shapes=[
            pltpu.VMEM((ROWS, D), jnp.bfloat16),
            pltpu.VMEM((ROWS, D), jnp.bfloat16),
            pltpu.VMEM((DRAFT, D), jnp.bfloat16),
            pltpu.VMEM((2, TOK, D), jnp.bfloat16),
            pltpu.VMEM((1, DRAFT), jnp.int32),
            pltpu.VMEM((TOPK, DRAFT), jnp.int32),
            pltpu.VMEM((DRAFT, EXPERTS), jnp.float32),
            pltpu.VMEM((ROWS, 2 * DRAFT), jnp.float32),
            pltpu.VMEM((H // 2, ROWS, 2 * DRAFT), jnp.float32),
            pltpu.VMEM((H // 2, ROWS, 2 * DRAFT), jnp.bfloat16),
            pltpu.SemaphoreType.DMA((2, PPD)),
            pltpu.SemaphoreType.DMA((5,)),
        ],
        compiler_params=pltpu.CompilerParams(vmem_limit_bytes=VMEM_LIMIT),
        name="attention",
    )(table, lens, queries, parents, draft_kv, kv_pool, out_proj, routes)


def merge_kernel(parts_ref, proj_ref, out_ref):
    stats = parts_ref[:, DRAFT:STAT, 0:HD].astype(jnp.float32)
    tops = stats[:, 0, :]
    totals = stats[:, 1, :] + stats[:, 2, :]
    scale = jnp.exp(tops - jnp.max(tops, axis=0, keepdims=True))
    scale = scale / jnp.sum(scale * totals, axis=0, keepdims=True)
    scale = jnp.transpose(scale)
    heads = []
    for head in range(2):
        joined = jnp.zeros((DRAFT, HD), jnp.float32)
        for source in range(SETS):
            part = parts_ref[source, 0:DRAFT, head * HD : (head + 1) * HD].astype(jnp.float32)
            joined = joined + part * scale[head * DRAFT : (head + 1) * DRAFT, source : source + 1]
        heads.append(joined.astype(jnp.bfloat16))
    out_ref[...] = nn(jnp.concatenate(heads, axis=1), proj_ref[...]).astype(jnp.bfloat16)


def merge(parts, out_proj):
    return pl.pallas_call(
        merge_kernel,
        out_shape=jax.ShapeDtypeStruct((DRAFT, D), jnp.bfloat16),
        compiler_params=pltpu.CompilerParams(vmem_limit_bytes=VMEM_LIMIT),
        name="merge",
    )(parts, *in_vmem(out_proj))


def norm_kernel(
    parts_ref,
    hidden_ref,
    gain_hbm,
    router_hbm,
    chosen_ref,
    residual_ref,
    row_ref,
    own_ref,
    gain_ref,
    router_ref,
    sems,
):
    mine = pl.ds(pl.multiple_of(lax.axis_index("exp") * TOK, TOK), TOK)
    copies = [
        pltpu.make_async_copy(hidden_ref.at[0, mine], own_ref, sems.at[0]),
        pltpu.make_async_copy(gain_hbm, gain_ref, sems.at[1]),
        pltpu.make_async_copy(router_hbm, router_ref, sems.at[2]),
    ]
    for copy in copies:
        copy.start()
    residual = parts_ref[0].astype(jnp.float32)
    for source in range(1, SETS):
        residual = residual + parts_ref[source].astype(jnp.float32)
    for copy in copies:
        copy.wait()
    residual = own_ref[...].astype(jnp.float32) + residual
    residual_ref[...] = residual
    mean_sq = jnp.mean(residual * residual, axis=1, keepdims=True)
    gain = gain_ref[...].astype(jnp.float32).reshape(1, D)
    normed = (residual * lax.rsqrt(mean_sq + EPS_NORM) * gain).astype(jnp.bfloat16)
    logits = nt(normed, router_ref[...])
    gates = jnp.where(chosen_ref[...] > 0.5, 1.0 / (1.0 + jnp.exp(-logits)), 0.0)
    high = gates.astype(jnp.bfloat16).astype(jnp.float32)
    row_ref[:, 0:D] = normed
    row_ref[:, D:WIDE] = jnp.concatenate([high, gates - high], axis=1).astype(jnp.bfloat16)


def norm(parts, hidden, norm_gain, router, chosen):
    vmem = pl.BlockSpec(memory_space=pltpu.VMEM)
    hbm = pl.BlockSpec(memory_space=pltpu.HBM)
    held = [
        pltpu.with_memory_space_constraint(x, pltpu.HBM) for x in (hidden, norm_gain, router)
    ]
    return pl.pallas_call(
        norm_kernel,
        out_shape=(
            pltpu.VMEM((TOK, D), jnp.float32),
            jax.ShapeDtypeStruct((TOK, WIDE), jnp.bfloat16),
        ),
        in_specs=[vmem, hbm, hbm, hbm, vmem],
        out_specs=(vmem, vmem),
        scratch_shapes=[
            pltpu.VMEM((TOK, D), jnp.bfloat16),
            pltpu.VMEM(norm_gain.shape, jnp.bfloat16),
            pltpu.VMEM((EXPERTS, D), jnp.bfloat16),
            pltpu.SemaphoreType.DMA((3,)),
        ],
        compiler_params=pltpu.CompilerParams(vmem_limit_bytes=VMEM_LIMIT),
        name="norm",
    )(*in_vmem(parts), *held, *in_vmem(chosen))


def pack_kernel(gate_ref, up_ref, down_ref, out_ref, buf, in_sems, out_sems):
    width = D // SETS
    pieces = []
    part = D // 4
    for piece in range(4):
        rows = pl.ds(piece * part, part)
        pieces.append(
            (
                [
                    (gate_ref.at[0, rows], buf.at[rows, pl.ds(0, BLK)]),
                    (up_ref.at[0, rows], buf.at[rows, pl.ds(BLK, BLK)]),
                ],
                rows,
            )
        )
    for half in range(2):
        blocks = range(half * SETS // 2, (half + 1) * SETS // 2)
        pieces.append(
            (
                [
                    (
                        down_ref.at[0, :, pl.ds(block * width, width)],
                        buf.at[pl.ds(D + block * BLK, BLK)],
                    )
                    for block in blocks
                ],
                pl.ds(D + half * FF // 2, FF // 2),
            )
        )
    loads = []
    count = 0
    for moves, rows in pieces:
        group = []
        for source, target in moves:
            group.append(pltpu.make_async_copy(source, target, in_sems.at[count]))
            count += 1
        loads.append((group, rows))
    for group, rows in loads:
        for copy in group:
            copy.start()
    stores = []
    for index, (group, rows) in enumerate(loads):
        for copy in group:
            copy.wait()
        store = pltpu.make_async_copy(buf.at[rows], out_ref.at[rows], out_sems.at[index])
        store.start()
        stores.append(store)
    for store in stores:
        store.wait()


def pack(gate_w, up_w, down_w):
    hbm = pl.BlockSpec(memory_space=pltpu.HBM)
    width = D // SETS
    return pl.pallas_call(
        pack_kernel,
        out_shape=jax.ShapeDtypeStruct((D + FF, width), gate_w.dtype),
        in_specs=[hbm] * 3,
        out_specs=hbm,
        scratch_shapes=[
            pltpu.VMEM((D + FF, width), jnp.bfloat16),
            pltpu.SemaphoreType.DMA((16,)),
            pltpu.SemaphoreType.DMA((6,)),
        ],
        compiler_params=pltpu.CompilerParams(vmem_limit_bytes=VMEM_LIMIT),
        name="pack",
    )(*(pltpu.with_memory_space_constraint(x, pltpu.HBM) for x in (gate_w, up_w, down_w)))


def expert_rows(my_expert, rows_ref, weights_ref, store, act_ref, before_block):
    gates = rows_ref[:, D:WIDE].astype(jnp.float32)
    lane = lax.broadcasted_iota(jnp.int32, gates.shape, 1) % EXPERTS
    scale = jnp.sum(jnp.where(lane == my_expert, gates, 0.0), axis=1, keepdims=True)
    for block in range(SETS):
        before_block(block)
        both = nn(rows_ref[:, 0:D], weights_ref[block, 0:D, :])
        gate, up = both[:, :BLK], both[:, BLK:]
        act = gate / (1.0 + jnp.exp(-gate)) * up
        act_ref[:, block * BLK : (block + 1) * BLK] = act.astype(jnp.bfloat16)
    width = D // SETS
    for block in range(SETS):
        down = weights_ref[:, D + block * BLK : D + (block + 1) * BLK, :].reshape(FF, width)
        store(block, (nn(act_ref[...], down) * scale).astype(jnp.bfloat16))


def columns_of(out_ref):
    width = D // SETS

    def store(block, value):
        out_ref[:, block * width : (block + 1) * width] = value

    return store


def own_kernel(rows_ref, weights_ref, out_ref, kept_ref, act_ref, sems):
    copies = [
        pltpu.make_async_copy(weights_ref.at[block], kept_ref.at[block], sems.at[block])
        for block in range(SETS)
    ]
    for copy in copies:
        copy.start()
    expert_rows(
        expert_index(),
        rows_ref,
        kept_ref,
        columns_of(out_ref),
        act_ref,
        lambda block: copies[block].wait(),
    )


def other_kernel(count, *refs):
    rows_refs, weights_ref, out_refs, act_ref = (
        refs[:count],
        refs[count],
        refs[count + 1 : 2 * count + 1],
        refs[2 * count + 1],
    )
    for rows_ref, out_ref in zip(rows_refs, out_refs):
        expert_rows(
            expert_index(), rows_ref, weights_ref, columns_of(out_ref), act_ref, lambda block: None
        )


def own_expert(rows, weights):
    count = rows.shape[0]
    vmem = pl.BlockSpec(memory_space=pltpu.VMEM)
    return pl.pallas_call(
        own_kernel,
        out_shape=(
            pltpu.VMEM((count, D), jnp.bfloat16),
            pltpu.VMEM(weights.shape, weights.dtype),
        ),
        in_specs=[vmem, pl.BlockSpec(memory_space=pltpu.HBM)],
        out_specs=(vmem, vmem),
        scratch_shapes=[
            pltpu.VMEM((count, FF), jnp.bfloat16),
            pltpu.SemaphoreType.DMA((SETS,)),
        ],
        compiler_params=pltpu.CompilerParams(vmem_limit_bytes=EXPERT_VMEM),
        name="own_expert",
    )(*in_vmem(rows), pltpu.with_memory_space_constraint(weights, pltpu.HBM))


def other_expert(weights, *blocks):
    rows = blocks[0].shape[0]
    vmem = pl.BlockSpec(memory_space=pltpu.VMEM)
    return pl.pallas_call(
        functools.partial(other_kernel, len(blocks)),
        out_shape=tuple(jax.ShapeDtypeStruct((rows, D), jnp.bfloat16) for block in blocks),
        in_specs=[vmem] * (len(blocks) + 1),
        out_specs=(vmem,) * len(blocks),
        scratch_shapes=[pltpu.VMEM((rows, FF), jnp.bfloat16)],
        compiler_params=pltpu.CompilerParams(vmem_limit_bytes=EXPERT_VMEM),
        name="other_expert",
    )(*in_vmem(*blocks, weights))


def summed(refs, rows):
    total = refs[0][rows].astype(jnp.float32)
    for ref in refs[1:]:
        total = total + ref[rows].astype(jnp.float32)
    return total


def join_kernel(residual_ref, *refs):
    parts_refs, out_ref, work_ref = refs[:-2], refs[-2], refs[-1]
    near = out_ref.shape[0]
    rows = work_ref.shape[0]
    step = 2 * TOK
    for start in range(0, rows, step):
        work_ref[start : start + step, :] = summed(parts_refs, slice(start, start + step))
    mine = pl.ds(pl.multiple_of(lax.axis_index("seq") * TOK, TOK), TOK)
    work_ref[mine, :] = work_ref[mine, :] + residual_ref[...]
    for seq in range(rows // TOK):
        far = seq // near
        out_ref[seq % near, far * TOK : (far + 1) * TOK, :] = work_ref[
            seq * TOK : (seq + 1) * TOK, :
        ].astype(jnp.bfloat16)


def join(residual, parts, near):
    rows = parts[0].shape[0]
    vmem = pl.BlockSpec(memory_space=pltpu.VMEM)
    return pl.pallas_call(
        join_kernel,
        out_shape=pltpu.VMEM((near, rows // near, D), jnp.bfloat16),
        in_specs=[vmem] * (len(parts) + 1),
        out_specs=vmem,
        scratch_shapes=[pltpu.VMEM((rows, D), jnp.float32)],
        compiler_params=pltpu.CompilerParams(vmem_limit_bytes=VMEM_LIMIT),
        name="join",
    )(*in_vmem(residual, *parts))


def fold_kernel(parts_ref, out_ref):
    width = D // SETS
    for far in range(parts_ref.shape[1] // TOK):
        for block in range(SETS):
            cols = slice(block * width, (block + 1) * width)
            total = parts_ref[0, far * TOK : (far + 1) * TOK, cols].astype(jnp.float32)
            for source in range(1, parts_ref.shape[0]):
                total = total + parts_ref[
                    source, far * TOK : (far + 1) * TOK, cols
                ].astype(jnp.float32)
            out_ref[far * SETS + block] = total.astype(jnp.bfloat16)


def fold(parts):
    far = parts.shape[1] // TOK
    vmem = pl.BlockSpec(memory_space=pltpu.VMEM)
    return pl.pallas_call(
        fold_kernel,
        out_shape=pltpu.VMEM((far * SETS, TOK, D // SETS), parts.dtype),
        in_specs=[vmem],
        out_specs=vmem,
        compiler_params=pltpu.CompilerParams(vmem_limit_bytes=VMEM_LIMIT),
        name="fold",
    )(*in_vmem(parts))


def total_kernel(parts_ref, out_ref):
    for source in range(SETS):
        total = parts_ref[source].astype(jnp.float32)
        for far in range(1, parts_ref.shape[0] // SETS):
            total = total + parts_ref[far * SETS + source].astype(jnp.float32)
        out_ref[0, source * TOK : (source + 1) * TOK, :] = total.astype(jnp.bfloat16)


def total(parts):
    vmem = pl.BlockSpec(memory_space=pltpu.VMEM)
    return pl.pallas_call(
        total_kernel,
        out_shape=jax.ShapeDtypeStruct((1, DRAFT, parts.shape[2]), parts.dtype),
        in_specs=[vmem],
        out_specs=vmem,
        compiler_params=pltpu.CompilerParams(vmem_limit_bytes=VMEM_LIMIT),
        name="total",
    )(*in_vmem(parts))


def shifted(value, axis, count, by):
    return lax.ppermute(value, axis, [(i, (i + by) % count) for i in range(count)])


def local(
    queries,
    draft_kv,
    kv_pool,
    page_table,
    cache_lens,
    parents,
    hidden,
    norm_gain,
    out_proj,
    router,
    routes,
    gate_w,
    up_w,
    down_w,
):
    kv_count = lax.axis_size("kv")
    seq_count = lax.axis_size("seq")
    weights = lax.all_gather(pack(gate_w, up_w, down_w), "exp")
    partials, out_proj, chosen = attention(
        page_table.reshape(PPD),
        cache_lens,
        queries,
        parents,
        draft_kv,
        kv_pool,
        out_proj,
        jnp.transpose(routes, (0, 2, 1)),
    )
    parts = lax.all_to_all(partials, "exp", 0, 0, tiled=True)
    projected = merge(parts, out_proj)
    shares = lax.all_to_all(projected.reshape(SETS, TOK, D), "exp", 0, 0, tiled=True)
    residual, row = norm(shares, hidden, norm_gain, jnp.transpose(router), chosen)
    rows = lax.all_gather(row, "seq").reshape(seq_count * TOK, WIDE)
    arrived = {by: shifted(rows, "kv", kv_count, by) for by in (1, kv_count - 1)}
    own, kept = own_expert(rows, weights)
    one, last, own = lax.optimization_barrier((arrived[1], arrived[kv_count - 1], own))
    near = other_expert(kept, one, last)
    parts = [
        own,
        shifted(near[0], "kv", kv_count, -1),
        shifted(near[1], "kv", kv_count, 1),
    ]
    relayed = last
    for by in range(kv_count - 2, 1, -1):
        relayed = shifted(relayed, "kv", kv_count, -1)
        relayed, near = lax.optimization_barrier((relayed, near))
        (far,) = other_expert(kept, relayed)
        half = D // 2
        straight = shifted(far[:, :half], "kv", kv_count, -by)
        around = far[:, half:]
        for hop in range(by):
            around = shifted(around, "kv", kv_count, -1)
        parts.append(jnp.concatenate([straight, around], axis=1))
    run = 4
    far_count = seq_count // run
    runs = [[far * run + near for near in range(run)] for far in range(far_count)]
    strides = [
        [
            (far * run + near) * SETS + block
            for far in range(far_count)
            for block in range(SETS)
        ]
        for near in range(run)
    ]
    back = join(residual, parts, run)
    back = lax.all_to_all(back, "seq", 0, 0, tiled=True, axis_index_groups=runs)
    back = lax.all_to_all(
        fold(back), ("seq", "exp"), 0, 0, tiled=True, axis_index_groups=strides
    )
    return total(back)


def solution(mesh):
    in_specs = (
        P(("kv", "seq"), None, None),
        P(None, ("kv", "seq"), "exp", None),
        P(None, ("kv", "seq", "exp"), None, None),
        P(("kv", "seq"), None, "exp"),
        P(("kv", "seq")),
        P(("kv", "seq"), None),
        P(("kv", "seq"), None, None),
        P(),
        P("exp", None),
        P(),
        P(("kv", "seq"), None, None),
        P(("kv", "seq"), None, "exp"),
        P(("kv", "seq"), None, "exp"),
        P(("kv", "seq"), "exp", None),
    )
    out_specs = P(("kv", "seq"), None, "exp")
    return jax.shard_map(local, mesh=mesh, in_specs=in_specs, out_specs=out_specs, check_vma=False)
```
